32 devices in a mesh: dp: 8 (over y, x, core), mp: 4 (over z).
Axes of the slice: x: 2, y: 2, z: 4, core: 2. Of those that a mesh axis runs over, the one named last changes fastest.
Arguments:
- hidden: bfloat16 [24576, 768], P('dp'), may hold values from -6 to 6
- timesteps: int32 [144], P('dp'), may hold values from 0 to 999
- cotangent: bfloat16 [24576, 768], P('dp'), may hold values from -6 to 6
- time_table: bfloat16 [1000, 768], replicated, may hold values from -3 to 3
- first_gain: float32 [768], replicated, may hold values from 0.25 to 1.75
- first_shift: float32 [768], replicated, may hold values from -1.5 to 1.5
- qkv_weight: bfloat16 [3, 768, 768], P(None, None, 'mp'), may hold values from -0.21875 to 0.21875
- out_weight: bfloat16 [768, 768], P('mp'), may hold values from -0.875 to 0.875
- out_bias: float32 [768], replicated, may hold values from -1.5 to 1.5
- second_gain: float32 [768], replicated, may hold values from 0.25 to 1.75
- second_shift: float32 [768], replicated, may hold values from -1.5 to 1.5
- up_weight: bfloat16 [768, 3072], P(None, 'mp'), may hold values from -0.21875 to 0.21875
- up_bias: float32 [3072], P('mp'), may hold values from -2.5 to 2.5
- down_weight: bfloat16 [3072, 768], P('mp'), may hold values from -0.15625 to 0.15625
- down_bias: float32 [768], replicated, may hold values from -1.5 to 1.5
Outputs:
- output: bfloat16 [24576, 768], P('dp')
- grad_hidden: bfloat16 [24576, 768], P('dp')
- grad_table: float32 [1000, 768], P(None, 'mp')
- grad_first_gain: float32 [768], replicated
- grad_first_shift: float32 [768], replicated
- grad_qkv_weight: float32 [3, 768, 768], P(None, 'dp', 'mp')
- grad_out_weight: float32 [768, 768], P('mp', 'dp')
- grad_out_bias: float32 [768], replicated
- grad_second_gain: float32 [768], replicated
- grad_second_shift: float32 [768], replicated
- grad_up_weight: float32 [768, 3072], P('dp', 'mp')
- grad_up_bias: float32 [3072], P('mp')
- grad_down_weight: float32 [3072, 768], P('mp', 'dp')
- grad_down_bias: float32 [768], replicated
The draws below stay inside these ranges and needn't reach their ends.
All inputs are finite; a program needn't handle non-finite values.
Results may differ from the reference program's by a relative error of at most 0.02.
Values may be sent and summed in bfloat16 or wider, within the bound.
A program may use at most 192 MiB of HBM per device.

```python
import jax
import jax.numpy as jnp
from jax import lax

D = 768
HEADS = 12
HD = 64
FF = 3072
STEPS = 1000
LEN_A = 128
LEN_B = 256
BLOCK = 512
TOKENS = 24576
ROWS = 144
N_MP = 4


def plant(values, rng, smallest, high):
    place = [jax.random.randint(jax.random.fold_in(rng, axis), (), 0, length) for axis, length in enumerate(values.shape)]
    main_axis = values.shape.index(max(values.shape))
    neighbour = place[:main_axis] + [(place[main_axis] + 1) % values.shape[main_axis]] + place[main_axis + 1:]
    return values.at[tuple(place)].set(smallest).at[tuple(neighbour)].set(high)


def level_of(own_key, shape, cuts, low, high):
    factor_of = 1.0
    for axis_at, blocks in cuts:
        draws = jax.random.uniform(jax.random.fold_in(jax.random.fold_in(own_key, 6), axis_at), (blocks,), jnp.float32, low / len(cuts), high / len(cuts))
        factor_of = factor_of * jnp.repeat(jnp.exp(draws), shape[axis_at] // blocks).reshape((-1,) + (1,) * (len(shape) - 1 - axis_at))
    return factor_of


def normal_values(key, shape, scale, limit, cuts=(), kind=jnp.bfloat16):
    values = jax.random.normal(key, shape, jnp.float32) * scale
    if len(cuts) > 0:
        values = level_of(key, shape, cuts, -0.22, 0.18) * values
    return jnp.clip(values, min=-limit, max=limit).astype(kind)


def setup_inputs(seed: int = 0) -> dict:
    key_of = jax.random.split(jax.random.key(seed), 16)
    return {
        "hidden": normal_values(key_of[0], (TOKENS, D), 1.0, 6.0, ((0, 8),)),
        "timesteps": plant(jax.random.randint(key_of[1], (ROWS,), 0, STEPS), jax.random.fold_in(key_of[1], 1), 0, STEPS - 1).astype(jnp.int32),
        "cotangent": normal_values(key_of[2], (TOKENS, D), 1.0, 6.0, ((0, 8),)),
        "time_table": normal_values(key_of[3], (STEPS, D), 0.5, 3.0),
        "first_gain": jnp.clip(1.0 + 0.15 * jax.random.normal(key_of[4], (D,), jnp.float32), 0.25, 1.75),
        "first_shift": normal_values(key_of[5], (D,), 0.3, 1.5, (), jnp.float32),
        "qkv_weight": normal_values(key_of[6], (3, D, D), D ** -0.5, 0.21875, ((2, 4),)),
        "out_weight": normal_values(key_of[7], (D, D), (D // 16) ** -0.5, 0.875, ((0, 4),)),
        "out_bias": normal_values(key_of[8], (D,), 0.3, 1.5, (), jnp.float32),
        "second_gain": jnp.clip(1.0 + 0.15 * jax.random.normal(key_of[9], (D,), jnp.float32), 0.25, 1.75),
        "second_shift": normal_values(key_of[10], (D,), 0.3, 1.5, (), jnp.float32),
        "up_weight": normal_values(key_of[11], (D, FF), D ** -0.5, 0.21875, ((1, 4),)),
        "up_bias": normal_values(key_of[12], (FF,), 0.5, 2.5, ((0, 4),), jnp.float32),
        "down_weight": normal_values(key_of[13], (FF, D), (FF // 2) ** -0.5, 0.15625, ((0, 4),)),
        "down_bias": normal_values(key_of[14], (D,), 0.3, 1.5, (), jnp.float32),
    }


@jax.custom_vjp
def low(v):
    return lax.optimization_barrier(v.astype(jnp.bfloat16)).astype(jnp.float32)

@jax.custom_vjp
def low_back(v):
    return v

def low_keep(v):
    return (low(v), None)

def low_pass(kept, grad):
    return (grad,)

def back_keep(v):
    return (v, None)

def back_low(kept, grad):
    return (low(grad),)
low.defvjp(low_keep, low_pass)
low_back.defvjp(back_keep, back_low)

def layer_norm(rows_in, gain_vec, shift_vec):
    centre = lax.optimization_barrier(jnp.mean(rows_in, axis=-1, keepdims=True))
    offset = rows_in - centre
    spread = lax.optimization_barrier(jnp.mean(offset * offset, axis=-1, keepdims=True))
    return offset * lax.rsqrt(spread + 1e-05) * gain_vec + shift_vec

def token_rows(count):
    places = jnp.arange(count, dtype=jnp.int32)
    pair_index = places // (2 * BLOCK)
    within = places % (2 * BLOCK)
    lead_row = within // LEN_A
    tail_row = 4 + (within - BLOCK) // LEN_B
    return pair_index * 6 + jnp.where(within < BLOCK, lead_row, tail_row)

def block_attend(queries, key_rows, value_rows, seg_len):
    scale = HD ** (-0.5)
    scores = low_back(jnp.einsum('qhd,khd->hqk', queries, key_rows, precision=lax.Precision.HIGHEST) * scale)
    segment = jnp.arange(BLOCK, dtype=jnp.int32) // seg_len
    same_row = segment[:, None] == segment[None, :]
    scores = jnp.where(same_row[None], scores, -1000000000.0)
    attn_probs = low(jax.nn.softmax(scores, axis=-1))
    return jnp.einsum('hqk,khd->qhd', attn_probs, value_rows, precision=lax.Precision.HIGHEST)

def pair_attend(carry, pieces):
    queries, key_rows, value_rows = pieces
    lead_out = block_attend(queries[0], key_rows[0], value_rows[0], LEN_A)
    tail_out = block_attend(queries[1], key_rows[1], value_rows[1], LEN_B)
    return (carry, jnp.stack([lead_out, tail_out]))

def layer(params, timesteps):
    hidden, table, first_gain, first_shift, qkv_weight, out_weight, out_bias, second_gain, second_shift, up_weight, up_bias, down_weight, down_bias = params
    count = hidden.shape[0]
    row_emb = jnp.take(table, timesteps, axis=0)
    stream_in = hidden + jnp.take(row_emb, token_rows(count), axis=0)
    normed = low(layer_norm(stream_in, first_gain, first_shift))
    width = D // N_MP
    pieces = []
    for member in range(N_MP):
        own_copy = low_back(normed)
        cols = qkv_weight[:, :, member * width:(member + 1) * width]
        pieces.append(jnp.einsum('td,cde->cte', own_copy, cols, precision=lax.Precision.HIGHEST))
    proj = low_back(low(jnp.concatenate(pieces, axis=2)))
    shaped = proj.reshape(3, count // (2 * BLOCK), 2, BLOCK, HEADS, HD)
    _, context = lax.scan(jax.checkpoint(pair_attend), jnp.zeros((), jnp.float32), (shaped[0], shaped[1], shaped[2]))
    context = low_back(low(context.reshape(count, D)))
    attn_total = jnp.zeros((count, D), jnp.float32)
    for member in range(N_MP):
        part_term = jnp.dot(context[:, member * width:(member + 1) * width], out_weight[member * width:(member + 1) * width, :], precision=lax.Precision.HIGHEST)
        attn_total = attn_total + low(part_term)
    middle = stream_in + low_back(attn_total) + out_bias
    normed_two = low(layer_norm(middle, second_gain, second_shift))
    fwidth = FF // N_MP
    mlp_total = jnp.zeros((count, D), jnp.float32)
    for member in range(N_MP):
        own_copy = low_back(normed_two)
        lo_col = member * fwidth
        pre_act = low_back(jnp.dot(own_copy, up_weight[:, lo_col:lo_col + fwidth], precision=lax.Precision.HIGHEST) + up_bias[lo_col:lo_col + fwidth])
        activated = low(jax.nn.gelu(pre_act, approximate=True))
        mlp_total = mlp_total + low(jnp.dot(activated, down_weight[lo_col:lo_col + fwidth, :], precision=lax.Precision.HIGHEST))
    return middle + low_back(mlp_total) + down_bias

def reference(hidden, timesteps, cotangent, time_table, first_gain, first_shift, qkv_weight, out_weight, out_bias, second_gain, second_shift, up_weight, up_bias, down_weight, down_bias):
    floats = (hidden.astype(jnp.float32), time_table.astype(jnp.float32), first_gain, first_shift, qkv_weight.astype(jnp.float32), out_weight.astype(jnp.float32), out_bias, second_gain, second_shift, up_weight.astype(jnp.float32), up_bias, down_weight.astype(jnp.float32), down_bias)

    def forward(*params):
        return layer(params, timesteps)
    result, pull = jax.vjp(forward, *floats)
    grads = pull(cotangent.astype(jnp.float32))
    return (result.astype(jnp.bfloat16), grads[0].astype(jnp.bfloat16), grads[1], grads[2], grads[3], grads[4], grads[5], grads[6], grads[7], grads[8], grads[9], grads[10], grads[11], grads[12])
```

```python
from functools import partial

import jax
import jax.numpy as jnp
from jax import lax
from jax.experimental import pallas as pl
from jax.experimental.pallas import tpu as pltpu
from jax.sharding import PartitionSpec as P

F32 = jnp.float32
BF16 = jnp.bfloat16
HD = 64
LEN_A = 128
LEN_B = 256
BLOCK = 512
WIN = 256
TILE = 512
EPS = 1e-05
GELU_C = 0.7978845608028654
GELU_A = 0.044715


def mm(a, b):
    return lax.dot_general(a, b, (((1,), (0,)), ((), ())), preferred_element_type=F32)


def mm_nt(a, b):
    return lax.dot_general(a, b, (((1,), (1,)), ((), ())), preferred_element_type=F32)


def mm_tn(a, b):
    return lax.dot_general(a, b, (((0,), (0,)), ((), ())), preferred_element_type=F32)


def norm_stats(rows):
    centre = jnp.mean(rows, axis=-1, keepdims=True)
    offset = rows - centre
    spread = jnp.mean(offset * offset, axis=-1, keepdims=True)
    inv = lax.rsqrt(spread + EPS)
    return offset * inv, inv


def norm_back(grad, gain, hat, inv):
    dhat = grad * gain
    first = jnp.mean(dhat, axis=-1, keepdims=True)
    second = jnp.mean(dhat * hat, axis=-1, keepdims=True)
    return inv * (dhat - first - hat * second)


def stream_tile(hidden_ref, emb_ref, tile):
    parts = []
    for unit in range(TILE // LEN_A):
        row = emb_ref[pl.ds(tile * (TILE // LEN_A) + unit, 1), :]
        parts.append(hidden_ref[unit * LEN_A : (unit + 1) * LEN_A, :].astype(F32) + row)
    return jnp.concatenate(parts, axis=0)


def attn_fwd_kernel(
    meta, hidden_ref, emb_ref, gain_ref, shift_ref, wqkv_ref, wo_ref, ob_ref,
    qkv_ref, probs_ref, ctx_ref, mid_ref, same_ref, ctx_acc,
):
    tile = pl.program_id(0)
    half = meta[0]
    stream = stream_tile(hidden_ref, emb_ref, tile)
    hat, _ = norm_stats(stream)
    normed = (hat * gain_ref[...] + shift_ref[...]).astype(BF16)
    mid_ref[...] = stream + ob_ref[...]
    for part in range(3):
        qkv_ref[part] = mm_nt(normed, wqkv_ref[part]).astype(BF16)
    lane = lax.broadcasted_iota(jnp.int32, (WIN, 2 * HD), 1)
    low = lane < HD
    row_i = lax.broadcasted_iota(jnp.int32, (WIN, WIN), 0)
    col_i = lax.broadcasted_iota(jnp.int32, (WIN, WIN), 1)
    same_half = (row_i < LEN_A) == (col_i < LEN_A)
    scale = HD ** (-0.5)
    pairs = qkv_ref.shape[2] // (2 * HD)
    for win in range(TILE // WIN):
        spot = (half * (3 * TILE // WIN) + tile * (TILE // WIN) + win) % 4
        same_ref[...] = jnp.where(same_half, 0.0, jnp.where(spot < 2, -1e9, 0.0))
        rows = slice(win * WIN, (win + 1) * WIN)
        for pair in range(pairs):
            cols = slice(pair * 2 * HD, (pair + 1) * 2 * HD)
            q2 = qkv_ref[0, rows, cols] * jnp.asarray(scale, BF16)
            k2 = qkv_ref[1, rows, cols]
            v2 = qkv_ref[2, rows, cols]
            outs = []
            for j in range(2):
                q1 = jnp.where(low == (j == 0), q2, jnp.zeros_like(q2))
                scores = mm_nt(q1, k2) + same_ref[...]
                top = jnp.max(scores, axis=-1, keepdims=True)
                expo = jnp.exp(scores - top)
                total = jnp.sum(expo, axis=-1, keepdims=True)
                probs = (expo * (1.0 / total)).astype(BF16)
                probs_ref[2 * pair + j, win] = probs
                outs.append(mm(probs, v2))
            ctx_acc[rows, cols] = jnp.where(low, outs[0], outs[1]).astype(BF16)
    ctx_ref[...] = ctx_acc[...]
    mid_ref[...] += mm(ctx_acc[...], wo_ref[...])


def mlp_kernel(
    meta, mid_ref, gy_ref, wu_ref, bu_ref, wd_ref, gain_ref, shift_ref, db_ref,
    out_ref, gmid_ref, gw_ref, vec_ref, gbu_ref,
    acc_u, acc_d, n2_ref, n2t_ref, gyt_ref, mlp_ref, dn_ref,
):
    tile = pl.program_id(0)
    last = pl.num_programs(0) - 1
    pair = meta[1]
    ff = wu_ref.shape[2]

    @pl.when(tile == 0)
    def _():
        acc_u[...] = jnp.zeros_like(acc_u)
        acc_d[...] = jnp.zeros_like(acc_d)
        vec_ref[...] = jnp.zeros_like(vec_ref)
        gbu_ref[...] = jnp.zeros_like(gbu_ref)

    hat, inv = norm_stats(mid_ref[...])
    normed = (hat * gain_ref[...] + shift_ref[...]).astype(BF16)
    n2_ref[...] = normed
    n2t_ref[...] = normed.T
    gyt_ref[...] = gy_ref[...].T
    mlp_ref[...] = mid_ref[...] + db_ref[...]
    dn_ref[...] = jnp.zeros_like(dn_ref)

    def step(turn, own):
        group = lax.rem(2 * pair + turn, 4)
        pre = mm(n2_ref[...], wu_ref[group]) + bu_ref[group, 0:1]
        grad_act = mm_nt(gy_ref[...], wd_ref[group])
        square = pre * pre
        bend = jnp.tanh(pre * (GELU_C + (GELU_C * GELU_A) * square))
        half_in = 0.5 * pre
        up = 1.0 + bend
        act = (half_in * up).astype(BF16)
        slope = 0.5 * up + half_in * (1.0 - bend * bend) * (GELU_C + (3.0 * GELU_C * GELU_A) * square)
        grad_f = grad_act * slope
        grad_pre = grad_f.astype(BF16)
        mlp_ref[...] += mm(act, wd_ref[group])
        dn_ref[...] += mm_nt(grad_pre, wu_ref[group])
        if own:
            acc_u[turn] += mm(n2t_ref[...], grad_pre)
            acc_d[turn] += mm(gyt_ref[...], act)
            gbu_ref[turn, 0:1] += jnp.sum(grad_pre.astype(F32), axis=0, keepdims=True)

    lax.fori_loop(0, 2, lambda turn, c: (step(turn, True), c)[1], 0)
    lax.fori_loop(2, 4, lambda turn, c: (step(turn, False), c)[1], 0)

    out_ref[...] = mlp_ref[...].astype(BF16)
    hat, inv = norm_stats(mid_ref[...])
    top = gy_ref[...].astype(F32)
    dn = dn_ref[...]
    vec_ref[0:1] += jnp.sum(dn * hat, axis=0, keepdims=True)
    vec_ref[1:2] += jnp.sum(dn, axis=0, keepdims=True)
    gmid = top + norm_back(dn, gain_ref[...], hat, inv)
    vec_ref[2:3] += jnp.sum(gmid, axis=0, keepdims=True)
    vec_ref[3:4] += jnp.sum(top, axis=0, keepdims=True)
    gmid_ref[...] = gmid

    @pl.when(tile == last)
    def _():
        gw_ref[:, :, 0:ff] = acc_u[...].astype(BF16)
        gw_ref[:, :, ff : 2 * ff] = acc_d[...].astype(BF16)


def attn_bwd_kernel(
    meta, hidden_ref, emb_ref, gain_ref, shift_ref, wqkv_ref, wo_ref,
    qkv_ref, probs_ref, ctx_ref, gmid_ref,
    gh_ref, gw_ref, vec_ref, usum_ref,
    acc, gp_ref, gc_ref, n1t_ref, gmt_ref,
):
    tile = pl.program_id(0)
    last = pl.num_programs(0) - 1
    pair_id = meta[1]
    width = wo_ref.shape[1]
    part_w = width // 2

    @pl.when(tile == 0)
    def _():
        acc[...] = jnp.zeros_like(acc)
        vec_ref[...] = jnp.zeros_like(vec_ref)
        usum_ref[...] = jnp.zeros_like(usum_ref)

    own = pl.ds(pl.multiple_of(pair_id * part_w, 128), part_w)
    stream = stream_tile(hidden_ref, emb_ref, tile)
    hat, inv = norm_stats(stream)
    n1t_ref[...] = (hat * gain_ref[...] + shift_ref[...]).astype(BF16).T
    gm_low = gmid_ref[...].astype(BF16)
    gmt_ref[...] = gm_low.T
    gc_ref[...] = mm_nt(gm_low, wo_ref[...]).astype(BF16)
    acc[3] += mm(gmt_ref[...], ctx_ref[:, own])
    lane = lax.broadcasted_iota(jnp.int32, (WIN, 2 * HD), 1)
    low = lane < HD
    scale = HD ** (-0.5)
    pairs = width // (2 * HD)
    for win in range(TILE // WIN):
        rows = slice(win * WIN, (win + 1) * WIN)
        for pair in range(pairs):
            cols = slice(pair * 2 * HD, (pair + 1) * 2 * HD)
            q2 = qkv_ref[0, rows, cols]
            k2 = qkv_ref[1, rows, cols]
            v2 = qkv_ref[2, rows, cols]
            gc2 = gc_ref[rows, cols]
            dq, dk, dv = [], [], []
            for j in range(2):
                gc1 = jnp.where(low == (j == 0), gc2, jnp.zeros_like(gc2))
                probs_low = probs_ref[2 * pair + j, win]
                probs = probs_low.astype(F32)
                dprob = mm_nt(gc1, v2)
                mix = probs * dprob
                total = jnp.sum(mix, axis=-1, keepdims=True)
                grad_s = (mix - probs * total).astype(BF16)
                dv.append(mm_tn(probs_low, gc2))
                dk.append(mm_tn(grad_s, q2))
                dq.append(mm(grad_s, k2))
            gp_ref[0, rows, cols] = (jnp.where(low, dq[0], dq[1]) * scale).astype(BF16)
            gp_ref[1, rows, cols] = (jnp.where(low, dk[0], dk[1]) * scale).astype(BF16)
            gp_ref[2, rows, cols] = jnp.where(low, dv[0], dv[1]).astype(BF16)
    grad_n = mm(gp_ref[0], wqkv_ref[0])
    for part in range(1, 3):
        grad_n = grad_n + mm(gp_ref[part], wqkv_ref[part])
    for part in range(3):
        acc[part] += mm(n1t_ref[...], gp_ref[part, :, own])
    stream = stream_tile(hidden_ref, emb_ref, tile)
    hat, inv = norm_stats(stream)
    vec_ref[0:1] += jnp.sum(grad_n * hat, axis=0, keepdims=True)
    vec_ref[1:2] += jnp.sum(grad_n, axis=0, keepdims=True)
    grad_in = gmid_ref[...] + norm_back(grad_n, gain_ref[...], hat, inv)
    gh_ref[...] = grad_in.astype(BF16)
    for unit in range(TILE // LEN_A):
        usum_ref[pl.ds(tile * (TILE // LEN_A) + unit, 1), :] = jnp.sum(
            grad_in[unit * LEN_A : (unit + 1) * LEN_A], axis=0, keepdims=True
        )

    @pl.when(tile == last)
    def _():
        piece = part_w // 2
        for group in range(2):
            for part in range(4):
                gw_ref[group, :, part * piece : (part + 1) * piece] = acc[
                    part, :, group * piece : (group + 1) * piece
                ].astype(BF16)


def whole(shape):
    zeros = (0,) * len(shape)
    return pl.BlockSpec(shape, lambda i, meta: zeros, pipeline_mode=pl.Buffered(1))


def held(shape):
    zeros = (0,) * len(shape)
    return pl.BlockSpec(shape, lambda i, meta: zeros)


LIMIT = 62 * 1024 * 1024


def attn_fwd(meta, hidden, emb, gain, shift, wqkv, wo, ob):
    count, width = hidden.shape[0] // 2, hidden.shape[1]
    steps = count // TILE
    heads = width // HD
    tok = pl.BlockSpec((TILE, width), lambda i, meta: (i, 0))
    return pl.pallas_call(
        attn_fwd_kernel,
        name="attn_fwd",
        grid_spec=pltpu.PrefetchScalarGridSpec(
            num_scalar_prefetch=1,
            grid=(steps,),
            in_specs=[
                pl.BlockSpec((TILE, width), lambda i, meta: (meta[0] * steps + i, 0)),
                whole(emb.shape), whole((1, width)), whole((1, width)),
                whole(wqkv.shape), whole(wo.shape), whole((1, width)),
            ],
            out_specs=[
                pl.BlockSpec((3, TILE, width), lambda i, meta: (0, i, 0)),
                pl.BlockSpec((heads, TILE // WIN, WIN, WIN), lambda i, meta: (0, i, 0, 0)),
                tok,
                tok,
            ],
            scratch_shapes=[pltpu.VMEM((WIN, WIN), F32), pltpu.VMEM((TILE, width), BF16)],
        ),
        out_shape=[
            jax.ShapeDtypeStruct((3, count, width), BF16),
            jax.ShapeDtypeStruct((heads, count // WIN, WIN, WIN), BF16),
            jax.ShapeDtypeStruct((count, width), BF16),
            jax.ShapeDtypeStruct((count, width), F32),
        ],
        compiler_params=pltpu.CompilerParams(vmem_limit_bytes=LIMIT),
        cost_estimate=pl.CostEstimate(flops=12_000_000_000, bytes_accessed=30_000_000, transcendentals=5_000_000),
    )(meta, hidden, emb, gain, shift, wqkv, wo, ob)


def mlp(meta, mid, gy, wu, bu, wd, gain, shift, db):
    count, width = mid.shape
    steps = count // TILE
    ff = wu.shape[2]
    tok = pl.BlockSpec((TILE, width), lambda i, meta: (i, 0))
    return pl.pallas_call(
        mlp_kernel,
        name="mlp_both",
        grid_spec=pltpu.PrefetchScalarGridSpec(
            num_scalar_prefetch=1,
            grid=(steps,),
            in_specs=[
                tok,
                pl.BlockSpec((TILE, width), lambda i, meta: (meta[0] * steps + i, 0)),
                whole(wu.shape), whole(bu.shape), whole(wd.shape),
                whole((1, width)), whole((1, width)), whole((1, width)),
            ],
            out_specs=[tok, tok, whole((2, width, 2 * ff)), held((8, width)), held((2, 8, ff))],
            scratch_shapes=[
                pltpu.VMEM((2, width, ff), F32), pltpu.VMEM((2, width, ff), F32),
                pltpu.VMEM((TILE, width), BF16), pltpu.VMEM((width, TILE), BF16),
                pltpu.VMEM((width, TILE), BF16),
                pltpu.VMEM((TILE, width), F32), pltpu.VMEM((TILE, width), F32),
            ],
        ),
        out_shape=[
            jax.ShapeDtypeStruct((count, width), BF16),
            jax.ShapeDtypeStruct((count, width), F32),
            jax.ShapeDtypeStruct((2, width, 2 * ff), BF16),
            jax.ShapeDtypeStruct((8, width), F32),
            jax.ShapeDtypeStruct((2, 8, ff), F32),
        ],
        compiler_params=pltpu.CompilerParams(vmem_limit_bytes=LIMIT),
        cost_estimate=pl.CostEstimate(flops=36_000_000_000, bytes_accessed=30_000_000, transcendentals=5_000_000),
    )(meta, mid, gy, wu, bu, wd, gain, shift, db)


def attn_bwd(meta, hidden, emb, gain, shift, wqkv, wo, qkv, probs, ctx, gmid):
    count, width = gmid.shape
    steps = count // TILE
    heads = width // HD
    tok = pl.BlockSpec((TILE, width), lambda i, meta: (i, 0))
    return pl.pallas_call(
        attn_bwd_kernel,
        name="attn_bwd",
        grid_spec=pltpu.PrefetchScalarGridSpec(
            num_scalar_prefetch=1,
            grid=(steps,),
            in_specs=[
                pl.BlockSpec((TILE, width), lambda i, meta: (meta[0] * steps + i, 0)),
                whole(emb.shape), whole((1, width)), whole((1, width)),
                whole(wqkv.shape), whole(wo.shape),
                pl.BlockSpec((3, TILE, width), lambda i, meta: (0, i, 0)),
                pl.BlockSpec((heads, TILE // WIN, WIN, WIN), lambda i, meta: (0, i, 0, 0)),
                tok, tok,
            ],
            out_specs=[tok, whole((2, width, width)), held((8, width)), held(emb.shape)],
            scratch_shapes=[
                pltpu.VMEM((4, width, width // 2), F32),
                pltpu.VMEM((3, TILE, width), BF16), pltpu.VMEM((TILE, width), BF16),
                pltpu.VMEM((width, TILE), BF16), pltpu.VMEM((width, TILE), BF16),
            ],
        ),
        out_shape=[
            jax.ShapeDtypeStruct((count, width), BF16),
            jax.ShapeDtypeStruct((2, width, width), BF16),
            jax.ShapeDtypeStruct((8, width), F32),
            jax.ShapeDtypeStruct(emb.shape, F32),
        ],
        compiler_params=pltpu.CompilerParams(vmem_limit_bytes=LIMIT),
        cost_estimate=pl.CostEstimate(flops=20_000_000_000, bytes_accessed=40_000_000, transcendentals=0),
    )(meta, hidden, emb, gain, shift, wqkv, wo, qkv, probs, ctx, gmid)
ARRAYS = 4


def gather_kernel(
    wqkv, wo, wu, wd, bu, wqkv_f, wo_f, wu_f, wd_f, bu_f,
    hold_qkv, hold_wo, hold_wu, hold_wd, hold_bu,
    loc_sem, z_send, z_recv, b_send, b_recv, n_send, n_recv,
):
    place = lax.axis_index("dp")
    member = lax.axis_index("mp")
    base = place - lax.rem(place, 8)
    spot = place - base
    bit0 = lax.rem(spot, 2)
    bit1 = lax.rem(spot // 2, 2)
    bit2 = spot // 4

    def flip(where, bit, size):
        return where + size - 2 * size * bit

    near = {
        "core": {"dp": flip(place, bit0, 1), "mp": member},
        "x": {"dp": flip(place, bit1, 2), "mp": member},
        "y": {"dp": flip(place, bit2, 4), "mp": member},
    }
    mine = spot
    from_x = flip(spot, bit1, 2)
    from_y = flip(spot, bit2, 4)
    from_d = flip(from_x, bit2, 4)

    def peer(turn):
        return {"dp": place, "mp": lax.rem(member + turn, 4)}

    barrier = pltpu.get_barrier_semaphore()
    for target in (peer(1), peer(2), peer(3), near["core"], near["x"], near["y"]):
        pl.semaphore_signal(barrier, inc=1, device_id=target, device_id_type=pl.DeviceIdType.MESH)
    pl.semaphore_wait(barrier, 6)

    rows_a = wo.shape[0]
    step_a = rows_a // 8
    step_m = wu.shape[1 - 1] // 8

    def full_at(array, shard, piece):
        if array == 0:
            return wqkv_f.at[:, pl.ds(shard * rows_a + piece * step_a, step_a), :]
        if array == 1:
            return wo_f.at[pl.ds(shard * rows_a + piece * step_a, step_a), :]
        full = wu_f if array == 2 else wd_f
        return full.at[shard, pl.ds(piece * step_m, step_m), :]

    def own_at(array, piece):
        if array == 0:
            return wqkv.at[:, pl.ds(piece * step_a, step_a), :]
        if array == 1:
            return wo.at[pl.ds(piece * step_a, step_a), :]
        return (wu if array == 2 else wd).at[pl.ds(piece * step_m, step_m), :]

    sends = []
    z_recvs, n_recvs = {}, {}
    for array in range(ARRAYS):
        for turn in (2, 1, 3):
            copy = pltpu.make_async_remote_copy(
                src_ref=own_at(array, spot),
                dst_ref=full_at(array, member, spot),
                send_sem=z_send.at[array, turn - 1],
                recv_sem=z_recv.at[array, turn - 1],
                device_id=peer(turn),
                device_id_type=pl.DeviceIdType.MESH,
            )
            copy.start()
            sends.append(copy)
            z_recvs[array, turn] = copy
        if array == 0:
            for turn in (1, 2, 3):
                copy = pltpu.make_async_remote_copy(
                    src_ref=bu, dst_ref=bu_f.at[member],
                    send_sem=b_send.at[turn - 1], recv_sem=b_recv.at[turn - 1],
                    device_id=peer(turn), device_id_type=pl.DeviceIdType.MESH,
                )
                copy.start()
                sends.append(copy)
                n_recvs["bias", turn] = copy

    own_full = (
        (wqkv, hold_qkv, wqkv_f.at[:, pl.ds(member * rows_a, rows_a), :]),
        (wo, hold_wo, wo_f.at[pl.ds(member * rows_a, rows_a), :]),
        (wu, hold_wu, wu_f.at[member]),
        (wd, hold_wd, wd_f.at[member]),
        (bu, hold_bu, bu_f.at[member]),
    )
    into = [pltpu.make_async_copy(src, hold, loc_sem.at[n]) for n, (src, hold, _) in enumerate(own_full)]
    for copy in into:
        copy.start()
    outof = []
    for n, (_, hold, dst) in enumerate(own_full):
        into[n].wait()
        copy = pltpu.make_async_copy(hold, dst, loc_sem.at[5 + n])
        copy.start()
        outof.append(copy)

    def push(array, turn, kind, piece, target):
        shard = lax.rem(member + 4 - turn, 4)
        copy = pltpu.make_async_remote_copy(
            src_ref=full_at(array, shard, piece),
            dst_ref=full_at(array, shard, piece),
            send_sem=n_send.at[array, turn - 1, kind],
            recv_sem=n_recv.at[array, turn - 1, kind],
            device_id=near[target],
            device_id_type=pl.DeviceIdType.MESH,
        )
        copy.start()
        sends.append(copy)
        n_recvs[array, turn, kind] = copy

    order = (1, 3, 2)

    def stage_z(array):
        for turn in order:
            z_recvs[array, turn].wait_recv()
            push(array, turn, 0, mine, "x")
            push(array, turn, 1, mine, "y")
            push(array, turn, 3, mine, "core")

    def stage_near(array):
        for turn in order:
            n_recvs[array, turn, 0].wait_recv()
            if (array + turn) % 2 == 0:
                push(array, turn, 2, from_x, "y")
            push(array, turn, 4, from_x, "core")
            n_recvs[array, turn, 1].wait_recv()
            if (array + turn) % 2 == 1:
                push(array, turn, 2, from_y, "x")
            push(array, turn, 5, from_y, "core")

    def stage_far(array):
        for turn in order:
            n_recvs[array, turn, 2].wait_recv()
            push(array, turn, 6, from_d, "core")

    for step in range(ARRAYS + 2):
        if step < ARRAYS:
            stage_z(step)
        if 0 <= step - 1 < ARRAYS:
            stage_near(step - 1)
        if 0 <= step - 2 < ARRAYS:
            stage_far(step - 2)
    for array in range(ARRAYS):
        for turn in order:
            for kind in range(3, 7):
                n_recvs[array, turn, kind].wait_recv()
    for turn in (1, 2, 3):
        n_recvs["bias", turn].wait_recv()
    for copy in sends:
        copy.wait_send()
    for copy in outof:
        copy.wait()


def gather_weights(wqkv, wo, wu, wd, bu):
    anywhere = pl.BlockSpec(memory_space=pl.ANY)
    rows, width = wo.shape
    ff = wu.shape[1]
    return pl.pallas_call(
        gather_kernel,
        name="gather_weights",
        in_specs=[anywhere] * 5,
        out_specs=[anywhere] * 5,
        out_shape=[
            jax.ShapeDtypeStruct((3, 4 * rows, width), BF16),
            jax.ShapeDtypeStruct((4 * rows, width), BF16),
            jax.ShapeDtypeStruct((4, width, ff), BF16),
            jax.ShapeDtypeStruct((4, ff, width), BF16),
            jax.ShapeDtypeStruct((4,) + bu.shape, F32),
        ],
        scratch_shapes=[
            pltpu.VMEM(wqkv.shape, BF16), pltpu.VMEM(wo.shape, BF16),
            pltpu.VMEM(wu.shape, BF16), pltpu.VMEM(wd.shape, BF16), pltpu.VMEM(bu.shape, F32),
            pltpu.SemaphoreType.DMA((10,)),
            pltpu.SemaphoreType.DMA((ARRAYS, 3)), pltpu.SemaphoreType.DMA((ARRAYS, 3)),
            pltpu.SemaphoreType.DMA((3,)), pltpu.SemaphoreType.DMA((3,)),
            pltpu.SemaphoreType.DMA((ARRAYS, 3, 7)), pltpu.SemaphoreType.DMA((ARRAYS, 3, 7)),
        ],
        compiler_params=pltpu.CompilerParams(
            collective_id=1, has_side_effects=True, vmem_limit_bytes=LIMIT
        ),
    )(wqkv, wo, wu, wd, bu)
def local(
    hidden, timesteps, cotangent, time_table, first_gain, first_shift, qkv_weight, out_weight,
    out_bias, second_gain, second_shift, up_weight, up_bias, down_weight, down_bias,
):
    count, width = hidden.shape
    steps = time_table.shape[0]
    local_ff = up_weight.shape[1]
    member = lax.axis_index("mp")
    half = lax.rem(member, 2)
    pair = member // 2
    meta = jnp.stack([half, pair]).astype(jnp.int32)
    units = count // (2 * LEN_A)
    unit = half * units + jnp.arange(units, dtype=jnp.int32)
    within = unit % 8
    row_of = unit // 8 * 6 + jnp.where(within < 4, within, 4 + (within - 4) // 2)
    unit_step = jnp.take(timesteps, row_of)
    emb = jnp.take(time_table, unit_step, axis=0).astype(F32)
    emb = jnp.concatenate([emb, jnp.zeros((16 - units, width), F32)], axis=0)

    def row(v):
        return v.reshape(1, -1)

    wqkv_f, wo_f, wu_f, wd_f, bu_f = gather_weights(
        jnp.swapaxes(qkv_weight, 1, 2),
        out_weight,
        up_weight,
        down_weight,
        jnp.broadcast_to(row(up_bias), (8, local_ff)),
    )
    qkv, probs, ctx, mid = attn_fwd(
        meta, hidden, emb, row(first_gain), row(first_shift), wqkv_f, wo_f, row(out_bias)
    )
    out_own, gmid, gw_mlp, vec_mlp, gbu = mlp(
        meta, mid, cotangent, wu_f, bu_f, wd_f, row(second_gain), row(second_shift), row(down_bias)
    )
    swap = [(0, 1), (1, 0), (2, 3), (3, 2)]
    out_other = lax.ppermute(out_own, "mp", swap)
    gh_own, gw_attn, vec_attn, usum = attn_bwd(
        meta, hidden, emb, row(first_gain), row(first_shift), wqkv_f, wo_f, qkv, probs, ctx, gmid
    )
    gh_other = lax.ppermute(gh_own, "mp", swap)

    def join(own, other):
        first = jnp.where(half == 0, own, other)
        second = jnp.where(half == 0, other, own)
        return jnp.concatenate([first, second], axis=0)

    output = join(out_own, out_other)
    grad_hidden = join(gh_own, gh_other)

    def spread(grads):
        mine = lax.psum_scatter(grads, "dp", scatter_dimension=1, tiled=True)
        keep = jnp.where(half == 0, mine[0], mine[1]).astype(F32)
        give = jnp.where(half == 0, mine[1], mine[0])
        return keep + lax.ppermute(give, "mp", swap).astype(F32)

    g_mlp = spread(gw_mlp)
    g_attn = spread(gw_attn)
    grad_up = g_mlp[:, :local_ff]
    grad_down = g_mlp[:, local_ff:].T
    head_w = qkv_weight.shape[2]
    grad_qkv = jnp.stack([g_attn[:, c * head_w : (c + 1) * head_w] for c in range(3)])
    grad_out = g_attn[:, 3 * head_w :].T

    chosen = (unit_step[:, None] == lax.broadcasted_iota(jnp.int32, (1, steps), 1)).astype(F32)
    part_w = width // 2
    sums = lax.dynamic_slice_in_dim(usum[:units], pair * part_w, part_w, 1)
    table = jnp.dot(chosen.T, sums, precision=lax.Precision.HIGHEST, preferred_element_type=F32)
    left, right = table[:, : part_w // 2], table[:, part_w // 2 :]
    table = jnp.where(half == 0, left, right) + lax.ppermute(
        jnp.where(half == 0, right, left), "mp", swap
    )
    table = lax.psum(table, "dp")

    slots = jnp.where(
        (jnp.arange(4) // 2 == pair)[:, None], jnp.concatenate([gbu[:, 0], gbu[:, 0]], axis=0), 0.0
    )
    small = jnp.concatenate([0.5 * vec_attn[:2], 0.5 * vec_mlp[:4], slots], axis=0)
    small = lax.psum(small, ("dp", "mp"))
    grad_up_bias = lax.dynamic_slice_in_dim(small[6:], member, 1, 0)[0]
    return (
        output, grad_hidden, table, small[0], small[1], grad_qkv, grad_out, small[4],
        small[2], small[3], grad_up, grad_up_bias, grad_down, small[5],
    )


def solution(mesh):
    return jax.shard_map(
        local,
        mesh=mesh,
        in_specs=(
            P("dp", None), P("dp"), P("dp", None), P(), P(), P(), P(None, None, "mp"),
            P("mp", None), P(), P(), P(), P(None, "mp"), P("mp"), P("mp", None), P(),
        ),
        out_specs=(
            P("dp", None), P("dp", None), P(None, "mp"), P(), P(), P(None, "dp", "mp"),
            P("mp", "dp"), P(), P(), P(), P("dp", "mp"), P("mp"), P("mp", "dp"), P(),
        ),
        check_vma=False,
    )
```

```python
from functools import partial

import jax
import jax.numpy as jnp
from jax import lax
from jax.experimental import pallas as pl
from jax.experimental.pallas import tpu as pltpu
from jax.sharding import PartitionSpec as P

F32 = jnp.float32
BF16 = jnp.bfloat16
HD = 64
LEN_A = 128
LEN_B = 256
BLOCK = 512
WIN = 256
TILE = 512
GROUP = 8
EPS = 1e-05
GELU_C = 0.7978845608028654
GELU_A = 0.044715


def mm(a, b):
    return lax.dot_general(a, b, (((1,), (0,)), ((), ())), preferred_element_type=F32)


def mm_nt(a, b):
    return lax.dot_general(a, b, (((1,), (1,)), ((), ())), preferred_element_type=F32)


def mm_tn(a, b):
    return lax.dot_general(a, b, (((0,), (0,)), ((), ())), preferred_element_type=F32)


def norm_stats(rows):
    centre = jnp.mean(rows, axis=-1, keepdims=True)
    offset = rows - centre
    spread = jnp.mean(offset * offset, axis=-1, keepdims=True)
    inv = lax.rsqrt(spread + EPS)
    return offset * inv, inv


def norm_back(grad, gain, hat, inv):
    dhat = grad * gain
    first = jnp.mean(dhat, axis=-1, keepdims=True)
    second = jnp.mean(dhat * hat, axis=-1, keepdims=True)
    return inv * (dhat - first - hat * second)


def stream_tile(hidden_ref, emb_ref, tile):
    parts = []
    for unit in range(TILE // LEN_A):
        row = emb_ref[pl.ds(tile * (TILE // LEN_A) + unit, 1), :]
        parts.append(hidden_ref[unit * LEN_A : (unit + 1) * LEN_A, :].astype(F32) + row)
    return jnp.concatenate(parts, axis=0)


def attn_fwd_kernel(
    meta, hidden_ref, emb_ref, gain_ref, shift_ref, wqkv_ref, wo_ref, ob_ref,
    qkv_ref, probs_ref, ctx_ref, mid_ref, same_ref, ctx_acc,
):
    tile = pl.program_id(0)
    half = meta[0]
    stream = stream_tile(hidden_ref, emb_ref, tile)
    hat, _ = norm_stats(stream)
    normed = (hat * gain_ref[...] + shift_ref[...]).astype(BF16)
    mid_ref[...] = stream + ob_ref[...]
    for part in range(3):
        qkv_ref[part] = mm_nt(normed, wqkv_ref[part]).astype(BF16)
    lane = lax.broadcasted_iota(jnp.int32, (WIN, 2 * HD), 1)
    low = lane < HD
    row_i = lax.broadcasted_iota(jnp.int32, (WIN, WIN), 0)
    col_i = lax.broadcasted_iota(jnp.int32, (WIN, WIN), 1)
    same_half = (row_i < LEN_A) == (col_i < LEN_A)
    scale = HD ** (-0.5)
    pairs = qkv_ref.shape[2] // (2 * HD)
    for win in range(TILE // WIN):
        spot = (half * (3 * TILE // WIN) + tile * (TILE // WIN) + win) % 4
        same_ref[...] = jnp.where(same_half, 0.0, jnp.where(spot < 2, -1e9, 0.0))
        rows = slice(win * WIN, (win + 1) * WIN)
        for pair in range(pairs):
            cols = slice(pair * 2 * HD, (pair + 1) * 2 * HD)
            q2 = qkv_ref[0, rows, cols] * jnp.asarray(scale, BF16)
            k2 = qkv_ref[1, rows, cols]
            v2 = qkv_ref[2, rows, cols]
            outs = []
            for j in range(2):
                q1 = jnp.where(low == (j == 0), q2, jnp.zeros_like(q2))
                scores = mm_nt(q1, k2) + same_ref[...]
                top = jnp.max(scores, axis=-1, keepdims=True)
                expo = jnp.exp(scores - top)
                total = jnp.sum(expo, axis=-1, keepdims=True)
                probs = (expo * (1.0 / total)).astype(BF16)
                probs_ref[2 * pair + j, win] = probs
                outs.append(mm(probs, v2))
            ctx_acc[rows, cols] = jnp.where(low, outs[0], outs[1]).astype(BF16)
    ctx_ref[...] = ctx_acc[...]
    mid_ref[...] += mm(ctx_acc[...], wo_ref[...])


def line_up(n):
    place = lax.axis_index("dp")
    spot = lax.rem(place, GROUP)
    return place - spot, spot


def ahead(ref, rows, dst, send, recv, target):
    return pltpu.make_async_remote_copy(
        src_ref=ref.at[rows] if rows is not None else ref,
        dst_ref=dst.at[rows] if rows is not None else dst,
        send_sem=send, recv_sem=recv, device_id=target, device_id_type=pl.DeviceIdType.MESH,
    )


def mate_of(member):
    return {"dp": lax.axis_index("dp"), "mp": member + 1 - 2 * lax.rem(member, 2)}


def greet(targets):
    barrier = pltpu.get_barrier_semaphore()
    for target in targets:
        pl.semaphore_signal(barrier, inc=1, device_id=target, device_id_type=pl.DeviceIdType.MESH)
    pl.semaphore_wait(barrier, len(targets))


def mlp_kernel(
    mid_ref, gy_ref, wu_ref, bu_ref, wd_ref, gain_ref, shift_ref, db_ref,
    out_ref, gmid_ref, gw_ref, vec_ref, gbu_ref,
    acc_u, acc_d, n2_ref, n2t_ref, gyt_ref, mlp_ref, dn_ref, stage, loc_sem, send_sem, recv_sem,
):
    tile = pl.program_id(0)
    steps = pl.num_programs(0)
    last = steps - 1
    member = lax.axis_index("mp")
    half = lax.rem(member, 2)
    pair = member // 2
    mate = mate_of(member)
    ff = wu_ref.shape[2]
    total = out_ref.shape[0] // (2 * TILE)

    def rows_of(t):
        return pl.ds(pl.multiple_of((half * total + t) * TILE, TILE), TILE)

    def local_copy(t):
        return pltpu.make_async_copy(stage.at[lax.rem(t, 2)], out_ref.at[rows_of(t)], loc_sem.at[t])

    def remote_copy(t):
        return ahead(out_ref, rows_of(t), out_ref, send_sem.at[t], recv_sem.at[t], mate)

    @pl.when(tile == 0)
    def _():
        acc_u[...] = jnp.zeros_like(acc_u)
        acc_d[...] = jnp.zeros_like(acc_d)
        vec_ref[...] = jnp.zeros_like(vec_ref)
        gbu_ref[...] = jnp.zeros_like(gbu_ref)
        greet([mate])

    @pl.when(tile > 0)
    def _():
        local_copy(tile - 1).wait()
        remote_copy(tile - 1).start()

    hat, inv = norm_stats(mid_ref[...])
    normed = (hat * gain_ref[...] + shift_ref[...]).astype(BF16)
    n2_ref[...] = normed
    n2t_ref[...] = normed.T
    gyt_ref[...] = gy_ref[...].T
    mlp_ref[...] = mid_ref[...] + db_ref[...]
    dn_ref[...] = jnp.zeros_like(dn_ref)

    def step(turn, own):
        group = lax.rem(2 * pair + turn, 4)
        pre = mm(n2_ref[...], wu_ref[group]) + bu_ref[group, 0:1]
        grad_act = mm_nt(gy_ref[...], wd_ref[group])
        square = pre * pre
        bend = jnp.tanh(pre * (GELU_C + (GELU_C * GELU_A) * square))
        half_in = 0.5 * pre
        up = 1.0 + bend
        act = (half_in * up).astype(BF16)
        slope = 0.5 * up + half_in * (1.0 - bend * bend) * (GELU_C + (3.0 * GELU_C * GELU_A) * square)
        grad_f = grad_act * slope
        grad_pre = grad_f.astype(BF16)
        mlp_ref[...] += mm(act, wd_ref[group])
        dn_ref[...] += mm_nt(grad_pre, wu_ref[group])
        if own:
            acc_u[turn] += mm(n2t_ref[...], grad_pre)
            acc_d[turn] += mm(gyt_ref[...], act)
            gbu_ref[turn, 0:1] += jnp.sum(grad_pre.astype(F32), axis=0, keepdims=True)

    lax.fori_loop(0, 2, lambda turn, c: (step(turn, True), c)[1], 0)
    lax.fori_loop(2, 4, lambda turn, c: (step(turn, False), c)[1], 0)

    stage[lax.rem(tile, 2)] = mlp_ref[...].astype(BF16)
    hat, inv = norm_stats(mid_ref[...])
    top = gy_ref[...].astype(F32)
    dn = dn_ref[...]
    vec_ref[0:1] += jnp.sum(dn * hat, axis=0, keepdims=True)
    vec_ref[1:2] += jnp.sum(dn, axis=0, keepdims=True)
    gmid = top + norm_back(dn, gain_ref[...], hat, inv)
    vec_ref[2:3] += jnp.sum(gmid, axis=0, keepdims=True)
    vec_ref[3:4] += jnp.sum(top, axis=0, keepdims=True)
    gmid_ref[...] = gmid
    local_copy(tile).start()

    @pl.when(tile == last)
    def _():
        gw_ref[:, :, 0:ff] = acc_u[...].astype(BF16)
        gw_ref[:, :, ff : 2 * ff] = acc_d[...].astype(BF16)
        local_copy(tile).wait()
        for t in range(total - 1):
            remote_copy(t).wait_send()
            remote_copy(t).wait_recv()


def attn_bwd_kernel(
    hidden_ref, emb_ref, gain_ref, shift_ref, wqkv_ref, wo_ref,
    qkv_ref, probs_ref, ctx_ref, gmid_ref, gwm_ref, vecm_ref, gbu_ref, out_in,
    out_ref, gh_ref, gm_ref, ga_ref, vec_out, u_out,
    acc, gp_ref, gc_ref, n1t_ref, gmt_ref, vec_ref, usum_ref, stage,
    m_own, m_core, m_sum, m_chip, m_give, m_got,
    a_src, a_core, a_sum, a_chip, a_give, a_got,
    s_src, s_rcv, v_src, v_rcv, u_give, u_got,
    own_sem, out_send, out_recv, loc_sem, gh_send, gh_recv,
    core_send, core_recv, chip_send, chip_recv, give_send, give_recv,
    s_send, s_recv, v_send, v_recv, u_send, u_recv,
):
    tile = pl.program_id(0)
    last = pl.num_programs(0) - 1
    member = lax.axis_index("mp")
    half = lax.rem(member, 2)
    pair_id = member // 2
    width = wo_ref.shape[1]
    part_w = width // 2
    piece = part_w // 2
    share = width // GROUP
    total = out_ref.shape[0] // (2 * TILE)
    base, spot = line_up(0)
    core = lax.rem(spot, 2)
    chip = spot // 2
    bit_x = lax.rem(chip, 2)
    bit_y = chip // 2
    mate = mate_of(member)
    flips = (
        chip + 1 - 2 * bit_x,
        chip + 2 - 4 * bit_y,
        3 - chip,
    )

    def device(where):
        return {"dp": base + where, "mp": member}

    sibling = device(spot + 1 - 2 * core)
    others = [device(lax.rem(spot + turn, GROUP)) for turn in range(1, GROUP)]
    line = [{"dp": base + spot, "mp": lax.rem(member + turn, 4)} for turn in range(1, 4)]

    def rows_of(t):
        return pl.ds(pl.multiple_of((half * total + t) * TILE, TILE), TILE)

    def share_of(where):
        return pl.ds(pl.multiple_of(where * share, 32), share)

    def out_copy(t):
        return ahead(out_ref, rows_of(t), out_ref, out_send, out_recv, mate)

    def gh_local(t):
        return pltpu.make_async_copy(stage.at[lax.rem(t, 2)], gh_ref.at[rows_of(t)], loc_sem.at[t])

    def gh_copy(t):
        return ahead(gh_ref, rows_of(t), gh_ref, gh_send.at[t], gh_recv.at[t], mate)

    def own_copy(k):
        return pltpu.make_async_copy(gwm_ref.at[:, share_of(2 * k + core), :], m_own.at[k], own_sem.at[k])

    def core_copy(kind, k):
        src, dst = ((gwm_ref, m_core), (a_src, a_core))[kind]
        return pltpu.make_async_remote_copy(
            src_ref=src.at[:, share_of(2 * k + 1 - core), :], dst_ref=dst.at[k],
            send_sem=core_send.at[kind, k], recv_sem=core_recv.at[kind, k],
            device_id=sibling, device_id_type=pl.DeviceIdType.MESH,
        )

    def chip_copy(kind, r):
        src, dst = ((m_sum, m_chip), (a_sum, a_chip))[kind]
        return pltpu.make_async_remote_copy(
            src_ref=src.at[flips[r]], dst_ref=dst.at[r],
            send_sem=chip_send.at[kind, r], recv_sem=chip_recv.at[kind, r],
            device_id=device(2 * flips[r] + core), device_id_type=pl.DeviceIdType.MESH,
        )

    def give_copy(kind):
        src, dst = ((m_give, m_got), (a_give, a_got))[kind]
        return ahead(src, None, dst, give_send.at[kind], give_recv.at[kind], mate)

    def small_copy(n):
        return pltpu.make_async_remote_copy(
            src_ref=s_src, dst_ref=s_rcv.at[spot],
            send_sem=s_send.at[n], recv_sem=s_recv.at[n],
            device_id=others[n], device_id_type=pl.DeviceIdType.MESH,
        )

    def line_copy(n):
        return pltpu.make_async_remote_copy(
            src_ref=v_src, dst_ref=v_rcv.at[member],
            send_sem=v_send.at[n], recv_sem=v_recv.at[n],
            device_id=line[n], device_id_type=pl.DeviceIdType.MESH,
        )

    def u_copy():
        return ahead(u_give, None, u_got, u_send, u_recv, mate)

    @pl.when(tile == 0)
    def _():
        acc[...] = jnp.zeros_like(acc)
        vec_ref[...] = jnp.zeros_like(vec_ref)
        usum_ref[...] = jnp.zeros_like(usum_ref)
        greet(others + line)
        out_copy(total - 1).start()
        for k in range(4):
            core_copy(0, k).start()
        for k in range(4):
            own_copy(k).start()

    @pl.when(tile > 0)
    def _():
        gh_local(tile - 1).wait()
        gh_copy(tile - 1).start()

    own = pl.ds(pl.multiple_of(pair_id * part_w, 128), part_w)
    stream = stream_tile(hidden_ref, emb_ref, tile)
    hat, inv = norm_stats(stream)
    n1t_ref[...] = (hat * gain_ref[...] + shift_ref[...]).astype(BF16).T
    gm_low = gmid_ref[...].astype(BF16)
    gmt_ref[...] = gm_low.T
    gc_ref[...] = mm_nt(gm_low, wo_ref[...]).astype(BF16)
    acc[3] += mm(gmt_ref[...], ctx_ref[:, own])
    lane = lax.broadcasted_iota(jnp.int32, (WIN, 2 * HD), 1)
    low = lane < HD
    scale = HD ** (-0.5)
    pairs = width // (2 * HD)
    for win in range(TILE // WIN):
        rows = slice(win * WIN, (win + 1) * WIN)
        for pair in range(pairs):
            cols = slice(pair * 2 * HD, (pair + 1) * 2 * HD)
            q2 = qkv_ref[0, rows, cols]
            k2 = qkv_ref[1, rows, cols]
            v2 = qkv_ref[2, rows, cols]
            gc2 = gc_ref[rows, cols]
            dq, dk, dv = [], [], []
            for j in range(2):
                gc1 = jnp.where(low == (j == 0), gc2, jnp.zeros_like(gc2))
                probs_low = probs_ref[2 * pair + j, win]
                probs = probs_low.astype(F32)
                dprob = mm_nt(gc1, v2)
                mix = probs * dprob
                total_row = jnp.sum(mix, axis=-1, keepdims=True)
                grad_s = (mix - probs * total_row).astype(BF16)
                dv.append(mm_tn(probs_low, gc2))
                dk.append(mm_tn(grad_s, q2))
                dq.append(mm(grad_s, k2))
            gp_ref[0, rows, cols] = (jnp.where(low, dq[0], dq[1]) * scale).astype(BF16)
            gp_ref[1, rows, cols] = (jnp.where(low, dk[0], dk[1]) * scale).astype(BF16)
            gp_ref[2, rows, cols] = jnp.where(low, dv[0], dv[1]).astype(BF16)

    @pl.when(tile == 0)
    def _():
        for k in range(4):
            own_copy(k).wait()
            core_copy(0, k).wait_recv()
            m_sum[k] = (m_own[k].astype(F32) + m_core[k].astype(F32)).astype(BF16)

    grad_n = mm(gp_ref[0], wqkv_ref[0])
    for part in range(1, 3):
        grad_n = grad_n + mm(gp_ref[part], wqkv_ref[part])
    for part in range(3):
        acc[part] += mm(n1t_ref[...], gp_ref[part, :, own])

    @pl.when(tile == 0)
    def _():
        for r in range(3):
            chip_copy(0, r).start()

    stream = stream_tile(hidden_ref, emb_ref, tile)
    hat, inv = norm_stats(stream)
    vec_ref[0:1] += jnp.sum(grad_n * hat, axis=0, keepdims=True)
    vec_ref[1:2] += jnp.sum(grad_n, axis=0, keepdims=True)
    grad_in = gmid_ref[...] + norm_back(grad_n, gain_ref[...], hat, inv)
    stage[lax.rem(tile, 2)] = grad_in.astype(BF16)
    for unit in range(TILE // LEN_A):
        usum_ref[pl.ds(tile * (TILE // LEN_A) + unit, 1), :] = jnp.sum(
            grad_in[unit * LEN_A : (unit + 1) * LEN_A], axis=0, keepdims=True
        )
    gh_local(tile).start()

    @pl.when(tile == last)
    def _():
        units = usum_ref.shape[0]
        for group in range(2):
            for part in range(4):
                a_src[group, :, part * piece : (part + 1) * piece] = acc[
                    part, :, group * piece : (group + 1) * piece
                ].astype(BF16)
        s_src[0:units, :] = usum_ref[:, own]
        for left in range(2):
            cols = slice(left * part_w, (left + 1) * part_w)
            at = units + 8 * left
            s_src[at : at + 2, :] = vec_ref[0:2, cols]
            s_src[at + 2 : at + 6, :] = vecm_ref[0:4, cols]
            s_src[at + 6 : at + 7, :] = gbu_ref[0, 0:1, cols]
            s_src[at + 7 : at + 8, :] = gbu_ref[1, 0:1, cols]
        gh_local(tile).wait()
        gh_copy(tile).start()
        for k in range(4):
            core_copy(1, k).start()
        s_rcv[spot] = s_src[...]
        for n in range(GROUP - 1):
            small_copy(n).start()
        for r in range(3):
            chip_copy(0, r).wait_recv()
        kept_m = m_sum[chip, half].astype(F32)
        give_m = m_sum[chip, 1 - half].astype(F32)
        for r in range(3):
            kept_m = kept_m + m_chip[r, half].astype(F32)
            give_m = give_m + m_chip[r, 1 - half].astype(F32)
        m_give[...] = give_m.astype(BF16)
        gm_ref[...] = kept_m
        for k in range(4):
            core_copy(1, k).wait_recv()
            a_sum[k] = (
                a_src[:, share_of(2 * k + core), :].astype(F32) + a_core[k].astype(F32)
            ).astype(BF16)
        give_copy(0).start()
        for n in range(GROUP - 1):
            small_copy(n).wait_recv()
        for r in range(3):
            chip_copy(1, r).start()
        v_sum = s_rcv[0, units : units + 16, :]
        for n in range(1, GROUP):
            v_sum = v_sum + s_rcv[n, units : units + 16, :]
        v_src[...] = v_sum
        v_rcv[member] = v_sum
        for n in range(GROUP):
            whole_u = s_rcv[n, 0:units, :]
            left, right = whole_u[:, :piece], whole_u[:, piece:]
            u_give[n] = jnp.where(half == 0, right, left)
            u_out[0, n] = jnp.where(half == 0, left, right)
        for n in range(3):
            line_copy(n).start()
        u_copy().start()
        give_copy(0).wait_recv()
        gm_ref[...] += m_got[...].astype(F32)
        for n in range(3):
            line_copy(n).wait_recv()
        every = 0.5 * ((v_rcv[0] + v_rcv[1]) + (v_rcv[2] + v_rcv[3]))
        other = member + 1 - 2 * half
        mine = v_rcv[member] + v_rcv[other]
        for left in range(2):
            cols = slice(left * part_w, (left + 1) * part_w)
            at = 8 * left
            vec_out[0:6, cols] = every[at : at + 6]
            vec_out[6:7, cols] = jnp.where(half == 0, mine[at + 6 : at + 7], mine[at + 7 : at + 8])
        u_copy().wait_recv()
        u_out[1] = u_got[...]
        for r in range(3):
            chip_copy(1, r).wait_recv()
        kept_a = a_sum[chip, half].astype(F32)
        give_a = a_sum[chip, 1 - half].astype(F32)
        for r in range(3):
            kept_a = kept_a + a_chip[r, half].astype(F32)
            give_a = give_a + a_chip[r, 1 - half].astype(F32)
        a_give[...] = give_a.astype(BF16)
        ga_ref[...] = kept_a
        give_copy(1).start()
        give_copy(1).wait_recv()
        ga_ref[...] += a_got[...].astype(F32)
        out_copy(total - 1).wait_recv()
        out_copy(total - 1).wait_send()
        for t in range(total):
            gh_copy(t).wait_recv()
            gh_copy(t).wait_send()
        for kind in range(2):
            for k in range(4):
                core_copy(kind, k).wait_send()
            for r in range(3):
                chip_copy(kind, r).wait_send()
            give_copy(kind).wait_send()
        for n in range(GROUP - 1):
            small_copy(n).wait_send()
        for n in range(3):
            line_copy(n).wait_send()
        u_copy().wait_send()


def finish_kernel(
    out_in, gh_in, gm_ref, ga_ref, vec_ref, u_ref, ts_ref,
    out_ref, gh_ref, table_ref, g1_ref, s1_ref, qkv_ref, wo_ref, ob_ref,
    g2_ref, s2_ref, up_ref, ub_ref, down_ref, db_ref,
):
    out_ref[...] = out_in[...]
    gh_ref[...] = gh_in[...]

    @pl.when(pl.program_id(0) == 0)
    def _():
        ff = up_ref.shape[1]
        piece = qkv_ref.shape[2]
        up_ref[...] = gm_ref[:, 0:ff]
        down_ref[...] = gm_ref[:, ff : 2 * ff].T
        for part in range(3):
            qkv_ref[part] = ga_ref[:, part * piece : (part + 1) * piece]
        wo_ref[...] = ga_ref[:, 3 * piece : 4 * piece].T
        for n, ref in enumerate((g1_ref, s1_ref, g2_ref, s2_ref, ob_ref, db_ref, ub_ref)):
            ref[...] = vec_ref[n]
        member = lax.axis_index("mp")
        half = lax.rem(member, 2)
        steps = table_ref.shape[0]
        at = lax.broadcasted_iota(jnp.int32, (16, steps), 1)
        table = jnp.zeros(table_ref.shape, F32)
        picks, parts = [], [[], [], []]
        for n in range(GROUP):
            for side in range(2):
                picks.append((ts_ref[n, 16 * side : 16 * side + 16, 0:1] == at).astype(F32))
                value = jnp.where(half == side, u_ref[0, n], u_ref[1, n])
                parts[0].append(value)
        pick = jnp.concatenate(picks, axis=0).astype(BF16)
        rest = jnp.concatenate(parts[0], axis=0)
        for _ in range(3):
            low = rest.astype(BF16)
            table = table + mm_tn(pick, low)
            rest = rest - low.astype(F32)
        table_ref[...] = table


def whole(shape):
    zeros = (0,) * len(shape)
    return pl.BlockSpec(shape, lambda i, meta: zeros, pipeline_mode=pl.Buffered(1))


def held(shape):
    zeros = (0,) * len(shape)
    return pl.BlockSpec(shape, lambda i, meta: zeros)


LIMIT = 62 * 1024 * 1024


def attn_fwd(meta, hidden, emb, gain, shift, wqkv, wo, ob):
    count, width = hidden.shape[0] // 2, hidden.shape[1]
    steps = count // TILE
    heads = width // HD
    tok = pl.BlockSpec((TILE, width), lambda i, meta: (i, 0))
    return pl.pallas_call(
        attn_fwd_kernel,
        name="attn_fwd",
        grid_spec=pltpu.PrefetchScalarGridSpec(
            num_scalar_prefetch=1,
            grid=(steps,),
            in_specs=[
                pl.BlockSpec((TILE, width), lambda i, meta: (meta[0] * steps + i, 0)),
                whole(emb.shape), whole((1, width)), whole((1, width)),
                whole(wqkv.shape), whole(wo.shape), whole((1, width)),
            ],
            out_specs=[
                pl.BlockSpec((3, TILE, width), lambda i, meta: (0, i, 0)),
                pl.BlockSpec((heads, TILE // WIN, WIN, WIN), lambda i, meta: (0, i, 0, 0)),
                tok,
                tok,
            ],
            scratch_shapes=[pltpu.VMEM((WIN, WIN), F32), pltpu.VMEM((TILE, width), BF16)],
        ),
        out_shape=[
            jax.ShapeDtypeStruct((3, count, width), BF16),
            jax.ShapeDtypeStruct((heads, count // WIN, WIN, WIN), BF16),
            jax.ShapeDtypeStruct((count, width), BF16),
            jax.ShapeDtypeStruct((count, width), F32),
        ],
        compiler_params=pltpu.CompilerParams(vmem_limit_bytes=LIMIT),
        cost_estimate=pl.CostEstimate(flops=12_000_000_000, bytes_accessed=30_000_000, transcendentals=5_000_000),
    )(meta, hidden, emb, gain, shift, wqkv, wo, ob)


def half_map(steps):
    return lambda i: (lax.rem(lax.axis_index("mp"), 2) * steps + i, 0)


def fixed(shape):
    zeros = (0,) * len(shape)
    return pl.BlockSpec(shape, lambda i: zeros, pipeline_mode=pl.Buffered(1))


def mlp(mid, gy, wu, bu, wd, gain, shift, db):
    count, width = mid.shape
    steps = count // TILE
    ff = wu.shape[2]
    tok = pl.BlockSpec((TILE, width), lambda i: (i, 0))
    dma = pltpu.SemaphoreType.DMA
    return pl.pallas_call(
        mlp_kernel,
        name="mlp_both",
        grid=(steps,),
        in_specs=[
            tok,
            pl.BlockSpec((TILE, width), half_map(steps)),
            fixed(wu.shape), fixed(bu.shape), fixed(wd.shape),
            fixed((1, width)), fixed((1, width)), fixed((1, width)),
        ],
        out_specs=[
            pl.BlockSpec(memory_space=pl.ANY), tok, fixed((2, width, 2 * ff)),
            fixed((8, width)), fixed((2, 8, ff)),
        ],
        scratch_shapes=[
            pltpu.VMEM((2, width, ff), F32), pltpu.VMEM((2, width, ff), F32),
            pltpu.VMEM((TILE, width), BF16), pltpu.VMEM((width, TILE), BF16),
            pltpu.VMEM((width, TILE), BF16),
            pltpu.VMEM((TILE, width), F32), pltpu.VMEM((TILE, width), F32),
            pltpu.VMEM((2, TILE, width), BF16), dma((steps,)), dma((steps,)), dma((steps,)),
        ],
        out_shape=[
            jax.ShapeDtypeStruct((2 * count, width), BF16),
            jax.ShapeDtypeStruct((count, width), F32),
            jax.ShapeDtypeStruct((2, width, 2 * ff), BF16),
            jax.ShapeDtypeStruct((8, width), F32),
            jax.ShapeDtypeStruct((2, 8, ff), F32),
        ],
        compiler_params=pltpu.CompilerParams(
            collective_id=2, has_side_effects=True, vmem_limit_bytes=LIMIT
        ),
        cost_estimate=pl.CostEstimate(flops=36_000_000_000, bytes_accessed=30_000_000, transcendentals=5_000_000),
    )(mid, gy, wu, bu, wd, gain, shift, db)


def attn_bwd(hidden, emb, gain, shift, wqkv, wo, qkv, probs, ctx, gmid, gwm, vecm, gbu, out):
    count, width = gmid.shape
    steps = count // TILE
    heads = width // HD
    share = width // GROUP
    wide = gwm.shape[2]
    units = emb.shape[0]
    piece = width // 4
    tok = pl.BlockSpec((TILE, width), lambda i: (i, 0))
    anywhere = pl.BlockSpec(memory_space=pl.ANY)
    dma = pltpu.SemaphoreType.DMA
    return pl.pallas_call(
        attn_bwd_kernel,
        name="attn_bwd",
        grid=(steps,),
        in_specs=[
            pl.BlockSpec((TILE, width), half_map(steps)),
            fixed(emb.shape), fixed((1, width)), fixed((1, width)),
            fixed(wqkv.shape), fixed(wo.shape),
            pl.BlockSpec((3, TILE, width), lambda i: (0, i, 0)),
            pl.BlockSpec((heads, TILE // WIN, WIN, WIN), lambda i: (0, i, 0, 0)),
            tok, tok, anywhere, fixed(vecm.shape), fixed(gbu.shape), anywhere,
        ],
        out_specs=[
            anywhere, anywhere, fixed((share, wide)), fixed((share, width)),
            fixed((8, width)), fixed((2, GROUP, units, piece)),
        ],
        scratch_shapes=[
            pltpu.VMEM((4, width, width // 2), F32),
            pltpu.VMEM((3, TILE, width), BF16), pltpu.VMEM((TILE, width), BF16),
            pltpu.VMEM((width, TILE), BF16), pltpu.VMEM((width, TILE), BF16),
            pltpu.VMEM((8, width), F32), pltpu.VMEM((units, width), F32),
            pltpu.VMEM((2, TILE, width), BF16),
            pltpu.VMEM((4, 2, share, wide), BF16), pltpu.VMEM((4, 2, share, wide), BF16),
            pltpu.VMEM((4, 2, share, wide), BF16), pltpu.VMEM((3, 2, share, wide), BF16),
            pltpu.VMEM((share, wide), BF16), pltpu.VMEM((share, wide), BF16),
            pltpu.VMEM((2, width, width), BF16), pltpu.VMEM((4, 2, share, width), BF16),
            pltpu.VMEM((4, 2, share, width), BF16), pltpu.VMEM((3, 2, share, width), BF16),
            pltpu.VMEM((share, width), BF16), pltpu.VMEM((share, width), BF16),
            pltpu.VMEM((units + 16, width // 2), F32), pltpu.VMEM((GROUP, units + 16, width // 2), F32),
            pltpu.VMEM((16, width // 2), F32), pltpu.VMEM((4, 16, width // 2), F32),
            pltpu.VMEM((GROUP, units, piece), F32), pltpu.VMEM((GROUP, units, piece), F32),
            dma((4,)), dma(()), dma(()), dma((steps,)), dma((steps,)), dma((steps,)),
            dma((2, 4)), dma((2, 4)), dma((2, 3)), dma((2, 3)), dma((2,)), dma((2,)),
            dma((GROUP - 1,)), dma((GROUP - 1,)), dma((3,)), dma((3,)), dma(()), dma(()),
        ],
        out_shape=[
            jax.ShapeDtypeStruct((2 * count, width), BF16),
            jax.ShapeDtypeStruct((2 * count, width), BF16),
            jax.ShapeDtypeStruct((share, wide), F32),
            jax.ShapeDtypeStruct((share, width), F32),
            jax.ShapeDtypeStruct((8, width), F32),
            jax.ShapeDtypeStruct((2, GROUP, units, piece), F32),
        ],
        input_output_aliases={13: 0},
        compiler_params=pltpu.CompilerParams(
            collective_id=3, has_side_effects=True, vmem_limit_bytes=LIMIT
        ),
        cost_estimate=pl.CostEstimate(flops=20_000_000_000, bytes_accessed=40_000_000, transcendentals=0),
    )(hidden, emb, gain, shift, wqkv, wo, qkv, probs, ctx, gmid, gwm, vecm, gbu, out)


def finish(out, gh, gm, ga, vec, u, ts, steps):
    count, width = out.shape
    share = gm.shape[0]
    ff = gm.shape[1] // 2
    piece = width // 4
    tok = pl.BlockSpec((2 * TILE, width), lambda i: (i, 0))
    line = jax.ShapeDtypeStruct((width,), F32)
    shapes = [
        jax.ShapeDtypeStruct((steps, piece), F32), line, line,
        jax.ShapeDtypeStruct((3, share, piece), F32), jax.ShapeDtypeStruct((piece, share), F32),
        line, line, line,
        jax.ShapeDtypeStruct((share, ff), F32), line, jax.ShapeDtypeStruct((ff, share), F32), line,
    ]
    return pl.pallas_call(
        finish_kernel,
        name="finish",
        grid=(count // (2 * TILE),),
        in_specs=[tok, tok] + [fixed(x.shape) for x in (gm, ga, vec, u, ts)],
        out_specs=[tok, tok] + [fixed(x.shape) for x in shapes],
        out_shape=[jax.ShapeDtypeStruct(out.shape, BF16), jax.ShapeDtypeStruct(gh.shape, BF16)] + shapes,
        compiler_params=pltpu.CompilerParams(vmem_limit_bytes=LIMIT),
        cost_estimate=pl.CostEstimate(flops=1_000_000, bytes_accessed=20_000_000, transcendentals=0),
    )(out, gh, gm, ga, vec, u, ts)


ARRAYS = 4


def gather_kernel(
    wqkv, wo, wu, wd, bu, ts, wqkv_f, wo_f, wu_f, wd_f, bu_f, ts_f,
    hold_qkv, hold_wo, hold_wu, hold_wd, hold_bu, hold_ts,
    loc_sem, z_send, z_recv, b_send, b_recv, n_send, n_recv, t_send, t_recv,
):
    place = lax.axis_index("dp")
    member = lax.axis_index("mp")
    base = place - lax.rem(place, 8)
    spot = place - base
    bit0 = lax.rem(spot, 2)
    bit1 = lax.rem(spot // 2, 2)
    bit2 = spot // 4

    def flip(where, bit, size):
        return where + size - 2 * size * bit

    near = {
        "core": {"dp": flip(place, bit0, 1), "mp": member},
        "x": {"dp": flip(place, bit1, 2), "mp": member},
        "y": {"dp": flip(place, bit2, 4), "mp": member},
    }
    mine = spot
    from_x = flip(spot, bit1, 2)
    from_y = flip(spot, bit2, 4)
    from_d = flip(from_x, bit2, 4)

    def peer(turn):
        return {"dp": place, "mp": lax.rem(member + turn, 4)}

    others = [{"dp": base + lax.rem(spot + turn, 8), "mp": member} for turn in range(1, 8)]
    greet([peer(1), peer(2), peer(3)] + others)

    rows_a = wo.shape[0]
    step_a = rows_a // 8
    step_m = wu.shape[1 - 1] // 8

    def full_at(array, shard, piece):
        if array == 0:
            return wqkv_f.at[:, pl.ds(shard * rows_a + piece * step_a, step_a), :]
        if array == 1:
            return wo_f.at[pl.ds(shard * rows_a + piece * step_a, step_a), :]
        full = wu_f if array == 2 else wd_f
        return full.at[shard, pl.ds(piece * step_m, step_m), :]

    def own_at(array, piece):
        if array == 0:
            return wqkv.at[:, pl.ds(piece * step_a, step_a), :]
        if array == 1:
            return wo.at[pl.ds(piece * step_a, step_a), :]
        return (wu if array == 2 else wd).at[pl.ds(piece * step_m, step_m), :]

    sends = []
    z_recvs, n_recvs = {}, {}
    for array in range(ARRAYS):
        for turn in (2, 1, 3):
            copy = pltpu.make_async_remote_copy(
                src_ref=own_at(array, spot),
                dst_ref=full_at(array, member, spot),
                send_sem=z_send.at[array, turn - 1],
                recv_sem=z_recv.at[array, turn - 1],
                device_id=peer(turn),
                device_id_type=pl.DeviceIdType.MESH,
            )
            copy.start()
            sends.append(copy)
            z_recvs[array, turn] = copy
        if array == 0:
            for turn in (1, 2, 3):
                copy = pltpu.make_async_remote_copy(
                    src_ref=bu, dst_ref=bu_f.at[member],
                    send_sem=b_send.at[turn - 1], recv_sem=b_recv.at[turn - 1],
                    device_id=peer(turn), device_id_type=pl.DeviceIdType.MESH,
                )
                copy.start()
                sends.append(copy)
                n_recvs["bias", turn] = copy
            for n in range(7):
                copy = pltpu.make_async_remote_copy(
                    src_ref=ts, dst_ref=ts_f.at[spot],
                    send_sem=t_send.at[n], recv_sem=t_recv.at[n],
                    device_id=others[n], device_id_type=pl.DeviceIdType.MESH,
                )
                copy.start()
                sends.append(copy)
                n_recvs["step", n] = copy

    own_full = (
        (wqkv, hold_qkv, wqkv_f.at[:, pl.ds(member * rows_a, rows_a), :]),
        (wo, hold_wo, wo_f.at[pl.ds(member * rows_a, rows_a), :]),
        (wu, hold_wu, wu_f.at[member]),
        (wd, hold_wd, wd_f.at[member]),
        (bu, hold_bu, bu_f.at[member]),
        (ts, hold_ts, ts_f.at[spot]),
    )
    into = [pltpu.make_async_copy(src, hold, loc_sem.at[n]) for n, (src, hold, _) in enumerate(own_full)]
    for copy in into:
        copy.start()
    outof = []
    for n, (_, hold, dst) in enumerate(own_full):
        into[n].wait()
        copy = pltpu.make_async_copy(hold, dst, loc_sem.at[6 + n])
        copy.start()
        outof.append(copy)

    def push(array, turn, kind, piece, target):
        shard = lax.rem(member + 4 - turn, 4)
        copy = pltpu.make_async_remote_copy(
            src_ref=full_at(array, shard, piece),
            dst_ref=full_at(array, shard, piece),
            send_sem=n_send.at[array, turn - 1, kind],
            recv_sem=n_recv.at[array, turn - 1, kind],
            device_id=near[target],
            device_id_type=pl.DeviceIdType.MESH,
        )
        copy.start()
        sends.append(copy)
        n_recvs[array, turn, kind] = copy

    order = (1, 3, 2)

    def stage_z(array):
        for turn in order:
            z_recvs[array, turn].wait_recv()
            push(array, turn, 0, mine, "x")
            push(array, turn, 1, mine, "y")
            push(array, turn, 3, mine, "core")

    def stage_near(array):
        for turn in order:
            n_recvs[array, turn, 0].wait_recv()
            if (array + turn) % 2 == 0:
                push(array, turn, 2, from_x, "y")
            push(array, turn, 4, from_x, "core")
            n_recvs[array, turn, 1].wait_recv()
            if (array + turn) % 2 == 1:
                push(array, turn, 2, from_y, "x")
            push(array, turn, 5, from_y, "core")

    def stage_far(array):
        for turn in order:
            n_recvs[array, turn, 2].wait_recv()
            push(array, turn, 6, from_d, "core")

    for step in range(ARRAYS + 2):
        if step < ARRAYS:
            stage_z(step)
        if 0 <= step - 1 < ARRAYS:
            stage_near(step - 1)
        if 0 <= step - 2 < ARRAYS:
            stage_far(step - 2)
    for array in range(ARRAYS):
        for turn in order:
            for kind in range(3, 7):
                n_recvs[array, turn, kind].wait_recv()
    for turn in (1, 2, 3):
        n_recvs["bias", turn].wait_recv()
    for n in range(7):
        n_recvs["step", n].wait_recv()
    for copy in sends:
        copy.wait_send()
    for copy in outof:
        copy.wait()


def gather_weights(wqkv, wo, wu, wd, bu, ts):
    anywhere = pl.BlockSpec(memory_space=pl.ANY)
    rows, width = wo.shape
    ff = wu.shape[1]
    return pl.pallas_call(
        gather_kernel,
        name="gather_weights",
        in_specs=[anywhere] * 6,
        out_specs=[anywhere] * 6,
        out_shape=[
            jax.ShapeDtypeStruct((3, 4 * rows, width), BF16),
            jax.ShapeDtypeStruct((4 * rows, width), BF16),
            jax.ShapeDtypeStruct((4, width, ff), BF16),
            jax.ShapeDtypeStruct((4, ff, width), BF16),
            jax.ShapeDtypeStruct((4,) + bu.shape, F32),
            jax.ShapeDtypeStruct((GROUP,) + ts.shape, jnp.int32),
        ],
        scratch_shapes=[
            pltpu.VMEM(wqkv.shape, BF16), pltpu.VMEM(wo.shape, BF16),
            pltpu.VMEM(wu.shape, BF16), pltpu.VMEM(wd.shape, BF16), pltpu.VMEM(bu.shape, F32),
            pltpu.VMEM(ts.shape, jnp.int32),
            pltpu.SemaphoreType.DMA((12,)),
            pltpu.SemaphoreType.DMA((ARRAYS, 3)), pltpu.SemaphoreType.DMA((ARRAYS, 3)),
            pltpu.SemaphoreType.DMA((3,)), pltpu.SemaphoreType.DMA((3,)),
            pltpu.SemaphoreType.DMA((ARRAYS, 3, 7)), pltpu.SemaphoreType.DMA((ARRAYS, 3, 7)),
            pltpu.SemaphoreType.DMA((7,)), pltpu.SemaphoreType.DMA((7,)),
        ],
        compiler_params=pltpu.CompilerParams(
            collective_id=1, has_side_effects=True, vmem_limit_bytes=LIMIT
        ),
    )(wqkv, wo, wu, wd, bu, ts)


def local(
    hidden, timesteps, cotangent, time_table, first_gain, first_shift, qkv_weight, out_weight,
    out_bias, second_gain, second_shift, up_weight, up_bias, down_weight, down_bias,
):
    count, width = hidden.shape
    steps = time_table.shape[0]
    local_ff = up_weight.shape[1]
    member = lax.axis_index("mp")
    half = lax.rem(member, 2)
    meta = jnp.stack([half, member // 2]).astype(jnp.int32)
    units = count // LEN_A
    unit = jnp.arange(units, dtype=jnp.int32)
    within = unit % 8
    row_of = unit // 8 * 6 + jnp.where(within < 4, within, 4 + (within - 4) // 2)
    unit_step = jnp.pad(
        jnp.take(timesteps, row_of).reshape(2, units // 2), ((0, 0), (0, 16 - units // 2)), constant_values=-1
    )
    emb = jnp.take(time_table, jnp.maximum(unit_step[half], 0), axis=0).astype(F32)
    stamps = jnp.broadcast_to(unit_step.reshape(32, 1), (32, 128))

    def row(v):
        return v.reshape(1, -1)

    wqkv_f, wo_f, wu_f, wd_f, bu_f, ts_f = gather_weights(
        jnp.swapaxes(qkv_weight, 1, 2),
        out_weight,
        up_weight,
        down_weight,
        jnp.broadcast_to(row(up_bias), (8, local_ff)),
        stamps,
    )
    qkv, probs, ctx, mid = attn_fwd(
        meta, hidden, emb, row(first_gain), row(first_shift), wqkv_f, wo_f, row(out_bias)
    )
    output, gmid, gw_mlp, vec_mlp, gbu = mlp(
        mid, cotangent, wu_f, bu_f, wd_f, row(second_gain), row(second_shift), row(down_bias)
    )
    output, grad_hidden, g_mlp, g_attn, vecs, sums = attn_bwd(
        hidden, emb, row(first_gain), row(first_shift), wqkv_f, wo_f, qkv, probs, ctx, gmid,
        gw_mlp, vec_mlp, gbu, output,
    )
    outs = list(finish(output, grad_hidden, g_mlp, g_attn, vecs, sums, ts_f, steps))
    groups = lax.axis_size("dp") // GROUP
    if groups > 1:
        spots = [[g * GROUP + n for n in range(GROUP)] for g in range(groups)]
        split = {5: 1, 6: 1, 10: 0, 12: 1}
        for n in range(2, len(outs)):
            value = outs[n] * (1.0 / GROUP)
            if n in split:
                value = lax.all_gather(value, "dp", axis_index_groups=spots, axis=split[n], tiled=True)
                outs[n] = lax.psum_scatter(value, "dp", scatter_dimension=split[n], tiled=True)
            else:
                outs[n] = lax.psum(value, "dp")
    return tuple(outs)


def solution(mesh):
    return jax.shard_map(
        local,
        mesh=mesh,
        in_specs=(
            P("dp", None), P("dp"), P("dp", None), P(), P(), P(), P(None, None, "mp"),
            P("mp", None), P(), P(), P(), P(None, "mp"), P("mp"), P("mp", None), P(),
        ),
        out_specs=(
            P("dp", None), P("dp", None), P(None, "mp"), P(), P(), P(None, "dp", "mp"),
            P("mp", "dp"), P(), P(), P(), P("dp", "mp"), P("mp"), P("mp", "dp"), P(),
        ),
        check_vma=False,
    )
```

```python
from functools import partial

import jax
import jax.numpy as jnp
from jax import lax
from jax.experimental import pallas as pl
from jax.experimental.pallas import tpu as pltpu
from jax.sharding import PartitionSpec as P

F32 = jnp.float32
BF16 = jnp.bfloat16
HD = 64
LEN_A = 128
LEN_B = 256
BLOCK = 512
WIN = 256
TILE = 512
GROUP = 8
EPS = 1e-05
GELU_C = 0.7978845608028654
GELU_A = 0.044715


def mm(a, b):
    return lax.dot_general(a, b, (((1,), (0,)), ((), ())), preferred_element_type=F32)


def mm_nt(a, b):
    return lax.dot_general(a, b, (((1,), (1,)), ((), ())), preferred_element_type=F32)


def mm_tn(a, b):
    return lax.dot_general(a, b, (((0,), (0,)), ((), ())), preferred_element_type=F32)


def norm_stats(rows):
    centre = jnp.mean(rows, axis=-1, keepdims=True)
    offset = rows - centre
    spread = jnp.mean(offset * offset, axis=-1, keepdims=True)
    inv = lax.rsqrt(spread + EPS)
    return offset * inv, inv


def norm_back(grad, gain, hat, inv):
    dhat = grad * gain
    first = jnp.mean(dhat, axis=-1, keepdims=True)
    second = jnp.mean(dhat * hat, axis=-1, keepdims=True)
    return inv * (dhat - first - hat * second)


def stream_tile(hidden_ref, emb_ref, tile):
    parts = []
    for unit in range(TILE // LEN_A):
        row = emb_ref[pl.ds(tile * (TILE // LEN_A) + unit, 1), :]
        parts.append(hidden_ref[unit * LEN_A : (unit + 1) * LEN_A, :].astype(F32) + row)
    return jnp.concatenate(parts, axis=0)


def line_up():
    place = lax.axis_index("dp")
    spot = lax.rem(place, GROUP)
    return place - spot, spot


def ahead(ref, rows, dst, send, recv, target):
    return pltpu.make_async_remote_copy(
        src_ref=ref.at[rows] if rows is not None else ref,
        dst_ref=dst.at[rows] if rows is not None else dst,
        send_sem=send, recv_sem=recv, device_id=target, device_id_type=pl.DeviceIdType.MESH,
    )


def mate_of(member):
    return {"dp": lax.axis_index("dp"), "mp": member + 1 - 2 * lax.rem(member, 2)}


def greet(targets):
    barrier = pltpu.get_barrier_semaphore()
    for target in targets:
        pl.semaphore_signal(barrier, inc=1, device_id=target, device_id_type=pl.DeviceIdType.MESH)
    pl.semaphore_wait(barrier, len(targets))


def attn_fwd_kernel(
    hidden_ref, emb_ref, gain_ref, shift_ref, ob_ref, bias_ref, ts_ref, wqkv, wo, wu, wd,
    wqkv_f, wo_f, wu_f, wd_f, bu_f, ts_f, qkv_ref, probs_ref, ctx_ref, mid_ref,
    same_ref, ctx_acc, wqkv_v, wo_v, norm_v, hold_wu, hold_wd, hold_bu, hold_ts,
    loc_sem, load_sem, z_send, z_recv, b_send, b_recv, n_send, n_recv, t_send, t_recv,
):
    tile = pl.program_id(0)
    steps = pl.num_programs(0)
    last = steps - 1
    member = lax.axis_index("mp")
    half = lax.rem(member, 2)
    place = lax.axis_index("dp")
    base, spot = line_up()
    bit0 = lax.rem(spot, 2)
    bit1 = lax.rem(spot // 2, 2)
    bit2 = spot // 4

    def flip(where, bit, size):
        return where + size - 2 * size * bit

    near = {
        "core": {"dp": flip(place, bit0, 1), "mp": member},
        "x": {"dp": flip(place, bit1, 2), "mp": member},
        "y": {"dp": flip(place, bit2, 4), "mp": member},
    }
    from_x = flip(spot, bit1, 2)
    from_y = flip(spot, bit2, 4)
    from_d = flip(from_x, bit2, 4)
    others = [{"dp": base + lax.rem(spot + turn, GROUP), "mp": member} for turn in range(1, GROUP)]

    def peer(turn):
        return {"dp": place, "mp": lax.rem(member + turn, 4)}

    rows_a = wo.shape[0]
    step_a = rows_a // GROUP
    step_m = wu.shape[0] // GROUP

    def full_at(array, shard, piece):
        if array == 0:
            return wqkv_f.at[:, pl.ds(shard * rows_a + piece * step_a, step_a), :]
        if array == 1:
            return wo_f.at[pl.ds(shard * rows_a + piece * step_a, step_a), :]
        full = wu_f if array == 2 else wd_f
        return full.at[shard, pl.ds(piece * step_m, step_m), :]

    def own_at(array, piece):
        if array == 0:
            return wqkv.at[:, pl.ds(piece * step_a, step_a), :]
        if array == 1:
            return wo.at[pl.ds(piece * step_a, step_a), :]
        return (wu if array == 2 else wd).at[pl.ds(piece * step_m, step_m), :]

    def remote(src, dst, send, recv, target):
        return pltpu.make_async_remote_copy(
            src_ref=src, dst_ref=dst, send_sem=send, recv_sem=recv,
            device_id=target, device_id_type=pl.DeviceIdType.MESH,
        )

    def z_copy(array, turn):
        return remote(
            own_at(array, spot), full_at(array, member, spot),
            z_send.at[array, turn - 1], z_recv.at[array, turn - 1], peer(turn),
        )

    def bias_copy(turn):
        return remote(hold_bu, bu_f.at[member], b_send.at[turn - 1], b_recv.at[turn - 1], peer(turn))

    def stamp_copy(n):
        return remote(ts_ref, ts_f.at[spot], t_send.at[n], t_recv.at[n], others[n])

    def push(array, turn, kind):
        shard = lax.rem(member + 4 - turn, 4)
        by_x = (array + turn) % 2 == 0
        piece = (spot, spot, from_x if by_x else from_y, spot, from_x, from_y, from_d)[kind]
        target = ("x", "y", "y" if by_x else "x", "core", "core", "core", "core")[kind]
        return remote(
            full_at(array, shard, piece), full_at(array, shard, piece),
            n_send.at[array, turn - 1, kind], n_recv.at[array, turn - 1, kind], near[target],
        )

    order = (1, 3, 2)

    def stage_z(array):
        for turn in order:
            z_copy(array, turn).wait_recv()
            for kind in (0, 1, 3):
                push(array, turn, kind).start()

    def stage_near(array):
        for turn in order:
            push(array, turn, 0).wait_recv()
            if (array + turn) % 2 == 0:
                push(array, turn, 2).start()
            push(array, turn, 4).start()
            push(array, turn, 1).wait_recv()
            if (array + turn) % 2 == 1:
                push(array, turn, 2).start()
            push(array, turn, 5).start()

    def stage_far(array):
        for turn in order:
            push(array, turn, 2).wait_recv()
            push(array, turn, 6).start()

    def settle(array):
        for turn in order:
            for kind in range(3, 7):
                push(array, turn, kind).wait_recv()

    own_rows = pl.ds(pl.multiple_of(member * rows_a, 64), rows_a)
    own_parts = (
        (wqkv, wqkv_v.at[:, own_rows, :], wqkv_f.at[:, own_rows, :]),
        (wo, wo_v.at[own_rows, :], wo_f.at[own_rows, :]),
        (wu, hold_wu, wu_f.at[member]),
        (wd, hold_wd, wd_f.at[member]),
        (ts_ref, hold_ts, ts_f.at[spot]),
    )

    def into(n):
        return pltpu.make_async_copy(own_parts[n][0], own_parts[n][1], loc_sem.at[n])

    def outof(n):
        return pltpu.make_async_copy(own_parts[n][1], own_parts[n][2], loc_sem.at[8 + n])

    def bias_out():
        return pltpu.make_async_copy(hold_bu, bu_f.at[member], loc_sem.at[15])

    def load(array):
        src, dst = ((wqkv_f, wqkv_v), (wo_f, wo_v))[array]
        return pltpu.make_async_copy(src, dst, load_sem.at[array])

    @pl.when(tile == 0)
    def _():
        hold_bu[...] = jnp.broadcast_to(bias_ref[...], hold_bu.shape)
        greet([peer(1), peer(2), peer(3)] + others)
        for array in range(4):
            for turn in (2, 1, 3):
                z_copy(array, turn).start()
        for n in range(5):
            into(n).start()
        for n in range(GROUP - 1):
            stamp_copy(n).start()
        for n in range(5):
            into(n).wait()
            outof(n).start()

    stream = stream_tile(hidden_ref, emb_ref, tile)
    hat, _ = norm_stats(stream)
    norm_v[...] = (hat * gain_ref[...] + shift_ref[...]).astype(BF16)
    mid_ref[...] = stream + ob_ref[...]

    @pl.when(tile == 0)
    def _():
        bias_out().start()
        for turn in (1, 2, 3):
            bias_copy(turn).start()
        stage_z(0)
        stage_z(1)
        stage_near(0)
        stage_far(0)
        settle(0)
        outof(0).wait()
        load(0).start()
        load(0).wait()

    @pl.when(tile == 1)
    def _():
        stage_z(3)

    for part in range(3):
        qkv_ref[part] = mm_nt(norm_v[...], wqkv_v[part]).astype(BF16)

    @pl.when(tile == 0)
    def _():
        stage_near(1)
        stage_z(2)
        stage_far(1)
        settle(1)
        outof(1).wait()
        load(1).start()

    lane = lax.broadcasted_iota(jnp.int32, (WIN, 2 * HD), 1)
    low = lane < HD
    row_i = lax.broadcasted_iota(jnp.int32, (WIN, WIN), 0)
    col_i = lax.broadcasted_iota(jnp.int32, (WIN, WIN), 1)
    same_half = (row_i < LEN_A) == (col_i < LEN_A)
    scale = HD ** (-0.5)
    pairs = qkv_ref.shape[2] // (2 * HD)
    for win in range(TILE // WIN):
        at = ((half * steps + tile) * (TILE // WIN) + win) % 4
        same_ref[...] = jnp.where(same_half, 0.0, jnp.where(at < 2, -1e9, 0.0))
        rows = slice(win * WIN, (win + 1) * WIN)
        for pair in range(pairs):
            cols = slice(pair * 2 * HD, (pair + 1) * 2 * HD)
            q2 = qkv_ref[0, rows, cols] * jnp.asarray(scale, BF16)
            k2 = qkv_ref[1, rows, cols]
            v2 = qkv_ref[2, rows, cols]
            outs = []
            for j in range(2):
                q1 = jnp.where(low == (j == 0), q2, jnp.zeros_like(q2))
                scores = mm_nt(q1, k2) + same_ref[...]
                top = jnp.max(scores, axis=-1, keepdims=True)
                expo = jnp.exp(scores - top)
                total = jnp.sum(expo, axis=-1, keepdims=True)
                probs = (expo * (1.0 / total)).astype(BF16)
                probs_ref[2 * pair + j, win] = probs
                outs.append(mm(probs, v2))
            ctx_acc[rows, cols] = jnp.where(low, outs[0], outs[1]).astype(BF16)
        if win == 0:

            @pl.when(tile == last)
            def _():
                stage_near(3)

    @pl.when(tile == 0)
    def _():
        load(1).wait()

    @pl.when(tile == 1)
    def _():
        stage_near(2)

    @pl.when(tile == last)
    def _():
        stage_far(2)

    ctx_ref[...] = ctx_acc[...]
    mid_ref[...] += mm(ctx_acc[...], wo_v[...])

    @pl.when(tile == last)
    def _():
        stage_far(3)
        settle(2)
        settle(3)
        for n in range(GROUP - 1):
            stamp_copy(n).wait_recv()
            stamp_copy(n).wait_send()
        for turn in (1, 2, 3):
            bias_copy(turn).wait_recv()
            bias_copy(turn).wait_send()
        for array in range(4):
            for turn in (1, 2, 3):
                z_copy(array, turn).wait_send()
                for kind in range(7):
                    push(array, turn, kind).wait_send()
        for n in range(2, 5):
            outof(n).wait()
        bias_out().wait()


def mlp_kernel(
    mid_ref, gy_ref, wu_ref, bu_ref, wd_ref, gain_ref, shift_ref, db_ref,
    out_ref, gmid_ref, gw_ref, vec_ref, gbu_ref,
    acc_u, acc_d, n2_ref, n2t_ref, gyt_ref, mlp_ref, dn_ref, stage, loc_sem, send_sem, recv_sem,
):
    tile = pl.program_id(0)
    steps = pl.num_programs(0)
    last = steps - 1
    member = lax.axis_index("mp")
    half = lax.rem(member, 2)
    pair = member // 2
    mate = mate_of(member)
    ff = wu_ref.shape[2]
    total = out_ref.shape[0] // (2 * TILE)

    def rows_of(t):
        return pl.ds(pl.multiple_of((half * total + t) * TILE, TILE), TILE)

    def local_copy(t):
        return pltpu.make_async_copy(stage.at[lax.rem(t, 2)], out_ref.at[rows_of(t)], loc_sem.at[t])

    def remote_copy(t):
        return ahead(out_ref, rows_of(t), out_ref, send_sem.at[t], recv_sem.at[t], mate)

    @pl.when(tile == 0)
    def _():
        acc_u[...] = jnp.zeros_like(acc_u)
        acc_d[...] = jnp.zeros_like(acc_d)
        vec_ref[...] = jnp.zeros_like(vec_ref)
        gbu_ref[...] = jnp.zeros_like(gbu_ref)
        greet([mate])

    @pl.when(tile > 0)
    def _():
        local_copy(tile - 1).wait()
        remote_copy(tile - 1).start()

    hat, inv = norm_stats(mid_ref[...])
    normed = (hat * gain_ref[...] + shift_ref[...]).astype(BF16)
    n2_ref[...] = normed
    n2t_ref[...] = normed.T
    gyt_ref[...] = gy_ref[...].T
    mlp_ref[...] = mid_ref[...] + db_ref[...]
    dn_ref[...] = jnp.zeros_like(dn_ref)

    def step(turn, own):
        group = lax.rem(2 * pair + turn, 4)
        pre = mm(n2_ref[...], wu_ref[group]) + bu_ref[group, 0:1]
        grad_act = mm_nt(gy_ref[...], wd_ref[group])
        square = pre * pre
        bend = jnp.tanh(pre * (GELU_C + (GELU_C * GELU_A) * square))
        half_in = 0.5 * pre
        up = 1.0 + bend
        act = (half_in * up).astype(BF16)
        slope = 0.5 * up + half_in * (1.0 - bend * bend) * (GELU_C + (3.0 * GELU_C * GELU_A) * square)
        grad_f = grad_act * slope
        grad_pre = grad_f.astype(BF16)
        mlp_ref[...] += mm(act, wd_ref[group])
        dn_ref[...] += mm_nt(grad_pre, wu_ref[group])
        if own:
            acc_u[turn] += mm(n2t_ref[...], grad_pre)
            acc_d[turn] += mm(gyt_ref[...], act)
            gbu_ref[turn, 0:1] += jnp.sum(grad_pre.astype(F32), axis=0, keepdims=True)

    lax.fori_loop(0, 2, lambda turn, c: (step(turn, True), c)[1], 0)
    lax.fori_loop(2, 4, lambda turn, c: (step(turn, False), c)[1], 0)

    stage[lax.rem(tile, 2)] = mlp_ref[...].astype(BF16)
    hat, inv = norm_stats(mid_ref[...])
    top = gy_ref[...].astype(F32)
    dn = dn_ref[...]
    vec_ref[0:1] += jnp.sum(dn * hat, axis=0, keepdims=True)
    vec_ref[1:2] += jnp.sum(dn, axis=0, keepdims=True)
    gmid = top + norm_back(dn, gain_ref[...], hat, inv)
    vec_ref[2:3] += jnp.sum(gmid, axis=0, keepdims=True)
    vec_ref[3:4] += jnp.sum(top, axis=0, keepdims=True)
    gmid_ref[...] = gmid
    local_copy(tile).start()

    @pl.when(tile == last)
    def _():
        gw_ref[:, :, 0:ff] = acc_u[...].astype(BF16)
        gw_ref[:, :, ff : 2 * ff] = acc_d[...].astype(BF16)
        local_copy(tile).wait()
        for t in range(total - 1):
            remote_copy(t).wait_send()
            remote_copy(t).wait_recv()


def attn_bwd_kernel(
    hidden_ref, emb_ref, gain_ref, shift_ref, wqkv_ref, wo_ref,
    qkv_ref, probs_ref, ctx_ref, gmid_ref, gwm_ref, vecm_ref, gbu_ref, ts_ref, out_in,
    out_ref, gh_ref, gm_ref, ga_ref, vec_out, table_ref,
    acc, gp_ref, gc_ref, n1t_ref, gmt_ref, vec_ref, usum_ref, stage,
    m_own, m_core, m_sum, m_chip, m_give, m_got,
    a_src, a_core, a_sum, a_chip, a_give, a_got,
    s_src, s_rcv, v_src, v_rcv, u_give, u_got, u_mine,
    own_sem, out_send, out_recv, loc_sem, gh_send, gh_recv,
    core_send, core_recv, chip_send, chip_recv, give_send, give_recv,
    s_send, s_recv, v_send, v_recv, u_send, u_recv,
):
    tile = pl.program_id(0)
    last = pl.num_programs(0) - 1
    member = lax.axis_index("mp")
    half = lax.rem(member, 2)
    pair_id = member // 2
    width = wo_ref.shape[1]
    part_w = width // 2
    piece = part_w // 2
    share = width // GROUP
    total = out_ref.shape[0] // (2 * TILE)
    base, spot = line_up()
    core = lax.rem(spot, 2)
    chip = spot // 2
    bit_x = lax.rem(chip, 2)
    bit_y = chip // 2
    mate = mate_of(member)
    flips = (
        chip + 1 - 2 * bit_x,
        chip + 2 - 4 * bit_y,
        3 - chip,
    )

    def device(where):
        return {"dp": base + where, "mp": member}

    sibling = device(spot + 1 - 2 * core)
    others = [device(lax.rem(spot + turn, GROUP)) for turn in range(1, GROUP)]
    line = [{"dp": base + spot, "mp": lax.rem(member + turn, 4)} for turn in range(1, 4)]

    def rows_of(t):
        return pl.ds(pl.multiple_of((half * total + t) * TILE, TILE), TILE)

    def share_of(where):
        return pl.ds(pl.multiple_of(where * share, 32), share)

    def out_copy(t):
        return ahead(out_ref, rows_of(t), out_ref, out_send, out_recv, mate)

    def gh_local(t):
        return pltpu.make_async_copy(stage.at[lax.rem(t, 2)], gh_ref.at[rows_of(t)], loc_sem.at[t])

    def gh_copy(t):
        return ahead(gh_ref, rows_of(t), gh_ref, gh_send.at[t], gh_recv.at[t], mate)

    def own_copy(k):
        return pltpu.make_async_copy(gwm_ref.at[:, share_of(2 * k + core), :], m_own.at[k], own_sem.at[k])

    def core_copy(kind, k):
        src, dst = ((gwm_ref, m_core), (a_src, a_core))[kind]
        return pltpu.make_async_remote_copy(
            src_ref=src.at[:, share_of(2 * k + 1 - core), :], dst_ref=dst.at[k],
            send_sem=core_send.at[kind, k], recv_sem=core_recv.at[kind, k],
            device_id=sibling, device_id_type=pl.DeviceIdType.MESH,
        )

    def chip_copy(kind, r):
        src, dst = ((m_sum, m_chip), (a_sum, a_chip))[kind]
        return pltpu.make_async_remote_copy(
            src_ref=src.at[flips[r]], dst_ref=dst.at[r],
            send_sem=chip_send.at[kind, r], recv_sem=chip_recv.at[kind, r],
            device_id=device(2 * flips[r] + core), device_id_type=pl.DeviceIdType.MESH,
        )

    def give_copy(kind):
        src, dst = ((m_give, m_got), (a_give, a_got))[kind]
        return ahead(src, None, dst, give_send.at[kind], give_recv.at[kind], mate)

    def small_copy(n):
        return pltpu.make_async_remote_copy(
            src_ref=s_src, dst_ref=s_rcv.at[spot],
            send_sem=s_send.at[n], recv_sem=s_recv.at[n],
            device_id=others[n], device_id_type=pl.DeviceIdType.MESH,
        )

    def line_copy(n):
        return pltpu.make_async_remote_copy(
            src_ref=v_src, dst_ref=v_rcv.at[member],
            send_sem=v_send.at[n], recv_sem=v_recv.at[n],
            device_id=line[n], device_id_type=pl.DeviceIdType.MESH,
        )

    def u_copy():
        return ahead(u_give, None, u_got, u_send, u_recv, mate)

    @pl.when(tile == 0)
    def _():
        acc[...] = jnp.zeros_like(acc)
        vec_ref[...] = jnp.zeros_like(vec_ref)
        usum_ref[...] = jnp.zeros_like(usum_ref)
        greet(others + line)
        out_copy(total - 1).start()
        for k in range(4):
            core_copy(0, k).start()
        for k in range(4):
            own_copy(k).start()

    @pl.when(tile > 0)
    def _():
        gh_local(tile - 1).wait()
        gh_copy(tile - 1).start()

    own = pl.ds(pl.multiple_of(pair_id * part_w, 128), part_w)
    stream = stream_tile(hidden_ref, emb_ref, tile)
    hat, inv = norm_stats(stream)
    n1t_ref[...] = (hat * gain_ref[...] + shift_ref[...]).astype(BF16).T
    gm_low = gmid_ref[...].astype(BF16)
    gmt_ref[...] = gm_low.T
    gc_ref[...] = mm_nt(gm_low, wo_ref[...]).astype(BF16)
    acc[3] += mm(gmt_ref[...], ctx_ref[:, own])
    lane = lax.broadcasted_iota(jnp.int32, (WIN, 2 * HD), 1)
    low = lane < HD
    scale = HD ** (-0.5)
    pairs = width // (2 * HD)
    for win in range(TILE // WIN):
        rows = slice(win * WIN, (win + 1) * WIN)
        for pair in range(pairs):
            cols = slice(pair * 2 * HD, (pair + 1) * 2 * HD)
            q2 = qkv_ref[0, rows, cols]
            k2 = qkv_ref[1, rows, cols]
            v2 = qkv_ref[2, rows, cols]
            gc2 = gc_ref[rows, cols]
            dq, dk, dv = [], [], []
            for j in range(2):
                gc1 = jnp.where(low == (j == 0), gc2, jnp.zeros_like(gc2))
                probs_low = probs_ref[2 * pair + j, win]
                probs = probs_low.astype(F32)
                dprob = mm_nt(gc1, v2)
                mix = probs * dprob
                total_row = jnp.sum(mix, axis=-1, keepdims=True)
                grad_s = (mix - probs * total_row).astype(BF16)
                dv.append(mm_tn(probs_low, gc2))
                dk.append(mm_tn(grad_s, q2))
                dq.append(mm(grad_s, k2))
            gp_ref[0, rows, cols] = (jnp.where(low, dq[0], dq[1]) * scale).astype(BF16)
            gp_ref[1, rows, cols] = (jnp.where(low, dk[0], dk[1]) * scale).astype(BF16)
            gp_ref[2, rows, cols] = jnp.where(low, dv[0], dv[1]).astype(BF16)

    @pl.when(tile == 0)
    def _():
        for k in range(4):
            own_copy(k).wait()
            core_copy(0, k).wait_recv()
            m_sum[k] = (m_own[k].astype(F32) + m_core[k].astype(F32)).astype(BF16)

    grad_n = mm(gp_ref[0], wqkv_ref[0])
    for part in range(1, 3):
        grad_n = grad_n + mm(gp_ref[part], wqkv_ref[part])
    for part in range(3):
        acc[part] += mm(n1t_ref[...], gp_ref[part, :, own])

    @pl.when(tile == 0)
    def _():
        for r in range(3):
            chip_copy(0, r).start()

    stream = stream_tile(hidden_ref, emb_ref, tile)
    hat, inv = norm_stats(stream)
    vec_ref[0:1] += jnp.sum(grad_n * hat, axis=0, keepdims=True)
    vec_ref[1:2] += jnp.sum(grad_n, axis=0, keepdims=True)
    grad_in = gmid_ref[...] + norm_back(grad_n, gain_ref[...], hat, inv)
    stage[lax.rem(tile, 2)] = grad_in.astype(BF16)
    for unit in range(TILE // LEN_A):
        usum_ref[pl.ds(tile * (TILE // LEN_A) + unit, 1), :] = jnp.sum(
            grad_in[unit * LEN_A : (unit + 1) * LEN_A], axis=0, keepdims=True
        )
    gh_local(tile).start()

    @pl.when(tile == last)
    def _():
        units = usum_ref.shape[0]
        for group in range(2):
            for part in range(4):
                a_src[group, :, part * piece : (part + 1) * piece] = acc[
                    part, :, group * piece : (group + 1) * piece
                ].astype(BF16)
        s_src[0:units, :] = usum_ref[:, own]
        for left in range(2):
            cols = slice(left * part_w, (left + 1) * part_w)
            at = units + 8 * left
            s_src[at : at + 2, :] = vec_ref[0:2, cols]
            s_src[at + 2 : at + 6, :] = vecm_ref[0:4, cols]
            s_src[at + 6 : at + 7, :] = gbu_ref[0, 0:1, cols]
            s_src[at + 7 : at + 8, :] = gbu_ref[1, 0:1, cols]
        gh_local(tile).wait()
        gh_copy(tile).start()
        for k in range(4):
            core_copy(1, k).start()
        s_rcv[spot] = s_src[...]
        for n in range(GROUP - 1):
            small_copy(n).start()
        for r in range(3):
            chip_copy(0, r).wait_recv()
        kept_m = m_sum[chip, half].astype(F32)
        give_m = m_sum[chip, 1 - half].astype(F32)
        for r in range(3):
            kept_m = kept_m + m_chip[r, half].astype(F32)
            give_m = give_m + m_chip[r, 1 - half].astype(F32)
        m_give[...] = give_m.astype(BF16)
        gm_ref[...] = kept_m
        for k in range(4):
            core_copy(1, k).wait_recv()
            a_sum[k] = (
                a_src[:, share_of(2 * k + core), :].astype(F32) + a_core[k].astype(F32)
            ).astype(BF16)
        give_copy(0).start()
        for n in range(GROUP - 1):
            small_copy(n).wait_recv()
        for r in range(3):
            chip_copy(1, r).start()
        v_sum = s_rcv[0, units : units + 16, :]
        for n in range(1, GROUP):
            v_sum = v_sum + s_rcv[n, units : units + 16, :]
        v_src[...] = v_sum
        v_rcv[member] = v_sum
        for n in range(GROUP):
            whole_u = s_rcv[n, 0:units, :]
            left, right = whole_u[:, :piece], whole_u[:, piece:]
            u_give[n] = jnp.where(half == 0, right, left)
            u_mine[n] = jnp.where(half == 0, left, right)
        for n in range(3):
            line_copy(n).start()
        u_copy().start()
        give_copy(0).wait_recv()
        gm_ref[...] += m_got[...].astype(F32)
        for n in range(3):
            line_copy(n).wait_recv()
        every = 0.5 * ((v_rcv[0] + v_rcv[1]) + (v_rcv[2] + v_rcv[3]))
        other = member + 1 - 2 * half
        mine = v_rcv[member] + v_rcv[other]
        for left in range(2):
            cols = slice(left * part_w, (left + 1) * part_w)
            at = 8 * left
            vec_out[0:6, cols] = every[at : at + 6]
            vec_out[6:7, cols] = jnp.where(half == 0, mine[at + 6 : at + 7], mine[at + 7 : at + 8])
        u_copy().wait_recv()
        at = lax.broadcasted_iota(jnp.int32, (units, table_ref.shape[1]), 1)
        picks, sums = [], []
        for n in range(GROUP):
            for side in range(2):
                rows = slice(units * side, units * (side + 1))
                picks.append((ts_ref[n, rows, 0:1] == at).astype(F32))
                sums.append(jnp.where(half == side, u_mine[n], u_got[n]))
        pick = jnp.concatenate(picks, axis=0).astype(BF16)
        rest = jnp.concatenate(sums, axis=0)
        table = jnp.zeros(table_ref.shape, F32)
        for _ in range(3):
            first = rest.astype(BF16)
            table = table + mm_tn(first, pick)
            rest = rest - first.astype(F32)
        table_ref[...] = table
        for r in range(3):
            chip_copy(1, r).wait_recv()
        kept_a = a_sum[chip, half].astype(F32)
        give_a = a_sum[chip, 1 - half].astype(F32)
        for r in range(3):
            kept_a = kept_a + a_chip[r, half].astype(F32)
            give_a = give_a + a_chip[r, 1 - half].astype(F32)
        a_give[...] = give_a.astype(BF16)
        ga_ref[...] = kept_a
        give_copy(1).start()
        give_copy(1).wait_recv()
        ga_ref[...] += a_got[...].astype(F32)
        out_copy(total - 1).wait_recv()
        out_copy(total - 1).wait_send()
        for t in range(total):
            gh_copy(t).wait_recv()
            gh_copy(t).wait_send()
        for kind in range(2):
            for k in range(4):
                core_copy(kind, k).wait_send()
            for r in range(3):
                chip_copy(kind, r).wait_send()
            give_copy(kind).wait_send()
        for n in range(GROUP - 1):
            small_copy(n).wait_send()
        for n in range(3):
            line_copy(n).wait_send()
        u_copy().wait_send()


def finish_kernel(
    out_in, gh_in, gm_ref, ga_ref, vec_ref, table_in,
    out_ref, gh_ref, table_ref, g1_ref, s1_ref, qkv_ref, wo_ref, ob_ref,
    g2_ref, s2_ref, up_ref, ub_ref, down_ref, db_ref,
):
    out_ref[...] = out_in[...]
    gh_ref[...] = gh_in[...]

    @pl.when(pl.program_id(0) == 0)
    def _():
        ff = up_ref.shape[1]
        piece = qkv_ref.shape[2]
        table_ref[...] = table_in[...]
        up_ref[...] = gm_ref[:, 0:ff]
        down_ref[...] = gm_ref[:, ff : 2 * ff]
        for part in range(3):
            qkv_ref[part] = ga_ref[:, part * piece : (part + 1) * piece]
        wo_ref[...] = ga_ref[:, 3 * piece : 4 * piece].T
        for n, ref in enumerate((g1_ref, s1_ref, g2_ref, s2_ref, ob_ref, db_ref, ub_ref)):
            ref[...] = vec_ref[n]


LIMIT = 62 * 1024 * 1024


def half_map(steps):
    return lambda i: (lax.rem(lax.axis_index("mp"), 2) * steps + i, 0)


def fixed(shape):
    zeros = (0,) * len(shape)
    return pl.BlockSpec(shape, lambda i: zeros, pipeline_mode=pl.Buffered(1))


def attn_fwd(hidden, emb, gain, shift, ob, bias, ts, wqkv, wo, wu, wd):
    count, width = hidden.shape[0] // 2, hidden.shape[1]
    steps = count // TILE
    heads = width // HD
    rows = wo.shape[0]
    ff = wu.shape[1]
    tok = pl.BlockSpec((TILE, width), lambda i: (i, 0))
    anywhere = pl.BlockSpec(memory_space=pl.ANY)
    dma = pltpu.SemaphoreType.DMA
    return pl.pallas_call(
        attn_fwd_kernel,
        name="attn_fwd",
        grid=(steps,),
        in_specs=[
            pl.BlockSpec((TILE, width), half_map(steps)),
            fixed(emb.shape), fixed(gain.shape), fixed(shift.shape), fixed(ob.shape), fixed(bias.shape),
        ] + [anywhere] * 5,
        out_specs=[anywhere] * 6 + [
            pl.BlockSpec((3, TILE, width), lambda i: (0, i, 0)),
            pl.BlockSpec((heads, TILE // WIN, WIN, WIN), lambda i: (0, i, 0, 0)),
            tok,
            tok,
        ],
        out_shape=[
            jax.ShapeDtypeStruct((3, 4 * rows, width), BF16),
            jax.ShapeDtypeStruct((4 * rows, width), BF16),
            jax.ShapeDtypeStruct((4, width, ff), BF16),
            jax.ShapeDtypeStruct((4, ff, width), BF16),
            jax.ShapeDtypeStruct((4, 8, ff), F32),
            jax.ShapeDtypeStruct((GROUP,) + ts.shape, jnp.int32),
            jax.ShapeDtypeStruct((3, count, width), BF16),
            jax.ShapeDtypeStruct((heads, count // WIN, WIN, WIN), BF16),
            jax.ShapeDtypeStruct((count, width), BF16),
            jax.ShapeDtypeStruct((count, width), F32),
        ],
        scratch_shapes=[
            pltpu.VMEM((WIN, WIN), F32), pltpu.VMEM((TILE, width), BF16),
            pltpu.VMEM((3, 4 * rows, width), BF16), pltpu.VMEM((4 * rows, width), BF16),
            pltpu.VMEM((TILE, width), BF16),
            pltpu.VMEM(wu.shape, BF16), pltpu.VMEM(wd.shape, BF16),
            pltpu.VMEM((8, ff), F32), pltpu.VMEM(ts.shape, jnp.int32),
            dma((16,)), dma((2,)), dma((4, 3)), dma((4, 3)), dma((3,)), dma((3,)),
            dma((4, 3, 7)), dma((4, 3, 7)), dma((GROUP - 1,)), dma((GROUP - 1,)),
        ],
        compiler_params=pltpu.CompilerParams(
            collective_id=1, has_side_effects=True, vmem_limit_bytes=LIMIT
        ),
        cost_estimate=pl.CostEstimate(flops=12_000_000_000, bytes_accessed=30_000_000, transcendentals=5_000_000),
    )(hidden, emb, gain, shift, ob, bias, ts, wqkv, wo, wu, wd)


def mlp(mid, gy, wu, bu, wd, gain, shift, db):
    count, width = mid.shape
    steps = count // TILE
    ff = wu.shape[2]
    tok = pl.BlockSpec((TILE, width), lambda i: (i, 0))
    dma = pltpu.SemaphoreType.DMA
    return pl.pallas_call(
        mlp_kernel,
        name="mlp_both",
        grid=(steps,),
        in_specs=[
            tok,
            pl.BlockSpec((TILE, width), half_map(steps)),
            fixed(wu.shape), fixed(bu.shape), fixed(wd.shape),
            fixed(gain.shape), fixed(shift.shape), fixed(db.shape),
        ],
        out_specs=[
            pl.BlockSpec(memory_space=pl.ANY), tok, fixed((2, width, 2 * ff)),
            fixed((8, width)), fixed((2, 8, ff)),
        ],
        scratch_shapes=[
            pltpu.VMEM((2, width, ff), F32), pltpu.VMEM((2, width, ff), F32),
            pltpu.VMEM((TILE, width), BF16), pltpu.VMEM((width, TILE), BF16),
            pltpu.VMEM((width, TILE), BF16),
            pltpu.VMEM((TILE, width), F32), pltpu.VMEM((TILE, width), F32),
            pltpu.VMEM((2, TILE, width), BF16), dma((steps,)), dma((steps,)), dma((steps,)),
        ],
        out_shape=[
            jax.ShapeDtypeStruct((2 * count, width), BF16),
            jax.ShapeDtypeStruct((count, width), F32),
            jax.ShapeDtypeStruct((2, width, 2 * ff), BF16),
            jax.ShapeDtypeStruct((8, width), F32),
            jax.ShapeDtypeStruct((2, 8, ff), F32),
        ],
        compiler_params=pltpu.CompilerParams(
            collective_id=2, has_side_effects=True, vmem_limit_bytes=LIMIT
        ),
        cost_estimate=pl.CostEstimate(flops=36_000_000_000, bytes_accessed=30_000_000, transcendentals=5_000_000),
    )(mid, gy, wu, bu, wd, gain, shift, db)


def attn_bwd(hidden, emb, gain, shift, wqkv, wo, qkv, probs, ctx, gmid, gwm, vecm, gbu, ts, out, table_rows):
    count, width = gmid.shape
    steps = count // TILE
    heads = width // HD
    share = width // GROUP
    wide = gwm.shape[2]
    units = emb.shape[0]
    piece = width // 4
    tok = pl.BlockSpec((TILE, width), lambda i: (i, 0))
    anywhere = pl.BlockSpec(memory_space=pl.ANY)
    dma = pltpu.SemaphoreType.DMA
    return pl.pallas_call(
        attn_bwd_kernel,
        name="attn_bwd",
        grid=(steps,),
        in_specs=[
            pl.BlockSpec((TILE, width), half_map(steps)),
            fixed(emb.shape), fixed(gain.shape), fixed(shift.shape),
            fixed(wqkv.shape), fixed(wo.shape),
            pl.BlockSpec((3, TILE, width), lambda i: (0, i, 0)),
            pl.BlockSpec((heads, TILE // WIN, WIN, WIN), lambda i: (0, i, 0, 0)),
            tok, tok, anywhere, fixed(vecm.shape), fixed(gbu.shape), fixed(ts.shape), anywhere,
        ],
        out_specs=[
            anywhere, anywhere, fixed((share, wide)), fixed((share, width)),
            fixed((8, width)), fixed((piece, table_rows)),
        ],
        scratch_shapes=[
            pltpu.VMEM((4, width, width // 2), F32),
            pltpu.VMEM((3, TILE, width), BF16), pltpu.VMEM((TILE, width), BF16),
            pltpu.VMEM((width, TILE), BF16), pltpu.VMEM((width, TILE), BF16),
            pltpu.VMEM((8, width), F32), pltpu.VMEM((units, width), F32),
            pltpu.VMEM((2, TILE, width), BF16),
            pltpu.VMEM((4, 2, share, wide), BF16), pltpu.VMEM((4, 2, share, wide), BF16),
            pltpu.VMEM((4, 2, share, wide), BF16), pltpu.VMEM((3, 2, share, wide), BF16),
            pltpu.VMEM((share, wide), BF16), pltpu.VMEM((share, wide), BF16),
            pltpu.VMEM((2, width, width), BF16), pltpu.VMEM((4, 2, share, width), BF16),
            pltpu.VMEM((4, 2, share, width), BF16), pltpu.VMEM((3, 2, share, width), BF16),
            pltpu.VMEM((share, width), BF16), pltpu.VMEM((share, width), BF16),
            pltpu.VMEM((units + 16, width // 2), F32), pltpu.VMEM((GROUP, units + 16, width // 2), F32),
            pltpu.VMEM((16, width // 2), F32), pltpu.VMEM((4, 16, width // 2), F32),
            pltpu.VMEM((GROUP, units, piece), F32), pltpu.VMEM((GROUP, units, piece), F32),
            pltpu.VMEM((GROUP, units, piece), F32),
            dma((4,)), dma(()), dma(()), dma((steps,)), dma((steps,)), dma((steps,)),
            dma((2, 4)), dma((2, 4)), dma((2, 3)), dma((2, 3)), dma((2,)), dma((2,)),
            dma((GROUP - 1,)), dma((GROUP - 1,)), dma((3,)), dma((3,)), dma(()), dma(()),
        ],
        out_shape=[
            jax.ShapeDtypeStruct((2 * count, width), BF16),
            jax.ShapeDtypeStruct((2 * count, width), BF16),
            jax.ShapeDtypeStruct((share, wide), F32),
            jax.ShapeDtypeStruct((share, width), F32),
            jax.ShapeDtypeStruct((8, width), F32),
            jax.ShapeDtypeStruct((piece, table_rows), F32),
        ],
        input_output_aliases={14: 0},
        compiler_params=pltpu.CompilerParams(
            collective_id=3, has_side_effects=True, vmem_limit_bytes=LIMIT
        ),
        cost_estimate=pl.CostEstimate(flops=20_000_000_000, bytes_accessed=40_000_000, transcendentals=0),
    )(hidden, emb, gain, shift, wqkv, wo, qkv, probs, ctx, gmid, gwm, vecm, gbu, ts, out)


def finish(out, gh, gm, ga, vec, table):
    count, width = out.shape
    share = gm.shape[0]
    ff = gm.shape[1] // 2
    piece = width // 4
    tok = pl.BlockSpec((2 * TILE, width), lambda i: (i, 0))
    line = jax.ShapeDtypeStruct((width,), F32)
    shapes = [
        jax.ShapeDtypeStruct(table.shape, F32), line, line,
        jax.ShapeDtypeStruct((3, share, piece), F32), jax.ShapeDtypeStruct((piece, share), F32),
        line, line, line,
        jax.ShapeDtypeStruct((share, ff), F32), line, jax.ShapeDtypeStruct((share, ff), F32), line,
    ]
    return pl.pallas_call(
        finish_kernel,
        name="finish",
        grid=(count // (2 * TILE),),
        in_specs=[tok, tok] + [fixed(x.shape) for x in (gm, ga, vec, table)],
        out_specs=[tok, tok] + [fixed(x.shape) for x in shapes],
        out_shape=[jax.ShapeDtypeStruct(out.shape, BF16), jax.ShapeDtypeStruct(gh.shape, BF16)] + shapes,
        compiler_params=pltpu.CompilerParams(vmem_limit_bytes=LIMIT),
        cost_estimate=pl.CostEstimate(flops=1_000_000, bytes_accessed=20_000_000, transcendentals=0),
    )(out, gh, gm, ga, vec, table)


def local(
    hidden, timesteps, cotangent, time_table, first_gain, first_shift, qkv_weight, out_weight,
    out_bias, second_gain, second_shift, up_weight, up_bias, down_weight, down_bias,
):
    count = hidden.shape[0]
    half = lax.rem(lax.axis_index("mp"), 2)
    units = count // LEN_A
    unit = jnp.arange(units, dtype=jnp.int32)
    within = unit % 8
    row_of = unit // 8 * 6 + jnp.where(within < 4, within, 4 + (within - 4) // 2)
    unit_step = jnp.pad(
        jnp.take(timesteps, row_of).reshape(2, units // 2), ((0, 0), (0, 16 - units // 2)), constant_values=-1
    )
    emb = jnp.take(time_table, jnp.maximum(unit_step[half], 0), axis=0).astype(F32)
    stamps = jnp.broadcast_to(unit_step.reshape(32, 1), (32, 128))

    wqkv_f, wo_f, wu_f, wd_f, bu_f, ts_f, qkv, probs, ctx, mid = attn_fwd(
        hidden, emb, first_gain, first_shift, out_bias, up_bias, stamps,
        jnp.swapaxes(qkv_weight, 1, 2), out_weight, up_weight, down_weight,
    )
    output, gmid, gw_mlp, vec_mlp, gbu = mlp(
        mid, cotangent, wu_f, bu_f, wd_f, second_gain, second_shift, down_bias
    )
    output, grad_hidden, g_mlp, g_attn, vecs, table = attn_bwd(
        hidden, emb, first_gain, first_shift, wqkv_f, wo_f, qkv, probs, ctx, gmid,
        gw_mlp, vec_mlp, gbu, ts_f, output, time_table.shape[0],
    )
    outs = list(finish(output, grad_hidden, g_mlp, g_attn, vecs, table))
    outs[2], outs[12] = outs[2].T, outs[12].T
    groups = lax.axis_size("dp") // GROUP
    if groups > 1:
        spots = [[g * GROUP + n for n in range(GROUP)] for g in range(groups)]
        split = {5: 1, 6: 1, 10: 0, 12: 1}
        for n in range(2, len(outs)):
            value = outs[n] * (1.0 / GROUP)
            if n in split:
                value = lax.all_gather(value, "dp", axis_index_groups=spots, axis=split[n], tiled=True)
                outs[n] = lax.psum_scatter(value, "dp", scatter_dimension=split[n], tiled=True)
            else:
                outs[n] = lax.psum(value, "dp")
    return tuple(outs)


def solution(mesh):
    return jax.shard_map(
        local,
        mesh=mesh,
        in_specs=(
            P("dp", None), P("dp"), P("dp", None), P(), P(), P(), P(None, None, "mp"),
            P("mp", None), P(), P(), P(), P(None, "mp"), P("mp"), P("mp", None), P(),
        ),
        out_specs=(
            P("dp", None), P("dp", None), P(None, "mp"), P(), P(), P(None, "dp", "mp"),
            P("mp", "dp"), P(), P(), P(), P("dp", "mp"), P("mp"), P("mp", "dp"), P(),
        ),
        check_vma=False,
    )
```

```python
from functools import partial

import jax
import jax.numpy as jnp
from jax import lax
from jax.experimental import pallas as pl
from jax.experimental.pallas import tpu as pltpu
from jax.sharding import PartitionSpec as P

F32 = jnp.float32
BF16 = jnp.bfloat16
HD = 64
LEN_A = 128
LEN_B = 256
BLOCK = 512
WIN = 256
TILE = 512
GROUP = 8
HALF = TILE // 2
EPS = 1e-05
GELU_C = 0.7978845608028654
GELU_A = 0.044715


def mm(a, b):
    return lax.dot_general(a, b, (((1,), (0,)), ((), ())), preferred_element_type=F32)


def mm_nt(a, b):
    return lax.dot_general(a, b, (((1,), (1,)), ((), ())), preferred_element_type=F32)


def mm_tn(a, b):
    return lax.dot_general(a, b, (((0,), (0,)), ((), ())), preferred_element_type=F32)


def norm_stats(rows):
    centre = jnp.mean(rows, axis=-1, keepdims=True)
    offset = rows - centre
    spread = jnp.mean(offset * offset, axis=-1, keepdims=True)
    inv = lax.rsqrt(spread + EPS)
    return offset * inv, inv


def norm_back(grad, gain, hat, inv):
    dhat = grad * gain
    first = jnp.mean(dhat, axis=-1, keepdims=True)
    second = jnp.mean(dhat * hat, axis=-1, keepdims=True)
    return inv * (dhat - first - hat * second)


def stream_tile(hidden_ref, emb_ref, tile):
    parts = []
    for unit in range(TILE // LEN_A):
        row = emb_ref[pl.ds(tile * (TILE // LEN_A) + unit, 1), :]
        parts.append(hidden_ref[unit * LEN_A : (unit + 1) * LEN_A, :].astype(F32) + row)
    return jnp.concatenate(parts, axis=0)


def line_up():
    place = lax.axis_index("dp")
    spot = lax.rem(place, GROUP)
    return place - spot, spot


def ahead(ref, rows, dst, send, recv, target):
    return pltpu.make_async_remote_copy(
        src_ref=ref.at[rows] if rows is not None else ref,
        dst_ref=dst.at[rows] if rows is not None else dst,
        send_sem=send, recv_sem=recv, device_id=target, device_id_type=pl.DeviceIdType.MESH,
    )


def mate_of(member):
    return {"dp": lax.axis_index("dp"), "mp": member + 1 - 2 * lax.rem(member, 2)}


def greet(targets):
    barrier = pltpu.get_barrier_semaphore()
    for target in targets:
        pl.semaphore_signal(barrier, inc=1, device_id=target, device_id_type=pl.DeviceIdType.MESH)
    pl.semaphore_wait(barrier, len(targets))


def attn_fwd_kernel(
    hidden_ref, emb_ref, gain_ref, shift_ref, ob_ref, bias_ref, ts_ref, wqkv, wo, wu, wd,
    wqkv_f, wo_f, wu_f, wd_f, bu_f, ts_f, qkv_ref, probs_ref, ctx_ref, mid_ref,
    same_ref, ctx_acc, wqkv_v, wo_v, norm_v, hold_wu, hold_wd, hold_bu, hold_ts,
    loc_sem, load_sem, z_send, z_recv, b_send, b_recv, n_send, n_recv, t_send, t_recv,
):
    tile = pl.program_id(0)
    steps = pl.num_programs(0)
    last = steps - 1
    member = lax.axis_index("mp")
    half = lax.rem(member, 2)
    place = lax.axis_index("dp")
    base, spot = line_up()
    bit0 = lax.rem(spot, 2)
    bit1 = lax.rem(spot // 2, 2)
    bit2 = spot // 4

    def flip(where, bit, size):
        return where + size - 2 * size * bit

    near = {
        "core": {"dp": flip(place, bit0, 1), "mp": member},
        "x": {"dp": flip(place, bit1, 2), "mp": member},
        "y": {"dp": flip(place, bit2, 4), "mp": member},
    }
    from_x = flip(spot, bit1, 2)
    from_y = flip(spot, bit2, 4)
    from_d = flip(from_x, bit2, 4)
    others = [{"dp": base + lax.rem(spot + turn, GROUP), "mp": member} for turn in range(1, GROUP)]

    def peer(turn):
        return {"dp": place, "mp": lax.rem(member + turn, 4)}

    rows_a = wo.shape[0]
    step_a = rows_a // GROUP
    step_m = wu.shape[0] // GROUP

    def full_at(array, shard, piece):
        if array == 0:
            return wqkv_f.at[:, pl.ds(shard * rows_a + piece * step_a, step_a), :]
        if array == 1:
            return wo_f.at[pl.ds(shard * rows_a + piece * step_a, step_a), :]
        full = wu_f if array == 2 else wd_f
        return full.at[shard, pl.ds(piece * step_m, step_m), :]

    def own_at(array, piece):
        if array == 0:
            return wqkv.at[:, pl.ds(piece * step_a, step_a), :]
        if array == 1:
            return wo.at[pl.ds(piece * step_a, step_a), :]
        return (wu if array == 2 else wd).at[pl.ds(piece * step_m, step_m), :]

    def remote(src, dst, send, recv, target):
        return pltpu.make_async_remote_copy(
            src_ref=src, dst_ref=dst, send_sem=send, recv_sem=recv,
            device_id=target, device_id_type=pl.DeviceIdType.MESH,
        )

    pair = member // 2
    mate = member + 1 - 2 * half
    beyond = 2 * member - mate
    middle = (member == 1) | (member == 2)
    shards = (mate, 2 - pair, 3 - 3 * pair)

    def z_own(array, side):
        return remote(
            own_at(array, spot), full_at(array, member, spot),
            z_send.at[array, side], z_recv.at[array, member],
            {"dp": place, "mp": (mate, beyond)[side]},
        )

    def z_on(array, turn):
        shard = shards[turn]
        onward = jnp.where(shard < member, member + 1, member - 1)
        return remote(
            full_at(array, shard, spot), full_at(array, shard, spot),
            z_send.at[array, 2 + turn], z_recv.at[array, shard],
            {"dp": place, "mp": onward},
        )

    def z_start(array):
        z_own(array, 0).start()

        @pl.when(middle)
        def _():
            z_own(array, 1).start()

    def bias_copy(turn):
        return remote(hold_bu, bu_f.at[member], b_send.at[turn - 1], b_recv.at[turn - 1], peer(turn))

    def stamp_copy(n):
        return remote(ts_ref, ts_f.at[spot], t_send.at[n], t_recv.at[n], others[n])

    def push(array, turn, kind):
        shard = shards[turn]
        by_x = (array + turn) % 2 == 0
        piece = (spot, spot, from_x if by_x else from_y, spot, from_x, from_y, from_d)[kind]
        target = ("x", "y", "y" if by_x else "x", "core", "core", "core", "core")[kind]
        return remote(
            full_at(array, shard, piece), full_at(array, shard, piece),
            n_send.at[array, turn, kind], n_recv.at[array, turn, kind], near[target],
        )

    order = (0, 1, 2)

    def stage_z(array):
        for turn in order:
            z_on(array, turn).wait_recv()

            @pl.when(middle)
            def _():
                z_on(array, turn).start()

            for kind in (0, 1, 3):
                push(array, turn, kind).start()

    def stage_near(array):
        for turn in order:
            push(array, turn, 0).wait_recv()
            if (array + turn) % 2 == 0:
                push(array, turn, 2).start()
            push(array, turn, 4).start()
            push(array, turn, 1).wait_recv()
            if (array + turn) % 2 == 1:
                push(array, turn, 2).start()
            push(array, turn, 5).start()

    def stage_far(array):
        for turn in order:
            push(array, turn, 2).wait_recv()
            push(array, turn, 6).start()

    def settle(array):
        for turn in order:
            for kind in range(3, 7):
                push(array, turn, kind).wait_recv()

    own_rows = pl.ds(pl.multiple_of(member * rows_a, 64), rows_a)
    own_parts = (
        (wqkv, wqkv_v.at[:, own_rows, :], wqkv_f.at[:, own_rows, :]),
        (wo, wo_v.at[own_rows, :], wo_f.at[own_rows, :]),
        (wu, hold_wu, wu_f.at[member]),
        (wd, hold_wd, wd_f.at[member]),
        (ts_ref, hold_ts, ts_f.at[spot]),
    )

    def into(n):
        return pltpu.make_async_copy(own_parts[n][0], own_parts[n][1], loc_sem.at[n])

    def outof(n):
        return pltpu.make_async_copy(own_parts[n][1], own_parts[n][2], loc_sem.at[8 + n])

    def bias_out():
        return pltpu.make_async_copy(hold_bu, bu_f.at[member], loc_sem.at[15])

    def load(array):
        src, dst = ((wqkv_f, wqkv_v), (wo_f, wo_v))[array]
        return pltpu.make_async_copy(src, dst, load_sem.at[array])

    @pl.when(tile == 0)
    def _():
        hold_bu[...] = jnp.broadcast_to(bias_ref[...], hold_bu.shape)
        for n in range(5):
            into(n).start()
        greet([peer(1), peer(2), peer(3)] + others)
        for array in range(3):
            z_start(array)

    stream = stream_tile(hidden_ref, emb_ref, tile)
    hat, _ = norm_stats(stream)
    norm_v[...] = (hat * gain_ref[...] + shift_ref[...]).astype(BF16)
    mid_ref[...] = stream + ob_ref[...]

    @pl.when(tile == 0)
    def _():
        for n in range(5):
            into(n).wait()
            outof(n).start()
        stage_z(0)
        stage_z(1)
        z_start(3)
        for n in range(GROUP - 1):
            stamp_copy(n).start()
        bias_out().start()
        for turn in (1, 2, 3):
            bias_copy(turn).start()
        stage_near(0)
        stage_near(1)
        stage_far(0)
        stage_far(1)
        stage_z(2)
        settle(0)
        outof(0).wait()
        load(0).start()
        load(0).wait()

    for part in range(3):
        qkv_ref[part] = mm_nt(norm_v[...], wqkv_v[part]).astype(BF16)

    @pl.when(tile == 0)
    def _():
        settle(1)
        outof(1).wait()
        load(1).start()

    lane = lax.broadcasted_iota(jnp.int32, (WIN, 2 * HD), 1)
    low = lane < HD
    row_i = lax.broadcasted_iota(jnp.int32, (WIN, WIN), 0)
    col_i = lax.broadcasted_iota(jnp.int32, (WIN, WIN), 1)
    same_half = (row_i < LEN_A) == (col_i < LEN_A)
    scale = HD ** (-0.5)
    pairs = qkv_ref.shape[2] // (2 * HD)
    for win in range(TILE // WIN):
        at = ((half * steps + tile) * (TILE // WIN) + win) % 4
        same_ref[...] = jnp.where(same_half, 0.0, jnp.where(at < 2, -1e9, 0.0))
        rows = slice(win * WIN, (win + 1) * WIN)
        for pair in range(pairs):
            cols = slice(pair * 2 * HD, (pair + 1) * 2 * HD)
            q2 = qkv_ref[0, rows, cols] * jnp.asarray(scale, BF16)
            k2 = qkv_ref[1, rows, cols]
            v2 = qkv_ref[2, rows, cols]
            outs = []
            for j in range(2):
                q1 = jnp.where(low == (j == 0), q2, jnp.zeros_like(q2))
                scores = mm_nt(k2, q1) + same_ref[...]
                top = jnp.max(scores, axis=0, keepdims=True)
                expo = jnp.exp(scores - top)
                total = jnp.sum(expo, axis=0, keepdims=True)
                probs = (expo * (1.0 / total)).astype(BF16)
                probs_ref[2 * pair + j, win] = probs
                outs.append(mm_tn(probs, v2))
            ctx_acc[rows, cols] = jnp.where(low, outs[0], outs[1]).astype(BF16)
        if win == 0:

            @pl.when(tile == 0)
            def _():
                stage_near(2)

            @pl.when(tile == 1)
            def _():
                stage_far(2)

            @pl.when(tile == last)
            def _():
                stage_far(3)

    @pl.when(tile == 0)
    def _():
        load(1).wait()

    ctx_ref[...] = ctx_acc[...]
    mid_ref[...] += mm(ctx_acc[...], wo_v[...])

    @pl.when(tile == 0)
    def _():
        stage_z(3)

    @pl.when(tile == 1)
    def _():
        stage_near(3)

    @pl.when(tile == last)
    def _():
        settle(2)
        settle(3)
        for n in range(GROUP - 1):
            stamp_copy(n).wait_recv()
            stamp_copy(n).wait_send()
        for turn in (1, 2, 3):
            bias_copy(turn).wait_recv()
            bias_copy(turn).wait_send()
        for array in range(4):
            z_own(array, 0).wait_send()

            @pl.when(middle)
            def _():
                z_own(array, 1).wait_send()
                for turn in order:
                    z_on(array, turn).wait_send()

            for turn in order:
                for kind in range(7):
                    push(array, turn, kind).wait_send()
        for n in range(2, 5):
            outof(n).wait()
        bias_out().wait()


def mlp_kernel(
    mid_ref, gy_ref, wu_ref, bu_ref, wd_ref, gain_ref, shift_ref, db_ref,
    out_ref, gmid_ref, gw_ref, vec_ref, gbu_ref,
    acc_u, acc_d, n2_ref, n2t_ref, gyt_ref, mlp_ref, dn_ref, stage, loc_sem, send_sem, recv_sem,
):
    tile = pl.program_id(0)
    steps = pl.num_programs(0)
    last = steps - 1
    member = lax.axis_index("mp")
    half = lax.rem(member, 2)
    pair = member // 2
    mate = mate_of(member)
    ff = wu_ref.shape[2]
    total = out_ref.shape[0] // (2 * HALF)

    def rows_of(t):
        return pl.ds(pl.multiple_of((half * total + t) * HALF, HALF), HALF)

    def local_copy(t):
        return pltpu.make_async_copy(stage.at[lax.rem(t, 2)], out_ref.at[rows_of(t)], loc_sem.at[t])

    def remote_copy(t):
        return ahead(out_ref, rows_of(t), out_ref, send_sem.at[t], recv_sem.at[t], mate)

    @pl.when(tile == 0)
    def _():
        acc_u[...] = jnp.zeros_like(acc_u)
        acc_d[...] = jnp.zeros_like(acc_d)
        vec_ref[...] = jnp.zeros_like(vec_ref)
        gbu_ref[...] = jnp.zeros_like(gbu_ref)
        greet([mate])

    @pl.when(tile > 0)
    def _():
        local_copy(tile - 1).wait()
        remote_copy(tile - 1).start()

    hat, inv = norm_stats(mid_ref[...])
    normed = (hat * gain_ref[...] + shift_ref[...]).astype(BF16)
    n2_ref[...] = normed
    n2t_ref[...] = normed.T
    gyt_ref[...] = gy_ref[...].T
    mlp_ref[...] = mid_ref[...] + db_ref[...]
    dn_ref[...] = jnp.zeros_like(dn_ref)

    def step(turn, own):
        group = lax.rem(2 * pair + turn, 4)
        pre = mm(n2_ref[...], wu_ref[group]) + bu_ref[group, 0:1]
        grad_act = mm_nt(gy_ref[...], wd_ref[group])
        square = pre * pre
        bend = jnp.tanh(pre * (GELU_C + (GELU_C * GELU_A) * square))
        half_in = 0.5 * pre
        up = 1.0 + bend
        act = (half_in * up).astype(BF16)
        slope = 0.5 * up + half_in * (1.0 - bend * bend) * (GELU_C + (3.0 * GELU_C * GELU_A) * square)
        grad_f = grad_act * slope
        grad_pre = grad_f.astype(BF16)
        mlp_ref[...] += mm(act, wd_ref[group])
        dn_ref[...] += mm_nt(grad_pre, wu_ref[group])
        if own:
            acc_u[turn] += mm(n2t_ref[...], grad_pre)
            acc_d[turn] += mm(gyt_ref[...], act)
            gbu_ref[turn, 0:1] += jnp.sum(grad_pre.astype(F32), axis=0, keepdims=True)

    lax.fori_loop(0, 2, lambda turn, c: (step(turn, True), c)[1], 0)
    lax.fori_loop(2, 4, lambda turn, c: (step(turn, False), c)[1], 0)

    stage[lax.rem(tile, 2)] = mlp_ref[...].astype(BF16)
    hat, inv = norm_stats(mid_ref[...])
    top = gy_ref[...].astype(F32)
    dn = dn_ref[...]
    vec_ref[0:1] += jnp.sum(dn * hat, axis=0, keepdims=True)
    vec_ref[1:2] += jnp.sum(dn, axis=0, keepdims=True)
    gmid = top + norm_back(dn, gain_ref[...], hat, inv)
    vec_ref[2:3] += jnp.sum(gmid, axis=0, keepdims=True)
    vec_ref[3:4] += jnp.sum(top, axis=0, keepdims=True)
    gmid_ref[...] = gmid
    local_copy(tile).start()

    @pl.when(tile == last)
    def _():
        gw_ref[:, :, 0:ff] = acc_u[...].astype(BF16)
        gw_ref[:, :, ff : 2 * ff] = acc_d[...].astype(BF16)
        local_copy(tile).wait()
        for t in range(total - 1):
            remote_copy(t).wait_send()
            remote_copy(t).wait_recv()


def attn_bwd_kernel(
    hidden_ref, emb_ref, gain_ref, shift_ref, wqkv_ref, wo_ref,
    qkv_ref, probs_ref, ctx_ref, gmid_ref, gwm_ref, vecm_ref, gbu_ref, ts_ref, out_in,
    out_ref, gh_ref, gm_ref, ga_ref, vec_out, table_ref,
    acc, gp_ref, gc_ref, n1t_ref, gmt_ref, vec_ref, usum_ref, stage,
    m_own, m_core, m_sum, m_chip, m_give, m_got,
    a_src, a_core, a_sum, a_chip, a_give, a_got,
    s_src, s_rcv, v_src, v_rcv, u_give, u_got, u_mine,
    own_sem, out_send, out_recv, loc_sem, gh_send, gh_recv,
    core_send, core_recv, chip_send, chip_recv, give_send, give_recv,
    s_send, s_recv, v_send, v_recv, u_send, u_recv,
):
    tile = pl.program_id(0)
    last = pl.num_programs(0) - 1
    member = lax.axis_index("mp")
    half = lax.rem(member, 2)
    pair_id = member // 2
    width = wo_ref.shape[1]
    part_w = width // 2
    piece = part_w // 2
    share = width // GROUP
    total = out_ref.shape[0] // (2 * TILE)
    base, spot = line_up()
    core = lax.rem(spot, 2)
    chip = spot // 2
    bit_x = lax.rem(chip, 2)
    bit_y = chip // 2
    mate = mate_of(member)
    flips = (
        chip + 1 - 2 * bit_x,
        chip + 2 - 4 * bit_y,
        3 - chip,
    )

    def device(where):
        return {"dp": base + where, "mp": member}

    sibling = device(spot + 1 - 2 * core)
    others = [device(lax.rem(spot + turn, GROUP)) for turn in range(1, GROUP)]
    line = [{"dp": base + spot, "mp": lax.rem(member + turn, 4)} for turn in range(1, 4)]

    def share_of(where):
        return pl.ds(pl.multiple_of(where * share, 32), share)

    def out_copy():
        rows = pl.ds(pl.multiple_of((half * 2 * total + 2 * total - 1) * HALF, HALF), HALF)
        return ahead(out_ref, rows, out_ref, out_send, out_recv, mate)

    chunks = 2 * total

    def gh_local(n):
        rows = pl.ds(pl.multiple_of((half * chunks + n) * HALF, HALF), HALF)
        return pltpu.make_async_copy(stage.at[lax.rem(n, 2)], gh_ref.at[rows], loc_sem.at[n])

    def gh_copy(n):
        rows = pl.ds(pl.multiple_of((half * chunks + n) * HALF, HALF), HALF)
        return ahead(gh_ref, rows, gh_ref, gh_send.at[n], gh_recv.at[n], mate)

    def gh_last(n):
        quarter = HALF // 2
        rows = pl.ds(pl.multiple_of((half * chunks + chunks - 1) * HALF + n * quarter, quarter), quarter)
        return ahead(gh_ref, rows, gh_ref, gh_send.at[chunks - 1 + n], gh_recv.at[chunks - 1 + n], mate)

    def own_copy(k):
        return pltpu.make_async_copy(gwm_ref.at[:, share_of(2 * k + core), :], m_own.at[k], own_sem.at[k])

    def core_copy(kind, k):
        src, dst = ((gwm_ref, m_core), (a_src, a_core))[kind]
        return pltpu.make_async_remote_copy(
            src_ref=src.at[:, share_of(2 * k + 1 - core), :], dst_ref=dst.at[k],
            send_sem=core_send.at[kind, k], recv_sem=core_recv.at[kind, k],
            device_id=sibling, device_id_type=pl.DeviceIdType.MESH,
        )

    def chip_copy(kind, r):
        src, dst = ((m_sum, m_chip), (a_sum, a_chip))[kind]
        return pltpu.make_async_remote_copy(
            src_ref=src.at[flips[r]], dst_ref=dst.at[r],
            send_sem=chip_send.at[kind, r], recv_sem=chip_recv.at[kind, r],
            device_id=device(2 * flips[r] + core), device_id_type=pl.DeviceIdType.MESH,
        )

    def give_copy(kind):
        src, dst = ((m_give, m_got), (a_give, a_got))[kind]
        return ahead(src, None, dst, give_send.at[kind], give_recv.at[kind], mate)

    def small_copy(n):
        return pltpu.make_async_remote_copy(
            src_ref=s_src, dst_ref=s_rcv.at[spot],
            send_sem=s_send.at[n], recv_sem=s_recv.at[n],
            device_id=others[n], device_id_type=pl.DeviceIdType.MESH,
        )

    def line_copy(n):
        return pltpu.make_async_remote_copy(
            src_ref=v_src, dst_ref=v_rcv.at[member],
            send_sem=v_send.at[n], recv_sem=v_recv.at[n],
            device_id=line[n], device_id_type=pl.DeviceIdType.MESH,
        )

    def u_copy():
        return ahead(u_give, None, u_got, u_send, u_recv, mate)

    @pl.when(tile == 0)
    def _():
        acc[...] = jnp.zeros_like(acc)
        vec_ref[...] = jnp.zeros_like(vec_ref)
        usum_ref[...] = jnp.zeros_like(usum_ref)
        greet(others + line)
        out_copy().start()
        for k in range(4):
            core_copy(0, k).start()
        for k in range(4):
            own_copy(k).start()

    @pl.when(tile > 0)
    def _():
        gh_local(2 * tile - 1).wait()
        gh_copy(2 * tile - 1).start()

    own = pl.ds(pl.multiple_of(pair_id * part_w, 128), part_w)
    stream = stream_tile(hidden_ref, emb_ref, tile)
    hat, inv = norm_stats(stream)
    n1t_ref[...] = (hat * gain_ref[...] + shift_ref[...]).astype(BF16).T
    gm_low = gmid_ref[...].astype(BF16)
    gmt_ref[...] = gm_low.T
    gc_ref[...] = mm_nt(gm_low, wo_ref[...]).astype(BF16)
    acc[3] += mm(gmt_ref[...], ctx_ref[:, own])
    lane = lax.broadcasted_iota(jnp.int32, (WIN, 2 * HD), 1)
    low = lane < HD
    scale = HD ** (-0.5)
    pairs = width // (2 * HD)
    for win in range(TILE // WIN):
        rows = slice(win * WIN, (win + 1) * WIN)
        for pair in range(pairs):
            cols = slice(pair * 2 * HD, (pair + 1) * 2 * HD)
            if win == 1 and pair == 1:
                gh_local(2 * tile).wait()
                gh_copy(2 * tile).start()
            q2 = qkv_ref[0, rows, cols]
            k2 = qkv_ref[1, rows, cols]
            v2 = qkv_ref[2, rows, cols]
            gc2 = gc_ref[rows, cols]
            dq, dk, dv = [], [], []
            for j in range(2):
                gc1 = jnp.where(low == (j == 0), gc2, jnp.zeros_like(gc2))
                probs_low = probs_ref[2 * pair + j, win]
                probs = probs_low.astype(F32)
                dprob = mm_nt(v2, gc1)
                mix = probs * dprob
                total_row = jnp.sum(mix, axis=0, keepdims=True)
                grad_s = (mix - probs * total_row).astype(BF16)
                dv.append(mm(probs_low, gc2))
                dk.append(mm(grad_s, q2))
                dq.append(mm_tn(grad_s, k2))
            gp_ref[0, rows, cols] = (jnp.where(low, dq[0], dq[1]) * scale).astype(BF16)
            gp_ref[1, rows, cols] = (jnp.where(low, dk[0], dk[1]) * scale).astype(BF16)
            gp_ref[2, rows, cols] = jnp.where(low, dv[0], dv[1]).astype(BF16)

        if win == 0:

            @pl.when(tile == 0)
            def _():
                for k in range(4):
                    own_copy(k).wait()
                    core_copy(0, k).wait_recv()
                    m_sum[k] = (m_own[k].astype(F32) + m_core[k].astype(F32)).astype(BF16)

        else:
            for part in range(3):
                acc[part] += mm(n1t_ref[...], gp_ref[part, :, own])

            @pl.when(tile == last)
            def _():
                a_src[...] = acc[...].astype(BF16)
                for r in range(3):
                    chip_copy(0, r).wait_recv()
                kept_m = m_sum[chip, half].astype(F32)
                give_m = m_sum[chip, 1 - half].astype(F32)
                for r in range(3):
                    kept_m = kept_m + m_chip[r, half].astype(F32)
                    give_m = give_m + m_chip[r, 1 - half].astype(F32)
                m_give[...] = give_m.astype(BF16)
                gm_ref[...] = kept_m
                for k in range(4):
                    core_copy(1, k).start()

        grad_n = mm(gp_ref[0, rows], wqkv_ref[0])
        for part in range(1, 3):
            grad_n = grad_n + mm(gp_ref[part, rows], wqkv_ref[part])
        if win == 0:

            @pl.when(tile == 0)
            def _():
                for r in range(3):
                    chip_copy(0, r).start()

        else:

            @pl.when(tile == last)
            def _():
                give_copy(0).start()

        unit_at = tile * (TILE // LEN_A) + win * (WIN // LEN_A)
        parts = []
        for unit in range(WIN // LEN_A):
            at = win * WIN + unit * LEN_A
            parts.append(hidden_ref[at : at + LEN_A, :].astype(F32) + emb_ref[pl.ds(unit_at + unit, 1), :])
        hat, inv = norm_stats(jnp.concatenate(parts, axis=0))
        vec_ref[0:1] += jnp.sum(grad_n * hat, axis=0, keepdims=True)
        vec_ref[1:2] += jnp.sum(grad_n, axis=0, keepdims=True)
        grad_in = gmid_ref[rows] + norm_back(grad_n, gain_ref[...], hat, inv)
        stage[win] = grad_in.astype(BF16)
        for unit in range(WIN // LEN_A):
            usum_ref[pl.ds(unit_at + unit, 1), :] = jnp.sum(
                grad_in[unit * LEN_A : (unit + 1) * LEN_A], axis=0, keepdims=True
            )
        gh_local(2 * tile + win).start()

    @pl.when(tile == last)
    def _():
        units = usum_ref.shape[0]
        for k in range(4):
            core_copy(1, k).wait_recv()
            a_sum[k] = (
                a_src[:, share_of(2 * k + core), :].astype(F32) + a_core[k].astype(F32)
            ).astype(BF16)
        s_src[0:units, :] = usum_ref[:, own]
        for left in range(2):
            cols = slice(left * part_w, (left + 1) * part_w)
            at = units + 8 * left
            s_src[at : at + 2, :] = vec_ref[0:2, cols]
            s_src[at + 2 : at + 6, :] = vecm_ref[0:4, cols]
            s_src[at + 6 : at + 7, :] = gbu_ref[0, 0:1, cols]
            s_src[at + 7 : at + 8, :] = gbu_ref[1, 0:1, cols]
        gh_local(2 * tile + 1).wait()
        for n in range(GROUP - 1):
            small_copy(n).start()
        for r in range(3):
            chip_copy(1, r).start()
        s_rcv[spot] = s_src[...]
        for n in range(GROUP - 1):
            small_copy(n).wait_recv()
        v_sum = s_rcv[0, units : units + 16, :]
        for n in range(1, GROUP):
            v_sum = v_sum + s_rcv[n, units : units + 16, :]
        v_src[...] = v_sum
        v_rcv[member] = v_sum
        for n in range(GROUP):
            whole_u = s_rcv[n, 0:units, :]
            left, right = whole_u[:, :piece], whole_u[:, piece:]
            u_give[n] = jnp.where(half == 0, right, left)
            u_mine[n] = jnp.where(half == 0, left, right)
        for n in range(3):
            line_copy(n).start()
        u_copy().start()
        gh_last(0).start()
        give_copy(0).wait_recv()
        gm_ref[...] += m_got[...].astype(F32)
        for n in range(3):
            line_copy(n).wait_recv()
        every = 0.5 * ((v_rcv[0] + v_rcv[1]) + (v_rcv[2] + v_rcv[3]))
        other = member + 1 - 2 * half
        both = v_rcv[member] + v_rcv[other]
        for left in range(2):
            cols = slice(left * part_w, (left + 1) * part_w)
            at = 8 * left
            vec_out[0:6, cols] = every[at : at + 6]
            vec_out[6:7, cols] = jnp.where(half == 0, both[at + 6 : at + 7], both[at + 7 : at + 8])
        for r in range(3):
            chip_copy(1, r).wait_recv()
        both_a = a_sum[chip].astype(F32)
        for r in range(3):
            both_a = both_a + a_chip[r].astype(F32)
        first_a, last_a = both_a[:, :, :piece], both_a[:, :, piece:]
        a_give[...] = jnp.where(half == 0, last_a, first_a).astype(BF16)
        ga_ref[...] = jnp.where(half == 0, first_a, last_a)
        give_copy(1).start()
        gh_last(1).start()
        u_copy().wait_recv()
        at = lax.broadcasted_iota(jnp.int32, (units, table_ref.shape[1]), 1)
        picks, sums = [], []
        for n in range(GROUP):
            for side in range(2):
                rows = slice(units * side, units * (side + 1))
                picks.append((ts_ref[n, rows, 0:1] == at).astype(F32))
                sums.append(jnp.where(half == side, u_mine[n], u_got[n]))
        pick = jnp.concatenate(picks, axis=0).astype(BF16)
        rest = jnp.concatenate(sums, axis=0)
        table = jnp.zeros(table_ref.shape, F32)
        for _ in range(3):
            first = rest.astype(BF16)
            table = table + mm_tn(first, pick)
            rest = rest - first.astype(F32)
        table_ref[...] = table
        give_copy(1).wait_recv()
        ga_ref[...] += a_got[...].astype(F32)
        out_copy().wait_recv()
        out_copy().wait_send()
        for t in range(chunks - 1):
            gh_copy(t).wait_recv()
            gh_copy(t).wait_send()
        for n in range(2):
            gh_last(n).wait_recv()
            gh_last(n).wait_send()
        for kind in range(2):
            for k in range(4):
                core_copy(kind, k).wait_send()
            for r in range(3):
                chip_copy(kind, r).wait_send()
            give_copy(kind).wait_send()
        for n in range(GROUP - 1):
            small_copy(n).wait_send()
        for n in range(3):
            line_copy(n).wait_send()
        u_copy().wait_send()


def finish_kernel(
    out_in, gh_in, gm_ref, ga_ref, vec_ref, table_in,
    out_ref, gh_ref, table_ref, g1_ref, s1_ref, qkv_ref, wo_ref, ob_ref,
    g2_ref, s2_ref, up_ref, ub_ref, down_ref, db_ref,
):
    out_ref[...] = out_in[...]
    gh_ref[...] = gh_in[...]

    @pl.when(pl.program_id(0) == 0)
    def _():
        ff = up_ref.shape[1]
        table_ref[...] = table_in[...]
        up_ref[...] = gm_ref[:, 0:ff]
        down_ref[...] = gm_ref[:, ff : 2 * ff]
        for part in range(3):
            qkv_ref[part] = ga_ref[part]
        wo_ref[...] = ga_ref[3].T
        for n, ref in enumerate((g1_ref, s1_ref, g2_ref, s2_ref, ob_ref, db_ref, ub_ref)):
            ref[...] = vec_ref[n]


LIMIT = 62 * 1024 * 1024


def half_map(steps):
    return lambda i: (lax.rem(lax.axis_index("mp"), 2) * steps + i, 0)


def fixed(shape):
    zeros = (0,) * len(shape)
    return pl.BlockSpec(shape, lambda i: zeros, pipeline_mode=pl.Buffered(1))


def attn_fwd(hidden, emb, gain, shift, ob, bias, ts, wqkv, wo, wu, wd):
    count, width = hidden.shape[0] // 2, hidden.shape[1]
    steps = count // TILE
    heads = width // HD
    rows = wo.shape[0]
    ff = wu.shape[1]
    tok = pl.BlockSpec((TILE, width), lambda i: (i, 0))
    anywhere = pl.BlockSpec(memory_space=pl.ANY)
    dma = pltpu.SemaphoreType.DMA
    return pl.pallas_call(
        attn_fwd_kernel,
        name="attn_fwd",
        grid=(steps,),
        in_specs=[
            pl.BlockSpec((TILE, width), half_map(steps)),
            fixed(emb.shape), fixed(gain.shape), fixed(shift.shape), fixed(ob.shape), fixed(bias.shape),
        ] + [anywhere] * 5,
        out_specs=[anywhere] * 6 + [
            pl.BlockSpec((3, TILE, width), lambda i: (0, i, 0)),
            pl.BlockSpec((heads, TILE // WIN, WIN, WIN), lambda i: (0, i, 0, 0)),
            tok,
            tok,
        ],
        out_shape=[
            jax.ShapeDtypeStruct((3, 4 * rows, width), BF16),
            jax.ShapeDtypeStruct((4 * rows, width), BF16),
            jax.ShapeDtypeStruct((4, width, ff), BF16),
            jax.ShapeDtypeStruct((4, ff, width), BF16),
            jax.ShapeDtypeStruct((4, 8, ff), F32),
            jax.ShapeDtypeStruct((GROUP,) + ts.shape, jnp.int32),
            jax.ShapeDtypeStruct((3, count, width), BF16),
            jax.ShapeDtypeStruct((heads, count // WIN, WIN, WIN), BF16),
            jax.ShapeDtypeStruct((count, width), BF16),
            jax.ShapeDtypeStruct((count, width), F32),
        ],
        scratch_shapes=[
            pltpu.VMEM((WIN, WIN), F32), pltpu.VMEM((TILE, width), BF16),
            pltpu.VMEM((3, 4 * rows, width), BF16), pltpu.VMEM((4 * rows, width), BF16),
            pltpu.VMEM((TILE, width), BF16),
            pltpu.VMEM(wu.shape, BF16), pltpu.VMEM(wd.shape, BF16),
            pltpu.VMEM((8, ff), F32), pltpu.VMEM(ts.shape, jnp.int32),
            dma((16,)), dma((2,)), dma((4, 5)), dma((4, 4)), dma((3,)), dma((3,)),
            dma((4, 3, 7)), dma((4, 3, 7)), dma((GROUP - 1,)), dma((GROUP - 1,)),
        ],
        compiler_params=pltpu.CompilerParams(
            collective_id=1, has_side_effects=True, vmem_limit_bytes=LIMIT
        ),
        cost_estimate=pl.CostEstimate(flops=12_000_000_000, bytes_accessed=30_000_000, transcendentals=5_000_000),
    )(hidden, emb, gain, shift, ob, bias, ts, wqkv, wo, wu, wd)


def mlp(mid, gy, wu, bu, wd, gain, shift, db):
    count, width = mid.shape
    steps = count // HALF
    ff = wu.shape[2]
    tok = pl.BlockSpec((HALF, width), lambda i: (i, 0))
    dma = pltpu.SemaphoreType.DMA
    return pl.pallas_call(
        mlp_kernel,
        name="mlp_both",
        grid=(steps,),
        in_specs=[
            tok,
            pl.BlockSpec((HALF, width), half_map(steps)),
            fixed(wu.shape), fixed(bu.shape), fixed(wd.shape),
            fixed(gain.shape), fixed(shift.shape), fixed(db.shape),
        ],
        out_specs=[
            pl.BlockSpec(memory_space=pl.ANY), tok, fixed((2, width, 2 * ff)),
            fixed((8, width)), fixed((2, 8, ff)),
        ],
        scratch_shapes=[
            pltpu.VMEM((2, width, ff), F32), pltpu.VMEM((2, width, ff), F32),
            pltpu.VMEM((HALF, width), BF16), pltpu.VMEM((width, HALF), BF16),
            pltpu.VMEM((width, HALF), BF16),
            pltpu.VMEM((HALF, width), F32), pltpu.VMEM((HALF, width), F32),
            pltpu.VMEM((2, HALF, width), BF16), dma((steps,)), dma((steps,)), dma((steps,)),
        ],
        out_shape=[
            jax.ShapeDtypeStruct((2 * count, width), BF16),
            jax.ShapeDtypeStruct((count, width), F32),
            jax.ShapeDtypeStruct((2, width, 2 * ff), BF16),
            jax.ShapeDtypeStruct((8, width), F32),
            jax.ShapeDtypeStruct((2, 8, ff), F32),
        ],
        compiler_params=pltpu.CompilerParams(
            collective_id=2, has_side_effects=True, vmem_limit_bytes=LIMIT
        ),
        cost_estimate=pl.CostEstimate(flops=36_000_000_000, bytes_accessed=30_000_000, transcendentals=5_000_000),
    )(mid, gy, wu, bu, wd, gain, shift, db)


def attn_bwd(hidden, emb, gain, shift, wqkv, wo, qkv, probs, ctx, gmid, gwm, vecm, gbu, ts, out, table_rows):
    count, width = gmid.shape
    steps = count // TILE
    heads = width // HD
    share = width // GROUP
    wide = gwm.shape[2]
    units = emb.shape[0]
    piece = width // 4
    tok = pl.BlockSpec((TILE, width), lambda i: (i, 0))
    anywhere = pl.BlockSpec(memory_space=pl.ANY)
    dma = pltpu.SemaphoreType.DMA
    return pl.pallas_call(
        attn_bwd_kernel,
        name="attn_bwd",
        grid=(steps,),
        in_specs=[
            pl.BlockSpec((TILE, width), half_map(steps)),
            fixed(emb.shape), fixed(gain.shape), fixed(shift.shape),
            fixed(wqkv.shape), fixed(wo.shape),
            pl.BlockSpec((3, TILE, width), lambda i: (0, i, 0)),
            pl.BlockSpec((heads, TILE // WIN, WIN, WIN), lambda i: (0, i, 0, 0)),
            tok, tok, anywhere, fixed(vecm.shape), fixed(gbu.shape), fixed(ts.shape), anywhere,
        ],
        out_specs=[
            anywhere, anywhere, fixed((share, wide)), fixed((4, share, piece)),
            fixed((8, width)), fixed((piece, table_rows)),
        ],
        scratch_shapes=[
            pltpu.VMEM((4, width, width // 2), F32),
            pltpu.VMEM((3, TILE, width), BF16), pltpu.VMEM((TILE, width), BF16),
            pltpu.VMEM((width, TILE), BF16), pltpu.VMEM((width, TILE), BF16),
            pltpu.VMEM((8, width), F32), pltpu.VMEM((units, width), F32),
            pltpu.VMEM((2, HALF, width), BF16),
            pltpu.VMEM((4, 2, share, wide), BF16), pltpu.VMEM((4, 2, share, wide), BF16),
            pltpu.VMEM((4, 2, share, wide), BF16), pltpu.VMEM((3, 2, share, wide), BF16),
            pltpu.VMEM((share, wide), BF16), pltpu.VMEM((share, wide), BF16),
            pltpu.VMEM((4, width, width // 2), BF16), pltpu.VMEM((4, 4, share, width // 2), BF16),
            pltpu.VMEM((4, 4, share, width // 2), BF16), pltpu.VMEM((3, 4, share, width // 2), BF16),
            pltpu.VMEM((4, share, piece), BF16), pltpu.VMEM((4, share, piece), BF16),
            pltpu.VMEM((units + 16, width // 2), F32), pltpu.VMEM((GROUP, units + 16, width // 2), F32),
            pltpu.VMEM((16, width // 2), F32), pltpu.VMEM((4, 16, width // 2), F32),
            pltpu.VMEM((GROUP, units, piece), F32), pltpu.VMEM((GROUP, units, piece), F32),
            pltpu.VMEM((GROUP, units, piece), F32),
            dma((4,)), dma(()), dma(()), dma((2 * steps,)), dma((2 * steps + 1,)), dma((2 * steps + 1,)),
            dma((2, 4)), dma((2, 4)), dma((2, 3)), dma((2, 3)), dma((2,)), dma((2,)),
            dma((GROUP - 1,)), dma((GROUP - 1,)), dma((3,)), dma((3,)), dma(()), dma(()),
        ],
        out_shape=[
            jax.ShapeDtypeStruct((2 * count, width), BF16),
            jax.ShapeDtypeStruct((2 * count, width), BF16),
            jax.ShapeDtypeStruct((share, wide), F32),
            jax.ShapeDtypeStruct((4, share, piece), F32),
            jax.ShapeDtypeStruct((8, width), F32),
            jax.ShapeDtypeStruct((piece, table_rows), F32),
        ],
        input_output_aliases={14: 0},
        compiler_params=pltpu.CompilerParams(
            collective_id=3, has_side_effects=True, vmem_limit_bytes=LIMIT
        ),
        cost_estimate=pl.CostEstimate(flops=20_000_000_000, bytes_accessed=40_000_000, transcendentals=0),
    )(hidden, emb, gain, shift, wqkv, wo, qkv, probs, ctx, gmid, gwm, vecm, gbu, ts, out)


def finish(out, gh, gm, ga, vec, table):
    count, width = out.shape
    share = gm.shape[0]
    ff = gm.shape[1] // 2
    piece = width // 4
    tok = pl.BlockSpec((2 * TILE, width), lambda i: (i, 0))
    line = jax.ShapeDtypeStruct((width,), F32)
    shapes = [
        jax.ShapeDtypeStruct(table.shape, F32), line, line,
        jax.ShapeDtypeStruct((3, share, piece), F32), jax.ShapeDtypeStruct((piece, share), F32),
        line, line, line,
        jax.ShapeDtypeStruct((share, ff), F32), line, jax.ShapeDtypeStruct((share, ff), F32), line,
    ]
    return pl.pallas_call(
        finish_kernel,
        name="finish",
        grid=(count // (2 * TILE),),
        in_specs=[tok, tok] + [fixed(x.shape) for x in (gm, ga, vec, table)],
        out_specs=[tok, tok] + [fixed(x.shape) for x in shapes],
        out_shape=[jax.ShapeDtypeStruct(out.shape, BF16), jax.ShapeDtypeStruct(gh.shape, BF16)] + shapes,
        compiler_params=pltpu.CompilerParams(vmem_limit_bytes=LIMIT),
        cost_estimate=pl.CostEstimate(flops=1_000_000, bytes_accessed=20_000_000, transcendentals=0),
    )(out, gh, gm, ga, vec, table)


def local(
    hidden, timesteps, cotangent, time_table, first_gain, first_shift, qkv_weight, out_weight,
    out_bias, second_gain, second_shift, up_weight, up_bias, down_weight, down_bias,
):
    count = hidden.shape[0]
    half = lax.rem(lax.axis_index("mp"), 2)
    units = count // LEN_A
    unit = jnp.arange(units, dtype=jnp.int32)
    within = unit % 8
    row_of = unit // 8 * 6 + jnp.where(within < 4, within, 4 + (within - 4) // 2)
    unit_step = jnp.pad(
        jnp.take(timesteps, row_of).reshape(2, units // 2), ((0, 0), (0, 16 - units // 2)), constant_values=-1
    )
    emb = jnp.take(time_table, jnp.maximum(unit_step[half], 0), axis=0).astype(F32)
    stamps = jnp.broadcast_to(unit_step.reshape(32, 1), (32, 128))

    wqkv_f, wo_f, wu_f, wd_f, bu_f, ts_f, qkv, probs, ctx, mid = attn_fwd(
        hidden, emb, first_gain, first_shift, out_bias, up_bias, stamps,
        jnp.swapaxes(qkv_weight, 1, 2), out_weight, up_weight, down_weight,
    )
    output, gmid, gw_mlp, vec_mlp, gbu = mlp(
        mid, cotangent, wu_f, bu_f, wd_f, second_gain, second_shift, down_bias
    )
    output, grad_hidden, g_mlp, g_attn, vecs, table = attn_bwd(
        hidden, emb, first_gain, first_shift, wqkv_f, wo_f, qkv, probs, ctx, gmid,
        gw_mlp, vec_mlp, gbu, ts_f, output, time_table.shape[0],
    )
    outs = list(finish(output, grad_hidden, g_mlp, g_attn, vecs, table))
    outs[2], outs[12] = outs[2].T, outs[12].T
    groups = lax.axis_size("dp") // GROUP
    if groups > 1:
        spots = [[g * GROUP + n for n in range(GROUP)] for g in range(groups)]
        split = {5: 1, 6: 1, 10: 0, 12: 1}
        for n in range(2, len(outs)):
            value = outs[n] * (1.0 / GROUP)
            if n in split:
                value = lax.all_gather(value, "dp", axis_index_groups=spots, axis=split[n], tiled=True)
                outs[n] = lax.psum_scatter(value, "dp", scatter_dimension=split[n], tiled=True)
            else:
                outs[n] = lax.psum(value, "dp")
    return tuple(outs)


def solution(mesh):
    return jax.shard_map(
        local,
        mesh=mesh,
        in_specs=(
            P("dp", None), P("dp"), P("dp", None), P(), P(), P(), P(None, None, "mp"),
            P("mp", None), P(), P(), P(), P(None, "mp"), P("mp"), P("mp", None), P(),
        ),
        out_specs=(
            P("dp", None), P("dp", None), P(None, "mp"), P(), P(), P(None, "dp", "mp"),
            P("mp", "dp"), P(), P(), P(), P("dp", "mp"), P("mp"), P("mp", "dp"), P(),
        ),
        check_vma=False,
    )
```

```python
from functools import partial

import jax
import jax.numpy as jnp
from jax import lax
from jax.experimental import pallas as pl
from jax.experimental.pallas import tpu as pltpu
from jax.sharding import PartitionSpec as P

F32 = jnp.float32
BF16 = jnp.bfloat16
HD = 64
LEN_A = 128
LEN_B = 256
BLOCK = 512
WIN = 256
TILE = 512
GROUP = 8
HALF = TILE // 2
EPS = 1e-05
GELU_C = 0.7978845608028654
GELU_A = 0.044715


def mm(a, b):
    return lax.dot_general(a, b, (((1,), (0,)), ((), ())), preferred_element_type=F32)


def mm_nt(a, b):
    return lax.dot_general(a, b, (((1,), (1,)), ((), ())), preferred_element_type=F32)


def mm_tn(a, b):
    return lax.dot_general(a, b, (((0,), (0,)), ((), ())), preferred_element_type=F32)


def norm_stats(rows):
    centre = jnp.mean(rows, axis=-1, keepdims=True)
    offset = rows - centre
    spread = jnp.mean(offset * offset, axis=-1, keepdims=True)
    inv = lax.rsqrt(spread + EPS)
    return offset * inv, inv


def norm_back(grad, gain, hat, inv):
    dhat = grad * gain
    first = jnp.mean(dhat, axis=-1, keepdims=True)
    second = jnp.mean(dhat * hat, axis=-1, keepdims=True)
    return inv * (dhat - first - hat * second)


def stream_tile(hidden_ref, emb_ref, tile):
    parts = []
    for unit in range(TILE // LEN_A):
        row = emb_ref[pl.ds(tile * (TILE // LEN_A) + unit, 1), :]
        parts.append(hidden_ref[unit * LEN_A : (unit + 1) * LEN_A, :].astype(F32) + row)
    return jnp.concatenate(parts, axis=0)


def line_up():
    place = lax.axis_index("dp")
    spot = lax.rem(place, GROUP)
    return place - spot, spot


def ahead(ref, rows, dst, send, recv, target):
    return pltpu.make_async_remote_copy(
        src_ref=ref.at[rows] if rows is not None else ref,
        dst_ref=dst.at[rows] if rows is not None else dst,
        send_sem=send, recv_sem=recv, device_id=target, device_id_type=pl.DeviceIdType.MESH,
    )


def mate_of(member):
    return {"dp": lax.axis_index("dp"), "mp": member + 1 - 2 * lax.rem(member, 2)}


def greet(targets):
    barrier = pltpu.get_barrier_semaphore()
    for target in targets:
        pl.semaphore_signal(barrier, inc=1, device_id=target, device_id_type=pl.DeviceIdType.MESH)
    pl.semaphore_wait(barrier, len(targets))


def attn_fwd_kernel(
    hidden_ref, emb_ref, gain_ref, shift_ref, ob_ref, bias_ref, ts_ref, wqkv, wo, wu, wd,
    wqkv_f, wo_f, wu_f, wd_f, bu_f, ts_f, qkv_ref, probs_ref, ctx_ref, mid_ref,
    same_ref, ctx_acc, wqkv_v, wo_v, norm_v, hold_wu, hold_wd, hold_bu, hold_ts,
    loc_sem, load_sem, z_send, z_recv, b_send, b_recv, n_send, n_recv, t_send, t_recv,
):
    tile = pl.program_id(0)
    steps = pl.num_programs(0)
    last = steps - 1
    member = lax.axis_index("mp")
    half = lax.rem(member, 2)
    place = lax.axis_index("dp")
    base, spot = line_up()
    bit0 = lax.rem(spot, 2)
    bit1 = lax.rem(spot // 2, 2)
    bit2 = spot // 4

    def flip(where, bit, size):
        return where + size - 2 * size * bit

    near = {
        "core": {"dp": flip(place, bit0, 1), "mp": member},
        "x": {"dp": flip(place, bit1, 2), "mp": member},
        "y": {"dp": flip(place, bit2, 4), "mp": member},
    }
    from_x = flip(spot, bit1, 2)
    from_y = flip(spot, bit2, 4)
    from_d = flip(from_x, bit2, 4)
    others = [{"dp": base + lax.rem(spot + turn, GROUP), "mp": member} for turn in range(1, GROUP)]

    def peer(turn):
        return {"dp": place, "mp": lax.rem(member + turn, 4)}

    rows_a = wo.shape[0]
    step_a = rows_a // GROUP
    step_m = wu.shape[0] // GROUP

    def full_at(array, shard, piece):
        if array == 0:
            return wqkv_f.at[:, pl.ds(shard * rows_a + piece * step_a, step_a), :]
        if array == 1:
            return wo_f.at[pl.ds(shard * rows_a + piece * step_a, step_a), :]
        full = wu_f if array == 2 else wd_f
        return full.at[shard, pl.ds(piece * step_m, step_m), :]

    def own_at(array, piece):
        if array == 0:
            return wqkv.at[:, pl.ds(piece * step_a, step_a), :]
        if array == 1:
            return wo.at[pl.ds(piece * step_a, step_a), :]
        return (wu if array == 2 else wd).at[pl.ds(piece * step_m, step_m), :]

    def remote(src, dst, send, recv, target):
        return pltpu.make_async_remote_copy(
            src_ref=src, dst_ref=dst, send_sem=send, recv_sem=recv,
            device_id=target, device_id_type=pl.DeviceIdType.MESH,
        )

    pair = member // 2
    mate = member + 1 - 2 * half
    beyond = 2 * member - mate
    middle = (member == 1) | (member == 2)
    shards = (mate, 2 - pair, 3 - 3 * pair)

    def z_own(array, side):
        return remote(
            own_at(array, spot), full_at(array, member, spot),
            z_send.at[array, side], z_recv.at[array, member],
            {"dp": place, "mp": (mate, beyond)[side]},
        )

    def z_on(array, turn):
        shard = shards[turn]
        onward = jnp.where(shard < member, member + 1, member - 1)
        return remote(
            full_at(array, shard, spot), full_at(array, shard, spot),
            z_send.at[array, 2 + turn], z_recv.at[array, shard],
            {"dp": place, "mp": onward},
        )

    def z_start(array):
        z_own(array, 0).start()

        @pl.when(middle)
        def _():
            z_own(array, 1).start()

    def bias_copy(turn):
        return remote(hold_bu, bu_f.at[member], b_send.at[turn - 1], b_recv.at[turn - 1], peer(turn))

    def stamp_copy(n):
        return remote(ts_ref, ts_f.at[spot], t_send.at[n], t_recv.at[n], others[n])

    def push(array, turn, kind):
        shard = shards[turn]
        by_x = (array + turn) % 2 == 0
        piece = (spot, spot, from_x if by_x else from_y, spot, from_x, from_y, from_d)[kind]
        target = ("x", "y", "y" if by_x else "x", "core", "core", "core", "core")[kind]
        return remote(
            full_at(array, shard, piece), full_at(array, shard, piece),
            n_send.at[array, turn, kind], n_recv.at[array, turn, kind], near[target],
        )

    order = (0, 1, 2)

    def onward(array, turns):
        @pl.when(middle)
        def _():
            for turn in turns:
                z_on(array, turn).wait_recv()
                z_on(array, turn).start()

    def stage_z(array):
        for turn in order:
            if array < 2:
                onward(array, (turn,))

            @pl.when(jnp.logical_not(middle))
            def _():
                z_on(array, turn).wait_recv()

            for kind in (0, 1, 3):
                push(array, turn, kind).start()

    def stage_near(array):
        for turn in order:
            push(array, turn, 0).wait_recv()
            if (array + turn) % 2 == 0:
                push(array, turn, 2).start()
            push(array, turn, 4).start()
            push(array, turn, 1).wait_recv()
            if (array + turn) % 2 == 1:
                push(array, turn, 2).start()
            push(array, turn, 5).start()

    def stage_far(array):
        for turn in order:
            push(array, turn, 2).wait_recv()
            push(array, turn, 6).start()

    def settle(array):
        for turn in order:
            for kind in range(3, 7):
                push(array, turn, kind).wait_recv()

    own_rows = pl.ds(pl.multiple_of(member * rows_a, 64), rows_a)
    own_parts = (
        (wqkv, wqkv_v.at[:, own_rows, :], wqkv_f.at[:, own_rows, :]),
        (wo, wo_v.at[own_rows, :], wo_f.at[own_rows, :]),
        (wu, hold_wu, wu_f.at[member]),
        (wd, hold_wd, wd_f.at[member]),
        (ts_ref, hold_ts, ts_f.at[spot]),
    )

    def into(n):
        return pltpu.make_async_copy(own_parts[n][0], own_parts[n][1], loc_sem.at[n])

    def outof(n):
        return pltpu.make_async_copy(own_parts[n][1], own_parts[n][2], loc_sem.at[8 + n])

    def bias_out():
        return pltpu.make_async_copy(hold_bu, bu_f.at[member], loc_sem.at[15])

    def load(array):
        src, dst = ((wqkv_f, wqkv_v), (wo_f, wo_v))[array]
        return pltpu.make_async_copy(src, dst, load_sem.at[array])

    @pl.when(tile == 0)
    def _():
        hold_bu[...] = jnp.broadcast_to(bias_ref[...], hold_bu.shape)
        for n in range(5):
            into(n).start()
        greet([peer(1), peer(2), peer(3)] + others)
        for array in range(3):
            z_start(array)

    stream = stream_tile(hidden_ref, emb_ref, tile)
    hat, _ = norm_stats(stream)
    norm_v[...] = (hat * gain_ref[...] + shift_ref[...]).astype(BF16)
    mid_ref[...] = stream + ob_ref[...]

    @pl.when(tile == 0)
    def _():
        for n in range(5):
            into(n).wait()
            outof(n).start()
        stage_z(0)
        stage_z(1)
        z_start(3)
        for n in range(GROUP - 1):
            stamp_copy(n).start()
        bias_out().start()
        for turn in (1, 2, 3):
            bias_copy(turn).start()
        onward(2, (0, 1))
        stage_near(0)
        stage_near(1)
        onward(2, (2,))
        stage_far(0)
        stage_far(1)
        onward(3, (0, 1))
        stage_z(2)
        settle(0)
        outof(0).wait()
        load(0).start()
        load(0).wait()

    for part in range(3):
        qkv_ref[part] = mm_nt(norm_v[...], wqkv_v[part]).astype(BF16)

    @pl.when(tile == 0)
    def _():
        onward(3, (2,))
        settle(1)
        outof(1).wait()
        load(1).start()

    lane = lax.broadcasted_iota(jnp.int32, (WIN, 2 * HD), 1)
    low = lane < HD
    row_i = lax.broadcasted_iota(jnp.int32, (WIN, WIN), 0)
    col_i = lax.broadcasted_iota(jnp.int32, (WIN, WIN), 1)
    same_half = (row_i < LEN_A) == (col_i < LEN_A)
    scale = HD ** (-0.5)
    pairs = qkv_ref.shape[2] // (2 * HD)
    for win in range(TILE // WIN):
        at = ((half * steps + tile) * (TILE // WIN) + win) % 4
        same_ref[...] = jnp.where(same_half, 0.0, jnp.where(at < 2, -1e9, 0.0))
        rows = slice(win * WIN, (win + 1) * WIN)
        for pair in range(pairs):
            cols = slice(pair * 2 * HD, (pair + 1) * 2 * HD)
            q2 = qkv_ref[0, rows, cols] * jnp.asarray(scale, BF16)
            k2 = qkv_ref[1, rows, cols]
            v2 = qkv_ref[2, rows, cols]
            outs = []
            for j in range(2):
                q1 = jnp.where(low == (j == 0), q2, jnp.zeros_like(q2))
                scores = mm_nt(k2, q1) + same_ref[...]
                top = jnp.max(scores, axis=0, keepdims=True)
                expo = jnp.exp(scores - top)
                total = jnp.sum(expo, axis=0, keepdims=True)
                probs = (expo * (1.0 / total)).astype(BF16)
                probs_ref[2 * pair + j, win] = probs
                outs.append(mm_tn(probs, v2))
            ctx_acc[rows, cols] = jnp.where(low, outs[0], outs[1]).astype(BF16)
        if win == 0:

            @pl.when(tile == 0)
            def _():
                stage_near(2)

            @pl.when(tile == 1)
            def _():
                stage_far(2)

            @pl.when(tile == last)
            def _():
                stage_far(3)

    @pl.when(tile == 0)
    def _():
        load(1).wait()

    ctx_ref[...] = ctx_acc[...]
    mid_ref[...] += mm(ctx_acc[...], wo_v[...])

    @pl.when(tile == 0)
    def _():
        stage_z(3)

    @pl.when(tile == 1)
    def _():
        stage_near(3)

    @pl.when(tile == last)
    def _():
        settle(2)
        settle(3)
        for n in range(GROUP - 1):
            stamp_copy(n).wait_recv()
            stamp_copy(n).wait_send()
        for turn in (1, 2, 3):
            bias_copy(turn).wait_recv()
            bias_copy(turn).wait_send()
        for array in range(4):
            z_own(array, 0).wait_send()

            @pl.when(middle)
            def _():
                z_own(array, 1).wait_send()
                for turn in order:
                    z_on(array, turn).wait_send()

            for turn in order:
                for kind in range(7):
                    push(array, turn, kind).wait_send()
        for n in range(2, 5):
            outof(n).wait()
        bias_out().wait()


def mlp_kernel(
    mid_ref, gy_ref, wu_ref, bu_ref, wd_ref, gain_ref, shift_ref, db_ref,
    out_ref, gmid_ref, gw_ref, vec_ref, gbu_ref,
    acc_u, acc_d, n2_ref, n2t_ref, gyt_ref, mlp_ref, dn_ref, stage, loc_sem, send_sem, recv_sem,
):
    tile = pl.program_id(0)
    steps = pl.num_programs(0)
    last = steps - 1
    member = lax.axis_index("mp")
    half = lax.rem(member, 2)
    pair = member // 2
    mate = mate_of(member)
    ff = wu_ref.shape[2]
    total = out_ref.shape[0] // (2 * HALF)

    def rows_of(t):
        return pl.ds(pl.multiple_of((half * total + t) * HALF, HALF), HALF)

    def local_copy(t):
        return pltpu.make_async_copy(stage.at[lax.rem(t, 2)], out_ref.at[rows_of(t)], loc_sem.at[t])

    def remote_copy(t):
        return ahead(out_ref, rows_of(t), out_ref, send_sem.at[t], recv_sem.at[t], mate)

    @pl.when(tile == 0)
    def _():
        acc_u[...] = jnp.zeros_like(acc_u)
        acc_d[...] = jnp.zeros_like(acc_d)
        vec_ref[...] = jnp.zeros_like(vec_ref)
        gbu_ref[...] = jnp.zeros_like(gbu_ref)
        greet([mate])

    @pl.when(tile > 0)
    def _():
        local_copy(tile - 1).wait()
        remote_copy(tile - 1).start()

    hat, inv = norm_stats(mid_ref[...])
    normed = (hat * gain_ref[...] + shift_ref[...]).astype(BF16)
    n2_ref[...] = normed
    n2t_ref[...] = normed.T
    gyt_ref[...] = gy_ref[...].T
    mlp_ref[...] = mid_ref[...] + db_ref[...]
    dn_ref[...] = jnp.zeros_like(dn_ref)

    def step(turn, own):
        group = lax.rem(2 * pair + turn, 4)
        pre = mm(n2_ref[...], wu_ref[group]) + bu_ref[group, 0:1]
        grad_act = mm_nt(gy_ref[...], wd_ref[group])
        square = pre * pre
        gate = 0.5 * jnp.tanh(pre * (GELU_C + (GELU_C * GELU_A) * square)) + 0.5
        value = pre * gate
        act = value.astype(BF16)
        slope = gate + value * (1.0 - gate) * (2.0 * GELU_C + (6.0 * GELU_C * GELU_A) * square)
        grad_f = grad_act * slope
        grad_pre = grad_f.astype(BF16)
        mlp_ref[...] += mm(act, wd_ref[group])
        dn_ref[...] += mm_nt(grad_pre, wu_ref[group])
        if own:
            acc_u[turn] += mm(n2t_ref[...], grad_pre)
            acc_d[turn] += mm(gyt_ref[...], act)
            gbu_ref[turn, 0:1] += jnp.sum(grad_pre.astype(F32), axis=0, keepdims=True)

    lax.fori_loop(0, 2, lambda turn, c: (step(turn, True), c)[1], 0)
    lax.fori_loop(2, 4, lambda turn, c: (step(turn, False), c)[1], 0)

    stage[lax.rem(tile, 2)] = mlp_ref[...].astype(BF16)
    hat, inv = norm_stats(mid_ref[...])
    top = gy_ref[...].astype(F32)
    dn = dn_ref[...]
    vec_ref[0:1] += jnp.sum(dn * hat, axis=0, keepdims=True)
    vec_ref[1:2] += jnp.sum(dn, axis=0, keepdims=True)
    gmid = top + norm_back(dn, gain_ref[...], hat, inv)
    vec_ref[2:3] += jnp.sum(gmid, axis=0, keepdims=True)
    vec_ref[3:4] += jnp.sum(top, axis=0, keepdims=True)
    gmid_ref[...] = gmid
    local_copy(tile).start()

    @pl.when(tile == last)
    def _():
        gw_ref[:, :, 0:ff] = acc_u[...].astype(BF16)
        gw_ref[:, :, ff : 2 * ff] = acc_d[...].astype(BF16)
        local_copy(tile).wait()
        for t in range(total - 1):
            remote_copy(t).wait_send()
            remote_copy(t).wait_recv()


def attn_bwd_kernel(
    hidden_ref, emb_ref, gain_ref, shift_ref, wqkv_ref, wo_ref,
    qkv_ref, probs_ref, ctx_ref, gmid_ref, gwm_ref, vecm_ref, gbu_ref, ts_ref, out_in,
    out_ref, gh_ref, gm_ref, ga_ref, vec_out, table_ref,
    acc, gp_ref, gc_ref, n1t_ref, gmt_ref, vec_ref, usum_ref, stage,
    m_own, m_core, m_sum, m_chip, m_give, m_got,
    a_src, a_core, a_sum, a_chip, a_give, a_got,
    s_src, s_rcv, v_src, v_rcv, u_give, u_got, u_mine,
    own_sem, out_send, out_recv, loc_sem, gh_send, gh_recv,
    core_send, core_recv, chip_send, chip_recv, give_send, give_recv,
    s_send, s_recv, v_send, v_recv, u_send, u_recv,
):
    tile = pl.program_id(0)
    last = pl.num_programs(0) - 1
    member = lax.axis_index("mp")
    half = lax.rem(member, 2)
    pair_id = member // 2
    width = wo_ref.shape[1]
    part_w = width // 2
    piece = part_w // 2
    share = width // GROUP
    total = out_ref.shape[0] // (2 * TILE)
    base, spot = line_up()
    core = lax.rem(spot, 2)
    chip = spot // 2
    bit_x = lax.rem(chip, 2)
    bit_y = chip // 2
    mate = mate_of(member)
    flips = (
        chip + 1 - 2 * bit_x,
        chip + 2 - 4 * bit_y,
        3 - chip,
    )

    def device(where):
        return {"dp": base + where, "mp": member}

    sibling = device(spot + 1 - 2 * core)
    others = [device(lax.rem(spot + turn, GROUP)) for turn in range(1, GROUP)]
    line = [{"dp": base + spot, "mp": lax.rem(member + turn, 4)} for turn in range(1, 4)]

    def share_of(where):
        return pl.ds(pl.multiple_of(where * share, 32), share)

    def out_copy():
        rows = pl.ds(pl.multiple_of((half * 2 * total + 2 * total - 1) * HALF, HALF), HALF)
        return ahead(out_ref, rows, out_ref, out_send, out_recv, mate)

    chunks = 2 * total

    def gh_local(n):
        rows = pl.ds(pl.multiple_of((half * chunks + n) * HALF, HALF), HALF)
        return pltpu.make_async_copy(stage.at[lax.rem(n, 2)], gh_ref.at[rows], loc_sem.at[n])

    def gh_copy(n):
        rows = pl.ds(pl.multiple_of((half * chunks + n) * HALF, HALF), HALF)
        return ahead(gh_ref, rows, gh_ref, gh_send.at[n], gh_recv.at[n], mate)

    def gh_last(n):
        quarter = HALF // 2
        rows = pl.ds(pl.multiple_of((half * chunks + chunks - 1) * HALF + n * quarter, quarter), quarter)
        return ahead(gh_ref, rows, gh_ref, gh_send.at[chunks - 1 + n], gh_recv.at[chunks - 1 + n], mate)

    def own_copy(k):
        return pltpu.make_async_copy(gwm_ref.at[:, share_of(2 * k + core), :], m_own.at[k], own_sem.at[k])

    def core_copy(kind, k):
        src, dst = ((gwm_ref, m_core), (a_src, a_core))[kind]
        return pltpu.make_async_remote_copy(
            src_ref=src.at[:, share_of(2 * k + 1 - core), :], dst_ref=dst.at[k],
            send_sem=core_send.at[kind, k], recv_sem=core_recv.at[kind, k],
            device_id=sibling, device_id_type=pl.DeviceIdType.MESH,
        )

    def chip_copy(kind, r):
        src, dst = ((m_sum, m_chip), (a_sum, a_chip))[kind]
        return pltpu.make_async_remote_copy(
            src_ref=src.at[flips[r]], dst_ref=dst.at[r],
            send_sem=chip_send.at[kind, r], recv_sem=chip_recv.at[kind, r],
            device_id=device(2 * flips[r] + core), device_id_type=pl.DeviceIdType.MESH,
        )

    def give_copy(kind):
        src, dst = ((m_give, m_got), (a_give, a_got))[kind]
        return ahead(src, None, dst, give_send.at[kind], give_recv.at[kind], mate)

    def small_copy(n):
        return pltpu.make_async_remote_copy(
            src_ref=s_src, dst_ref=s_rcv.at[spot],
            send_sem=s_send.at[n], recv_sem=s_recv.at[n],
            device_id=others[n], device_id_type=pl.DeviceIdType.MESH,
        )

    def line_copy(n):
        return pltpu.make_async_remote_copy(
            src_ref=v_src, dst_ref=v_rcv.at[member],
            send_sem=v_send.at[n], recv_sem=v_recv.at[n],
            device_id=line[n], device_id_type=pl.DeviceIdType.MESH,
        )

    def u_copy():
        return ahead(u_give, None, u_got, u_send, u_recv, mate)

    @pl.when(tile == 0)
    def _():
        acc[...] = jnp.zeros_like(acc)
        vec_ref[...] = jnp.zeros_like(vec_ref)
        usum_ref[...] = jnp.zeros_like(usum_ref)
        greet(others + line)
        out_copy().start()
        for k in range(4):
            core_copy(0, k).start()
        for k in range(4):
            own_copy(k).start()

    @pl.when(tile > 0)
    def _():
        gh_local(2 * tile - 1).wait()
        gh_copy(2 * tile - 1).start()

    own = pl.ds(pl.multiple_of(pair_id * part_w, 128), part_w)
    stream = stream_tile(hidden_ref, emb_ref, tile)
    hat, inv = norm_stats(stream)
    n1t_ref[...] = (hat * gain_ref[...] + shift_ref[...]).astype(BF16).T
    gm_low = gmid_ref[...].astype(BF16)
    gmt_ref[...] = gm_low.T
    gc_ref[...] = mm_nt(gm_low, wo_ref[...]).astype(BF16)
    acc[3] += mm(gmt_ref[...], ctx_ref[:, own])
    lane = lax.broadcasted_iota(jnp.int32, (WIN, 2 * HD), 1)
    low = lane < HD
    scale = HD ** (-0.5)
    pairs = width // (2 * HD)
    for win in range(TILE // WIN):
        rows = slice(win * WIN, (win + 1) * WIN)
        for pair in range(pairs):
            cols = slice(pair * 2 * HD, (pair + 1) * 2 * HD)
            if win == 1 and pair == 1:
                gh_local(2 * tile).wait()
                gh_copy(2 * tile).start()
            q2 = qkv_ref[0, rows, cols]
            k2 = qkv_ref[1, rows, cols]
            v2 = qkv_ref[2, rows, cols]
            gc2 = gc_ref[rows, cols]
            dq, dk, dv = [], [], []
            for j in range(2):
                gc1 = jnp.where(low == (j == 0), gc2, jnp.zeros_like(gc2))
                probs_low = probs_ref[2 * pair + j, win]
                probs = probs_low.astype(F32)
                dprob = mm_nt(v2, gc1)
                mix = probs * dprob
                total_row = jnp.sum(mix, axis=0, keepdims=True)
                grad_s = (mix - probs * total_row).astype(BF16)
                dv.append(mm(probs_low, gc2))
                dk.append(mm(grad_s, q2))
                dq.append(mm_tn(grad_s, k2))
            gp_ref[0, rows, cols] = (jnp.where(low, dq[0], dq[1]) * scale).astype(BF16)
            gp_ref[1, rows, cols] = (jnp.where(low, dk[0], dk[1]) * scale).astype(BF16)
            gp_ref[2, rows, cols] = jnp.where(low, dv[0], dv[1]).astype(BF16)

        if win == 0:

            @pl.when(tile == 0)
            def _():
                for k in range(4):
                    own_copy(k).wait()
                    core_copy(0, k).wait_recv()
                    m_sum[k] = (m_own[k].astype(F32) + m_core[k].astype(F32)).astype(BF16)

        else:
            for part in range(3):
                acc[part] += mm(n1t_ref[...], gp_ref[part, :, own])

            @pl.when(tile == last)
            def _():
                a_src[...] = acc[...].astype(BF16)
                for r in range(3):
                    chip_copy(0, r).wait_recv()
                kept_m = m_sum[chip, half].astype(F32)
                give_m = m_sum[chip, 1 - half].astype(F32)
                for r in range(3):
                    kept_m = kept_m + m_chip[r, half].astype(F32)
                    give_m = give_m + m_chip[r, 1 - half].astype(F32)
                m_give[...] = give_m.astype(BF16)
                gm_ref[...] = kept_m
                for k in range(4):
                    core_copy(1, k).start()

        grad_n = mm(gp_ref[0, rows], wqkv_ref[0])
        for part in range(1, 3):
            grad_n = grad_n + mm(gp_ref[part, rows], wqkv_ref[part])
        if win == 0:

            @pl.when(tile == 0)
            def _():
                for r in range(3):
                    chip_copy(0, r).start()

        else:

            @pl.when(tile == last)
            def _():
                give_copy(0).start()

        unit_at = tile * (TILE // LEN_A) + win * (WIN // LEN_A)
        parts = []
        for unit in range(WIN // LEN_A):
            at = win * WIN + unit * LEN_A
            parts.append(hidden_ref[at : at + LEN_A, :].astype(F32) + emb_ref[pl.ds(unit_at + unit, 1), :])
        hat, inv = norm_stats(jnp.concatenate(parts, axis=0))
        vec_ref[0:1] += jnp.sum(grad_n * hat, axis=0, keepdims=True)
        vec_ref[1:2] += jnp.sum(grad_n, axis=0, keepdims=True)
        grad_in = gmid_ref[rows] + norm_back(grad_n, gain_ref[...], hat, inv)
        stage[win] = grad_in.astype(BF16)
        for unit in range(WIN // LEN_A):
            usum_ref[pl.ds(unit_at + unit, 1), :] = jnp.sum(
                grad_in[unit * LEN_A : (unit + 1) * LEN_A], axis=0, keepdims=True
            )
        gh_local(2 * tile + win).start()

    @pl.when(tile == last)
    def _():
        units = usum_ref.shape[0]
        for k in range(4):
            core_copy(1, k).wait_recv()
            a_sum[k] = (
                a_src[:, share_of(2 * k + core), :].astype(F32) + a_core[k].astype(F32)
            ).astype(BF16)
        s_src[0:units, :] = usum_ref[:, own]
        for left in range(2):
            cols = slice(left * part_w, (left + 1) * part_w)
            at = units + 8 * left
            s_src[at : at + 2, :] = vec_ref[0:2, cols]
            s_src[at + 2 : at + 6, :] = vecm_ref[0:4, cols]
            s_src[at + 6 : at + 7, :] = gbu_ref[0, 0:1, cols]
            s_src[at + 7 : at + 8, :] = gbu_ref[1, 0:1, cols]
        gh_local(2 * tile + 1).wait()
        for n in range(GROUP - 1):
            small_copy(n).start()
        for r in range(3):
            chip_copy(1, r).start()
        s_rcv[spot] = s_src[...]
        for n in range(GROUP - 1):
            small_copy(n).wait_recv()
        v_sum = s_rcv[0, units : units + 16, :]
        for n in range(1, GROUP):
            v_sum = v_sum + s_rcv[n, units : units + 16, :]
        v_src[...] = v_sum
        v_rcv[member] = v_sum
        for n in range(GROUP):
            whole_u = s_rcv[n, 0:units, :]
            left, right = whole_u[:, :piece], whole_u[:, piece:]
            u_give[n] = jnp.where(half == 0, right, left)
            u_mine[n] = jnp.where(half == 0, left, right)
        for n in range(3):
            line_copy(n).start()
        u_copy().start()
        gh_last(0).start()
        give_copy(0).wait_recv()
        gm_ref[...] += m_got[...].astype(F32)
        for n in range(3):
            line_copy(n).wait_recv()
        every = 0.5 * ((v_rcv[0] + v_rcv[1]) + (v_rcv[2] + v_rcv[3]))
        other = member + 1 - 2 * half
        both = v_rcv[member] + v_rcv[other]
        for left in range(2):
            cols = slice(left * part_w, (left + 1) * part_w)
            at = 8 * left
            vec_out[0:6, cols] = every[at : at + 6]
            vec_out[6:7, cols] = jnp.where(half == 0, both[at + 6 : at + 7], both[at + 7 : at + 8])
        for r in range(3):
            chip_copy(1, r).wait_recv()
        both_a = a_sum[chip].astype(F32)
        for r in range(3):
            both_a = both_a + a_chip[r].astype(F32)
        first_a, last_a = both_a[:, :, :piece], both_a[:, :, piece:]
        a_give[...] = jnp.where(half == 0, last_a, first_a).astype(BF16)
        ga_ref[...] = jnp.where(half == 0, first_a, last_a)
        give_copy(1).start()
        gh_last(1).start()
        u_copy().wait_recv()
        at = lax.broadcasted_iota(jnp.int32, (units, table_ref.shape[1]), 1)
        picks, sums = [], []
        for n in range(GROUP):
            for side in range(2):
                rows = slice(units * side, units * (side + 1))
                picks.append((ts_ref[n, rows, 0:1] == at).astype(F32))
                sums.append(jnp.where(half == side, u_mine[n], u_got[n]))
        pick = jnp.concatenate(picks, axis=0).astype(BF16)
        rest = jnp.concatenate(sums, axis=0)
        table = jnp.zeros(table_ref.shape, F32)
        for _ in range(3):
            first = rest.astype(BF16)
            table = table + mm_tn(first, pick)
            rest = rest - first.astype(F32)
        table_ref[...] = table
        give_copy(1).wait_recv()
        ga_ref[...] += a_got[...].astype(F32)
        out_copy().wait_recv()
        out_copy().wait_send()
        for t in range(chunks - 1):
            gh_copy(t).wait_recv()
            gh_copy(t).wait_send()
        for n in range(2):
            gh_last(n).wait_recv()
            gh_last(n).wait_send()
        for kind in range(2):
            for k in range(4):
                core_copy(kind, k).wait_send()
            for r in range(3):
                chip_copy(kind, r).wait_send()
            give_copy(kind).wait_send()
        for n in range(GROUP - 1):
            small_copy(n).wait_send()
        for n in range(3):
            line_copy(n).wait_send()
        u_copy().wait_send()


def finish_kernel(
    out_in, gh_in, gm_ref, ga_ref, vec_ref, table_in,
    out_ref, gh_ref, table_ref, g1_ref, s1_ref, qkv_ref, wo_ref, ob_ref,
    g2_ref, s2_ref, up_ref, ub_ref, down_ref, db_ref,
):
    out_ref[...] = out_in[...]
    gh_ref[...] = gh_in[...]

    @pl.when(pl.program_id(0) == 0)
    def _():
        ff = up_ref.shape[1]
        table_ref[...] = table_in[...]
        up_ref[...] = gm_ref[:, 0:ff]
        down_ref[...] = gm_ref[:, ff : 2 * ff]
        for part in range(3):
            qkv_ref[part] = ga_ref[part]
        wo_ref[...] = ga_ref[3].T
        for n, ref in enumerate((g1_ref, s1_ref, g2_ref, s2_ref, ob_ref, db_ref, ub_ref)):
            ref[...] = vec_ref[n]


LIMIT = 62 * 1024 * 1024


def half_map(steps):
    return lambda i: (lax.rem(lax.axis_index("mp"), 2) * steps + i, 0)


def fixed(shape):
    zeros = (0,) * len(shape)
    return pl.BlockSpec(shape, lambda i: zeros, pipeline_mode=pl.Buffered(1))


def attn_fwd(hidden, emb, gain, shift, ob, bias, ts, wqkv, wo, wu, wd):
    count, width = hidden.shape[0] // 2, hidden.shape[1]
    steps = count // TILE
    heads = width // HD
    rows = wo.shape[0]
    ff = wu.shape[1]
    tok = pl.BlockSpec((TILE, width), lambda i: (i, 0))
    anywhere = pl.BlockSpec(memory_space=pl.ANY)
    dma = pltpu.SemaphoreType.DMA
    return pl.pallas_call(
        attn_fwd_kernel,
        name="attn_fwd",
        grid=(steps,),
        in_specs=[
            pl.BlockSpec((TILE, width), half_map(steps)),
            fixed(emb.shape), fixed(gain.shape), fixed(shift.shape), fixed(ob.shape), fixed(bias.shape),
        ] + [anywhere] * 5,
        out_specs=[anywhere] * 6 + [
            pl.BlockSpec((3, TILE, width), lambda i: (0, i, 0)),
            pl.BlockSpec((heads, TILE // WIN, WIN, WIN), lambda i: (0, i, 0, 0)),
            tok,
            tok,
        ],
        out_shape=[
            jax.ShapeDtypeStruct((3, 4 * rows, width), BF16),
            jax.ShapeDtypeStruct((4 * rows, width), BF16),
            jax.ShapeDtypeStruct((4, width, ff), BF16),
            jax.ShapeDtypeStruct((4, ff, width), BF16),
            jax.ShapeDtypeStruct((4, 8, ff), F32),
            jax.ShapeDtypeStruct((GROUP,) + ts.shape, jnp.int32),
            jax.ShapeDtypeStruct((3, count, width), BF16),
            jax.ShapeDtypeStruct((heads, count // WIN, WIN, WIN), BF16),
            jax.ShapeDtypeStruct((count, width), BF16),
            jax.ShapeDtypeStruct((count, width), F32),
        ],
        scratch_shapes=[
            pltpu.VMEM((WIN, WIN), F32), pltpu.VMEM((TILE, width), BF16),
            pltpu.VMEM((3, 4 * rows, width), BF16), pltpu.VMEM((4 * rows, width), BF16),
            pltpu.VMEM((TILE, width), BF16),
            pltpu.VMEM(wu.shape, BF16), pltpu.VMEM(wd.shape, BF16),
            pltpu.VMEM((8, ff), F32), pltpu.VMEM(ts.shape, jnp.int32),
            dma((16,)), dma((2,)), dma((4, 5)), dma((4, 4)), dma((3,)), dma((3,)),
            dma((4, 3, 7)), dma((4, 3, 7)), dma((GROUP - 1,)), dma((GROUP - 1,)),
        ],
        compiler_params=pltpu.CompilerParams(
            collective_id=1, has_side_effects=True, vmem_limit_bytes=LIMIT
        ),
        cost_estimate=pl.CostEstimate(flops=12_000_000_000, bytes_accessed=30_000_000, transcendentals=5_000_000),
    )(hidden, emb, gain, shift, ob, bias, ts, wqkv, wo, wu, wd)


def mlp(mid, gy, wu, bu, wd, gain, shift, db):
    count, width = mid.shape
    steps = count // HALF
    ff = wu.shape[2]
    tok = pl.BlockSpec((HALF, width), lambda i: (i, 0))
    dma = pltpu.SemaphoreType.DMA
    return pl.pallas_call(
        mlp_kernel,
        name="mlp_both",
        grid=(steps,),
        in_specs=[
            tok,
            pl.BlockSpec((HALF, width), half_map(steps)),
            fixed(wu.shape), fixed(bu.shape), fixed(wd.shape),
            fixed(gain.shape), fixed(shift.shape), fixed(db.shape),
        ],
        out_specs=[
            pl.BlockSpec(memory_space=pl.ANY), tok, fixed((2, width, 2 * ff)),
            fixed((8, width)), fixed((2, 8, ff)),
        ],
        scratch_shapes=[
            pltpu.VMEM((2, width, ff), F32), pltpu.VMEM((2, width, ff), F32),
            pltpu.VMEM((HALF, width), BF16), pltpu.VMEM((width, HALF), BF16),
            pltpu.VMEM((width, HALF), BF16),
            pltpu.VMEM((HALF, width), F32), pltpu.VMEM((HALF, width), F32),
            pltpu.VMEM((2, HALF, width), BF16), dma((steps,)), dma((steps,)), dma((steps,)),
        ],
        out_shape=[
            jax.ShapeDtypeStruct((2 * count, width), BF16),
            jax.ShapeDtypeStruct((count, width), F32),
            jax.ShapeDtypeStruct((2, width, 2 * ff), BF16),
            jax.ShapeDtypeStruct((8, width), F32),
            jax.ShapeDtypeStruct((2, 8, ff), F32),
        ],
        compiler_params=pltpu.CompilerParams(
            collective_id=2, has_side_effects=True, vmem_limit_bytes=LIMIT
        ),
        cost_estimate=pl.CostEstimate(flops=36_000_000_000, bytes_accessed=30_000_000, transcendentals=5_000_000),
    )(mid, gy, wu, bu, wd, gain, shift, db)


def attn_bwd(hidden, emb, gain, shift, wqkv, wo, qkv, probs, ctx, gmid, gwm, vecm, gbu, ts, out, table_rows):
    count, width = gmid.shape
    steps = count // TILE
    heads = width // HD
    share = width // GROUP
    wide = gwm.shape[2]
    units = emb.shape[0]
    piece = width // 4
    tok = pl.BlockSpec((TILE, width), lambda i: (i, 0))
    anywhere = pl.BlockSpec(memory_space=pl.ANY)
    dma = pltpu.SemaphoreType.DMA
    return pl.pallas_call(
        attn_bwd_kernel,
        name="attn_bwd",
        grid=(steps,),
        in_specs=[
            pl.BlockSpec((TILE, width), half_map(steps)),
            fixed(emb.shape), fixed(gain.shape), fixed(shift.shape),
            fixed(wqkv.shape), fixed(wo.shape),
            pl.BlockSpec((3, TILE, width), lambda i: (0, i, 0)),
            pl.BlockSpec((heads, TILE // WIN, WIN, WIN), lambda i: (0, i, 0, 0)),
            tok, tok, anywhere, fixed(vecm.shape), fixed(gbu.shape), fixed(ts.shape), anywhere,
        ],
        out_specs=[
            anywhere, anywhere, fixed((share, wide)), fixed((4, share, piece)),
            fixed((8, width)), fixed((piece, table_rows)),
        ],
        scratch_shapes=[
            pltpu.VMEM((4, width, width // 2), F32),
            pltpu.VMEM((3, TILE, width), BF16), pltpu.VMEM((TILE, width), BF16),
            pltpu.VMEM((width, TILE), BF16), pltpu.VMEM((width, TILE), BF16),
            pltpu.VMEM((8, width), F32), pltpu.VMEM((units, width), F32),
            pltpu.VMEM((2, HALF, width), BF16),
            pltpu.VMEM((4, 2, share, wide), BF16), pltpu.VMEM((4, 2, share, wide), BF16),
            pltpu.VMEM((4, 2, share, wide), BF16), pltpu.VMEM((3, 2, share, wide), BF16),
            pltpu.VMEM((share, wide), BF16), pltpu.VMEM((share, wide), BF16),
            pltpu.VMEM((4, width, width // 2), BF16), pltpu.VMEM((4, 4, share, width // 2), BF16),
            pltpu.VMEM((4, 4, share, width // 2), BF16), pltpu.VMEM((3, 4, share, width // 2), BF16),
            pltpu.VMEM((4, share, piece), BF16), pltpu.VMEM((4, share, piece), BF16),
            pltpu.VMEM((units + 16, width // 2), F32), pltpu.VMEM((GROUP, units + 16, width // 2), F32),
            pltpu.VMEM((16, width // 2), F32), pltpu.VMEM((4, 16, width // 2), F32),
            pltpu.VMEM((GROUP, units, piece), F32), pltpu.VMEM((GROUP, units, piece), F32),
            pltpu.VMEM((GROUP, units, piece), F32),
            dma((4,)), dma(()), dma(()), dma((2 * steps,)), dma((2 * steps + 1,)), dma((2 * steps + 1,)),
            dma((2, 4)), dma((2, 4)), dma((2, 3)), dma((2, 3)), dma((2,)), dma((2,)),
            dma((GROUP - 1,)), dma((GROUP - 1,)), dma((3,)), dma((3,)), dma(()), dma(()),
        ],
        out_shape=[
            jax.ShapeDtypeStruct((2 * count, width), BF16),
            jax.ShapeDtypeStruct((2 * count, width), BF16),
            jax.ShapeDtypeStruct((share, wide), F32),
            jax.ShapeDtypeStruct((4, share, piece), F32),
            jax.ShapeDtypeStruct((8, width), F32),
            jax.ShapeDtypeStruct((piece, table_rows), F32),
        ],
        input_output_aliases={14: 0},
        compiler_params=pltpu.CompilerParams(
            collective_id=3, has_side_effects=True, vmem_limit_bytes=LIMIT
        ),
        cost_estimate=pl.CostEstimate(flops=20_000_000_000, bytes_accessed=40_000_000, transcendentals=0),
    )(hidden, emb, gain, shift, wqkv, wo, qkv, probs, ctx, gmid, gwm, vecm, gbu, ts, out)


def finish(out, gh, gm, ga, vec, table):
    count, width = out.shape
    share = gm.shape[0]
    ff = gm.shape[1] // 2
    piece = width // 4
    tok = pl.BlockSpec((2 * TILE, width), lambda i: (i, 0))
    line = jax.ShapeDtypeStruct((width,), F32)
    shapes = [
        jax.ShapeDtypeStruct(table.shape, F32), line, line,
        jax.ShapeDtypeStruct((3, share, piece), F32), jax.ShapeDtypeStruct((piece, share), F32),
        line, line, line,
        jax.ShapeDtypeStruct((share, ff), F32), line, jax.ShapeDtypeStruct((share, ff), F32), line,
    ]
    return pl.pallas_call(
        finish_kernel,
        name="finish",
        grid=(count // (2 * TILE),),
        in_specs=[tok, tok] + [fixed(x.shape) for x in (gm, ga, vec, table)],
        out_specs=[tok, tok] + [fixed(x.shape) for x in shapes],
        out_shape=[jax.ShapeDtypeStruct(out.shape, BF16), jax.ShapeDtypeStruct(gh.shape, BF16)] + shapes,
        compiler_params=pltpu.CompilerParams(vmem_limit_bytes=LIMIT),
        cost_estimate=pl.CostEstimate(flops=1_000_000, bytes_accessed=20_000_000, transcendentals=0),
    )(out, gh, gm, ga, vec, table)


def local(
    hidden, timesteps, cotangent, time_table, first_gain, first_shift, qkv_weight, out_weight,
    out_bias, second_gain, second_shift, up_weight, up_bias, down_weight, down_bias,
):
    count = hidden.shape[0]
    half = lax.rem(lax.axis_index("mp"), 2)
    units = count // LEN_A
    unit = jnp.arange(units, dtype=jnp.int32)
    within = unit % 8
    row_of = unit // 8 * 6 + jnp.where(within < 4, within, 4 + (within - 4) // 2)
    unit_step = jnp.pad(
        jnp.take(timesteps, row_of).reshape(2, units // 2), ((0, 0), (0, 16 - units // 2)), constant_values=-1
    )
    emb = jnp.take(time_table, jnp.maximum(unit_step[half], 0), axis=0).astype(F32)
    stamps = jnp.broadcast_to(unit_step.reshape(32, 1), (32, 128))

    wqkv_f, wo_f, wu_f, wd_f, bu_f, ts_f, qkv, probs, ctx, mid = attn_fwd(
        hidden, emb, first_gain, first_shift, out_bias, up_bias, stamps,
        jnp.swapaxes(qkv_weight, 1, 2), out_weight, up_weight, down_weight,
    )
    output, gmid, gw_mlp, vec_mlp, gbu = mlp(
        mid, cotangent, wu_f, bu_f, wd_f, second_gain, second_shift, down_bias
    )
    output, grad_hidden, g_mlp, g_attn, vecs, table = attn_bwd(
        hidden, emb, first_gain, first_shift, wqkv_f, wo_f, qkv, probs, ctx, gmid,
        gw_mlp, vec_mlp, gbu, ts_f, output, time_table.shape[0],
    )
    outs = list(finish(output, grad_hidden, g_mlp, g_attn, vecs, table))
    outs[2], outs[12] = outs[2].T, outs[12].T
    groups = lax.axis_size("dp") // GROUP
    if groups > 1:
        spots = [[g * GROUP + n for n in range(GROUP)] for g in range(groups)]
        split = {5: 1, 6: 1, 10: 0, 12: 1}
        for n in range(2, len(outs)):
            value = outs[n] * (1.0 / GROUP)
            if n in split:
                value = lax.all_gather(value, "dp", axis_index_groups=spots, axis=split[n], tiled=True)
                outs[n] = lax.psum_scatter(value, "dp", scatter_dimension=split[n], tiled=True)
            else:
                outs[n] = lax.psum(value, "dp")
    return tuple(outs)


def solution(mesh):
    return jax.shard_map(
        local,
        mesh=mesh,
        in_specs=(
            P("dp", None), P("dp"), P("dp", None), P(), P(), P(), P(None, None, "mp"),
            P("mp", None), P(), P(), P(), P(None, "mp"), P("mp"), P("mp", None), P(),
        ),
        out_specs=(
            P("dp", None), P("dp", None), P(None, "mp"), P(), P(), P(None, "dp", "mp"),
            P("mp", "dp"), P(), P(), P(), P("dp", "mp"), P("mp"), P("mp", "dp"), P(),
        ),
        check_vma=False,
    )
```
